256 devices in a mesh: seq: 32 (over z, y), tp: 8 (over x, core).
Axes of the slice: x: 4, y: 4, z: 8, core: 2. Of those that a mesh axis runs over, the one named last changes fastest.
Arguments:
- query_in: bfloat16 [4096, 8192], P('seq', 'tp'), may hold values from -6 to 6
- key_in: bfloat16 [4096, 8192], P('seq', 'tp'), may hold values from -6 to 6
- value_in: bfloat16 [4096, 8192], P('seq', 'tp'), may hold values from -6 to 6
- stream: bfloat16 [4096, 8192], P('seq', 'tp'), may hold values from -6 to 6
- short_filter: float32 [3, 3, 8192], P(None, None, 'tp'), may hold values from -3 to 3
- decay_rate: float32 [16, 8192], P(None, 'tp'), as said below
- residue: float32 [16, 8192], P(None, 'tp'), as said below
- norm_gain: float32 [8192], P('tp'), may hold values from 0.5 to 1.5
- cotangent: bfloat16 [4096, 8192], P('seq', 'tp'), may hold values from -6 to 6
Outputs:
- normed: bfloat16 [4096, 8192], P('seq', 'tp')
- stream_grad: bfloat16 [4096, 8192], P('seq', 'tp')
- query_grad: bfloat16 [4096, 8192], P('seq', 'tp')
- key_grad: bfloat16 [4096, 8192], P('seq', 'tp')
- value_grad: bfloat16 [4096, 8192], P('seq', 'tp')
The draws below stay inside these ranges and needn't reach their ends.
Inputs may be any that keep to these rules, and one draw needn't show every extreme that they name: The pole of mode m of channel c is exp(-decay_rate[m, c]); every rate is positive and at most 1/30. `residue`: residues are real numbers.
All inputs are finite; a program needn't handle non-finite values.
Results may differ from the reference program's by a relative error of at most 0.0012.
Values may be sent and summed in bfloat16 or wider, within the bound.
A program may use at most 128 MiB of HBM per device.

```python
import math
import jax
import jax.numpy as jnp
from jax import lax

D = 8192
MODES = 16
SHORT = 3
TOKENS = 4096
N_TP = 8


def mode_rates(key):
    base = jax.random.fold_in(key, 17)
    chooser = jax.random.uniform(jax.random.fold_in(base, 1), (MODES, D), jnp.float32)
    placing = jax.random.uniform(jax.random.fold_in(base, 2), (MODES, D), jnp.float32)
    slow_share = 0.4
    middle_share = 0.3
    top_rate = 1.0 / 30.0
    slow_low = math.log(0.05 / TOKENS)
    slow_high = math.log(min(2.0 / TOKENS, top_rate))
    middle_low = slow_high
    middle_high = math.log(top_rate)
    fast_low = math.log(1.0 / 50.0)
    fast_high = math.log(top_rate)
    slow_rate = jnp.exp(slow_low + placing * (slow_high - slow_low))
    middle_rate = jnp.exp(middle_low + placing * (middle_high - middle_low))
    fast_rate = jnp.exp(fast_low + placing * (fast_high - fast_low))
    return jnp.where(chooser < slow_share, slow_rate, jnp.where(chooser < slow_share + middle_share, middle_rate, fast_rate))


def draw_decay_rate(key, part):
    return mode_rates(key)


def draw_residue(key, part):
    rates = mode_rates(key)
    normals = jax.random.normal(jax.random.fold_in(key, 29), (MODES, D), jnp.float32)
    return normals * jnp.sqrt(2.0 * rates / MODES)


def block_levels(stream_key, shape, pieces, smallest, high):
    gain, own = 1.0, jax.random.fold_in(stream_key, 6)
    for position, blocks in pieces:
        steps = jnp.exp(jax.random.uniform(jax.random.fold_in(own, position), (blocks,), jnp.float32, smallest / len(pieces), high / len(pieces)))
        gain = gain * jnp.repeat(steps, shape[position] // blocks).reshape([-1 if axis == position else 1 for axis in range(len(shape))])
    return gain


def scatter_about(key, extent, scale, limit, shards=(), held_as=jnp.bfloat16):
    factor_of = block_levels(key, extent, shards, -0.22, 0.18) if shards else 1.0
    drawn = jax.random.normal(key, extent, jnp.float32) * scale * factor_of
    return jnp.minimum(jnp.maximum(drawn, -limit), limit).astype(held_as)


def setup_inputs(seed: int = 0) -> dict:
    splits = jax.random.split(jax.random.key(seed), 10)
    return {
        "query_in": scatter_about(splits[0], (TOKENS, D), 1.0, 6.0, ((0, 32), (1, 8))),
        "key_in": scatter_about(splits[1], (TOKENS, D), 1.0, 6.0, ((0, 32), (1, 8))),
        "value_in": scatter_about(splits[2], (TOKENS, D), 1.0, 6.0, ((0, 32), (1, 8))),
        "stream": scatter_about(splits[3], (TOKENS, D), 1.0, 6.0, ((0, 32), (1, 8))),
        "short_filter": scatter_about(splits[4], (3, SHORT, D), 0.6, 3.0, ((2, 8),), jnp.float32),
        "decay_rate": draw_decay_rate(jax.random.fold_in(splits[9], 71), 0),
        "residue": draw_residue(jax.random.fold_in(splits[9], 71), 0),
        "norm_gain": jnp.clip(1.0 + 0.1 * jax.random.normal(splits[7], (D,), jnp.float32), 0.5, 1.5),
        "cotangent": scatter_about(splits[8], (TOKENS, D), 1.0, 6.0, ((0, 32), (1, 8))),
    }


highest = lax.Precision.HIGHEST
epsilon = 1e-05

def modal_parts(signal, decay_rate, residue):
    length, channels = signal.shape
    modes = decay_rate.shape[0]
    block_len = min(64, length)
    count_blocks = length // block_len
    offsets = jnp.arange(block_len, dtype=jnp.int32)
    positions = offsets.astype(jnp.float32)
    rising = jnp.exp(decay_rate[None] * positions[:, None, None])
    falling = jnp.exp(-decay_rate[None] * positions[:, None, None])
    lower = (offsets[:, None] >= offsets[None, :]).astype(jnp.float32)
    blocked = signal.reshape(count_blocks, block_len, channels)
    weighted = (blocked[:, :, None, :] * rising[None]).reshape(count_blocks, block_len, modes * channels)
    summed = jnp.einsum('ts,nsx->ntx', lower, weighted, precision=highest).reshape(count_blocks, block_len, modes, channels)
    states = summed * falling[None]
    inside = lax.optimization_barrier(jnp.sum(states * residue[None, None], axis=2))
    endings = states[:, block_len - 1]
    block_decay = jnp.exp(-decay_rate * block_len)

    def advance(state, ended):
        return (block_decay * state + ended, state)
    final, starting = lax.scan(advance, jnp.zeros(decay_rate.shape, jnp.float32), endings)
    return (inside, starting, final)

def modal_finish(inside, starting, arriving, decay_rate, residue):
    count_blocks, block_len, channels = inside.shape
    positions = jnp.arange(block_len, dtype=jnp.float32)
    block_starts = jnp.arange(count_blocks, dtype=jnp.float32) * block_len
    carried = starting + jnp.exp(-decay_rate[None] * block_starts[:, None, None]) * arriving[None]
    entering = residue[None] * jnp.exp(-decay_rate[None] * (positions + 1.0)[:, None, None])
    output = inside + lax.optimization_barrier(jnp.sum(entering[None] * carried[:, None], axis=2))
    return output.reshape(count_blocks * block_len, channels)

def short_mix(signal, taps):
    padded = jnp.pad(signal, ((2, 0), (0, 0)))
    return taps[0] * padded[2:] + taps[1] * padded[1:-1] + taps[2] * padded[:-2]

def group_mix(query_in, key_in, value_in, taps, decay_rate, residue):
    query_mix = short_mix(query_in, taps[0])
    key_mix = short_mix(key_in, taps[1])
    value_mix = short_mix(value_in, taps[2])
    product = key_mix * value_mix
    inside, starting, final = modal_parts(product, decay_rate, residue)
    conv = modal_finish(inside, starting, jnp.zeros(decay_rate.shape, jnp.float32), decay_rate, residue)
    return query_mix * conv

def reference(query_in, key_in, value_in, stream, short_filter, decay_rate, residue, norm_gain, cotangent):
    groups = N_TP
    channels = D // groups

    def split(array):
        return array.reshape(TOKENS, groups, channels).transpose(1, 0, 2)

    def merge(array):
        return array.transpose(1, 0, 2).reshape(TOKENS, D).astype(jnp.bfloat16)
    taps_grouped = short_filter.reshape(3, SHORT, groups, channels).transpose(2, 0, 1, 3)
    rates_grouped = decay_rate.reshape(MODES, groups, channels).transpose(1, 0, 2)
    residues_grouped = residue.reshape(MODES, groups, channels).transpose(1, 0, 2)
    query_split = split(query_in)
    key_split = split(key_in)
    value_split = split(value_in)

    def forward_group(items):
        query_part, key_part, value_part, stream_part, taps, rates, residues = items
        return stream_part.astype(jnp.float32) + group_mix(query_part.astype(jnp.float32), key_part.astype(jnp.float32), value_part.astype(jnp.float32), taps, rates, residues)
    mixed = lax.map(forward_group, (query_split, key_split, value_split, split(stream), taps_grouped, rates_grouped, residues_grouped))
    squares = lax.optimization_barrier(jnp.sum(mixed * mixed, axis=(0, 2)))
    inverse = lax.rsqrt(squares / D + epsilon)
    gains = norm_gain.reshape(groups, 1, channels)
    normed = mixed * inverse[None, :, None] * gains
    scaled = gains * split(cotangent).astype(jnp.float32)
    inner = lax.optimization_barrier(jnp.sum(scaled * mixed, axis=(0, 2)))
    dmixed = inverse[None, :, None] * scaled - mixed * (inverse ** 3 * inner / D)[None, :, None]

    def backward_group(items):
        query_part, key_part, value_part, taps, rates, residues, upstream = items

        def local_mix(first, second, third):
            return group_mix(first, second, third, taps, rates, residues)
        unused, pullback = jax.vjp(local_mix, query_part.astype(jnp.float32), key_part.astype(jnp.float32), value_part.astype(jnp.float32))
        return pullback(upstream)
    query_grad, key_grad, value_grad = lax.map(backward_group, (query_split, key_split, value_split, taps_grouped, rates_grouped, residues_grouped, dmixed))
    return (merge(normed), merge(dmixed), merge(query_grad), merge(key_grad), merge(value_grad))
```

```python
import functools

import jax
import jax.numpy as jnp
from jax import lax
from jax.experimental import pallas as pl
from jax.experimental.pallas import tpu as pltpu
from jax.sharding import PartitionSpec as P

MESH = pl.DeviceIdType.MESH
f32 = jnp.float32
epsilon = 1e-05
LANES = 128
SUBS = 8


def kernel(
    n_seq,
    n_tp,
    q_hbm,
    k_hbm,
    v_hbm,
    s_hbm,
    c_hbm,
    taps_ref,
    rate_ref,
    res_ref,
    gain_ref,
    normed_hbm,
    sgrad_hbm,
    qgrad_hbm,
    kgrad_hbm,
    vgrad_hbm,
    inb,
    nat,
    par,
    tapn,
    dec,
    res,
    km,
    vm,
    qm,
    pr,
    cv,
    st,
    sc,
    mx,
    dm,
    dc,
    dp,
    rows,
    outb,
    halo_s,
    halo_r,
    head_s,
    head_r,
    big,
    fs,
    rx,
    ax,
    ar,
    pss,
    psr,
    in_sem,
    out_sem,
    send_sem,
    recv_sem,
):
    me = lax.axis_index("seq")
    mt = lax.axis_index("tp")
    length = km.shape[0]
    modes = rate_ref.shape[0]
    chunks = length // SUBS
    width = float(n_tp * SUBS * LANES)

    loads = []
    for a, src in enumerate((k_hbm, v_hbm, q_hbm, s_hbm, c_hbm)):
        copy = pltpu.make_async_copy(src, inb.at[a], in_sem.at[a])
        copy.start()
        loads.append(copy)

    barrier = pltpu.get_barrier_semaphore()

    def greet_seq(k, carry):
        other = lax.rem(me + 1 + k, n_seq)
        pl.semaphore_signal(barrier, inc=1, device_id={"seq": other}, device_id_type=MESH)
        return carry

    def greet_tp(k, carry):
        other = lax.rem(mt + 1 + k, n_tp)
        pl.semaphore_signal(barrier, inc=1, device_id={"tp": other}, device_id_type=MESH)
        return carry

    lax.fori_loop(0, n_seq - 1, greet_seq, 0)
    lax.fori_loop(0, n_tp - 1, greet_tp, 0)

    for source, into in ((rate_ref, dec), (res_ref, res)):
        for i in range(modes // SUBS):
            for j in range(SUBS):
                par[pl.ds(i * 64 + j * 8, 8), :] = source[
                    pl.ds(i * 8, 8), pl.ds(j * LANES, LANES)
                ]
        for m in range(modes):
            into[m] = par[pl.ds((m // 8) * 64 + m % 8, 8, stride=8), :]
    for a in range(3):
        for j in range(SUBS):
            tapn[pl.ds((a * 8 + j) * 8, 3), :] = taps_ref[a, :, pl.ds(j * LANES, LANES)]

    def tap(a, b):
        return tapn[pl.ds(a * 64 + b, 8, stride=8), :]

    rate = dec[...]
    big[0] = jnp.exp(rate * (-float(length)))
    big[1] = jnp.exp(rate * (-float(length - 2)))
    dec[...] = jnp.exp(-rate)

    def to_tiles(a):
        loads[a].wait()

        def step(i, carry):
            block = inb[a, pl.ds(pl.multiple_of(i * 16, 16), 16), :].astype(f32)
            for h in range(2):
                for j in range(SUBS):
                    nat[a, pl.ds(pl.multiple_of(i * 128 + h * 64 + j * 8, 8), 8), :] = block[
                        h * 8 : h * 8 + 8, j * LANES : (j + 1) * LANES
                    ]
            return carry

        lax.fori_loop(0, length // 16, step, 0)

    def row(a, i, s):
        return nat[a, pl.ds(i * 64 + s, 8, stride=8), :]

    def put_row(a, i, s, value):
        nat[a, pl.ds(i * 64 + s, 8, stride=8), :] = value

    zero = jnp.zeros((SUBS, LANES), f32)
    to_tiles(0)
    to_tiles(1)

    def first_pass(i, carry):
        state, k1, k2, v1, v2 = carry
        d = dec[...]
        for s in range(SUBS):
            k0, v0 = row(0, i, s), row(1, i, s)
            kmix = tap(1, 0) * k0 + tap(1, 1) * k1 + tap(1, 2) * k2
            vmix = tap(2, 0) * v0 + tap(2, 1) * v1 + tap(2, 2) * v2
            prod = kmix * vmix
            km[i * 8 + s] = kmix
            vm[i * 8 + s] = vmix
            pr[i * 8 + s] = prod
            state = d * state + prod[None]
            k1, k2, v1, v2 = k0, k1, v0, v1
        return state, k1, k2, v1, v2

    state0 = jnp.zeros((modes, SUBS, LANES), f32)
    final, k1, k2, v1, v2 = lax.fori_loop(0, chunks, first_pass, (state0, zero, zero, zero, zero))
    dp[pl.ds(0, modes)] = final
    halo_s[0], halo_s[1], halo_s[2], halo_s[3] = k2, k1, v2, v1

    to_tiles(2)
    halo_s[4] = row(2, chunks - 1, 6)
    halo_s[5] = row(2, chunks - 1, 7)

    pl.semaphore_wait(barrier, n_seq - 1 + n_tp - 1)

    def halo_copy():
        return pltpu.make_async_remote_copy(
            src_ref=halo_s,
            dst_ref=halo_r,
            send_sem=send_sem.at[0],
            recv_sem=recv_sem.at[0],
            device_id={"seq": me + 1},
            device_id_type=MESH,
        )

    @pl.when(me < n_seq - 1)
    def _():
        halo_copy().start()

    @pl.when(me == 0)
    def _():
        halo_r[...] = jnp.zeros_like(halo_r)

    @pl.when(me > 0)
    def _():
        halo_copy().wait_recv()

    d = dec[...]
    hk2, hk1, hv2, hv1 = halo_r[0], halo_r[1], halo_r[2], halo_r[3]
    old0, old1 = pr[0], pr[1]
    km0 = km[0] + tap(1, 1) * hk1 + tap(1, 2) * hk2
    km1 = km[1] + tap(1, 2) * hk1
    vm0 = vm[0] + tap(2, 1) * hv1 + tap(2, 2) * hv2
    vm1 = vm[1] + tap(2, 2) * hv1
    km[0], km[1], vm[0], vm[1] = km0, km1, vm0, vm1
    pr0, pr1 = km0 * vm0, km1 * vm1
    pr[0], pr[1] = pr0, pr1
    lift = (d * (pr0 - old0)[None] + (pr1 - old1)[None]) * big[1]
    final = dp[pl.ds(0, modes)] + lift

    def exchange(which, source, into):
        def send(k, carry):
            sign = 1 - 2 * lax.rem(k, 2)
            offset = n_seq // 2 + sign * ((k + 1) // 2)
            other = lax.rem(me + offset, n_seq)
            pltpu.make_async_remote_copy(
                src_ref=source.at[other],
                dst_ref=into.at[me],
                send_sem=send_sem.at[which],
                recv_sem=recv_sem.at[which],
                device_id={"seq": other},
                device_id_type=MESH,
            ).start()
            return carry

        lax.fori_loop(0, n_seq - 1, send, 0)
        into[me] = source[me]

    def landed(which, into):
        others = into.at[pl.ds(0, n_seq - 1)]
        pltpu.make_async_copy(others, others, recv_sem.at[which]).wait()

    def sent(which, source):
        others = source.at[pl.ds(0, n_seq - 1)]
        pltpu.make_async_copy(others, others, send_sem.at[which]).wait()

    def put_state(slot, value):
        for m in range(modes):
            fs[slot, 2 * m] = value[m, 0:4]
            fs[slot, 2 * m + 1] = value[m, 4:8]

    def get_state(slot):
        return ar[slot].reshape(modes, SUBS, LANES)

    for m in range(modes):
        fs[2, 2 * m] = big[0, m, 0:4]
        fs[2, 2 * m + 1] = big[0, m, 4:8]

    put_state(0, final)
    exchange(1, fs.at[0], rx.at[0])

    to_tiles(3)
    to_tiles(4)
    hq2, hq1 = halo_r[4], halo_r[5]
    gain = gain_ref[...]

    def middle_pass(i, carry):
        q1, q2 = carry
        for s in range(SUBS):
            q0 = row(2, i, s)
            qm[i * 8 + s] = tap(0, 0) * q0 + tap(0, 1) * q1 + tap(0, 2) * q2
            st[i * 8 + s] = row(3, i, s)
            sc[i * 8 + s] = gain * row(4, i, s)
            q1, q2 = q0, q1
        return q1, q2

    landed(1, rx.at[0])
    step_decay = fs[2, me]

    def scan_forward(p, state):
        ax[0, p] = state
        return step_decay * state + rx[0, p]

    lax.fori_loop(0, n_seq, scan_forward, jnp.zeros((4, LANES), f32))
    exchange(2, ax.at[0], ar.at[0])

    lax.fori_loop(0, chunks, middle_pass, (hq1, hq2))

    def local_pass(i, state):
        d, r = dec[...], res[...]
        block = pr[pl.ds(i * 8, 8)]
        for s in range(SUBS):
            state = d * state + block[s][None]
            cv[i * 8 + s] = jnp.sum(r * state, axis=0)
        return state

    lax.fori_loop(0, chunks, local_pass, state0)

    landed(2, ar.at[0])
    arrived = res[...] * dec[...] * get_state(0)

    def join_pass(i, state):
        d = dec[...]
        for s in range(SUBS):
            t = i * 8 + s
            conv = cv[t] + jnp.sum(state, axis=0)
            state = d * state
            mixed = st[t] + qm[t] * conv
            cv[t] = conv
            mx[t] = mixed
            put_row(0, i, s, mixed * mixed)
            put_row(1, i, s, sc[t] * mixed)
        return state

    lax.fori_loop(0, chunks, join_pass, arrived)

    for a in range(2):
        for i in range(chunks):
            total = nat[a, pl.ds(i * 64, 8), :]
            for j in range(1, SUBS):
                total = total + nat[a, pl.ds(i * 64 + j * 8, 8), :]
            rows[a, pl.ds(i * 8, 8), :] = total
        pss[pl.ds(a, 1), :] = jnp.sum(rows[a].T, axis=0, keepdims=True)

    def share(k, carry):
        other = lax.rem(mt + 1 + k, n_tp)
        pltpu.make_async_remote_copy(
            src_ref=pss,
            dst_ref=psr.at[mt],
            send_sem=send_sem.at[3],
            recv_sem=recv_sem.at[3],
            device_id={"tp": other},
            device_id_type=MESH,
        ).start()
        return carry

    lax.fori_loop(0, n_tp - 1, share, 0)
    psr[mt] = pss[...]
    peers = psr.at[pl.ds(0, n_tp - 1)]
    pltpu.make_async_copy(peers, peers, recv_sem.at[3]).wait()
    totals = jnp.sum(psr[...], axis=0)
    inverse = lax.rsqrt(totals[0:1] / width + epsilon)
    factor = inverse * inverse * inverse * totals[1:2] / width
    rows[0] = jnp.broadcast_to(inverse, (length, LANES)).T
    rows[1] = jnp.broadcast_to(factor, (length, LANES)).T

    def spread(a, t):
        return jnp.broadcast_to(rows[a, pl.ds(t, 1), :], (SUBS, LANES))

    def back_pass(n, state):
        i = chunks - 1 - n
        d = dec[...]
        for s in reversed(range(SUBS)):
            t = i * 8 + s
            dmixed = spread(0, t) * sc[t] - mx[t] * spread(1, t)
            dconv = dmixed * qm[t]
            dm[t] = dmixed
            dc[t] = dconv
            state = d * state + dconv[None]
        return state

    final_back = lax.fori_loop(0, chunks, back_pass, state0)
    put_state(1, final_back)
    exchange(4, fs.at[1], rx.at[1])

    head_s[0] = dm[0] * cv[0]
    head_s[1] = dm[1] * cv[1]
    head_s[2] = dc[0]
    head_s[3], head_s[4] = km[0], km[1]
    head_s[5], head_s[6] = vm[0], vm[1]

    def head_copy():
        return pltpu.make_async_remote_copy(
            src_ref=head_s,
            dst_ref=head_r,
            send_sem=send_sem.at[6],
            recv_sem=recv_sem.at[6],
            device_id={"seq": me - 1},
            device_id_type=MESH,
        )

    @pl.when(me > 0)
    def _():
        head_copy().start()

    @pl.when(me == n_seq - 1)
    def _():
        head_r[...] = jnp.zeros_like(head_r)

    landed(4, rx.at[1])

    def scan_backward(n, state):
        p = n_seq - 1 - n
        ax[1, p] = state
        return step_decay * state + rx[1, p]

    lax.fori_loop(0, n_seq, scan_backward, jnp.zeros((4, LANES), f32))
    exchange(5, ax.at[1], ar.at[1])

    def adjoint_pass(n, state):
        i = chunks - 1 - n
        d, r = dec[...], res[...]
        for s in reversed(range(SUBS)):
            state = d * state + dc[i * 8 + s][None]
            dp[i * 8 + s] = jnp.sum(r * state, axis=0)
        return state

    lax.fori_loop(0, chunks, adjoint_pass, state0)

    @pl.when(me < n_seq - 1)
    def _():
        head_copy().wait_recv()

    def query_pass(n, carry):
        g1, g2 = carry
        i = chunks - 1 - n
        for s in reversed(range(SUBS)):
            t = i * 8 + s
            dmixed = dm[t]
            g0 = dmixed * cv[t]
            put_row(0, i, s, mx[t] * spread(0, t) * gain)
            put_row(1, i, s, dmixed)
            put_row(2, i, s, tap(0, 0) * g0 + tap(0, 1) * g1 + tap(0, 2) * g2)
            g1, g2 = g0, g1
        return g1, g2

    lax.fori_loop(0, chunks, query_pass, (head_r[0], head_r[1]))

    stores = []

    def from_tiles(a, out, target):
        def step(i, carry):
            for j in range(SUBS):
                block = jnp.concatenate(
                    [
                        nat[a, pl.ds(pl.multiple_of(i * 128 + j * 8, 8), 8), :],
                        nat[a, pl.ds(pl.multiple_of(i * 128 + 64 + j * 8, 8), 8), :],
                    ],
                    axis=0,
                )
                outb[out, pl.ds(pl.multiple_of(i * 16, 16), 16), pl.ds(j * LANES, LANES)] = (
                    block.astype(jnp.bfloat16)
                )
            return carry

        lax.fori_loop(0, length // 16, step, 0)
        copy = pltpu.make_async_copy(outb.at[out], target, out_sem.at[out])
        copy.start()
        stores.append(copy)

    from_tiles(0, 0, normed_hbm)
    from_tiles(1, 1, sgrad_hbm)
    from_tiles(2, 2, qgrad_hbm)

    landed(5, ar.at[1])
    d, r = dec[...], res[...]
    after = get_state(1)
    arrived_back = r * d * after
    dp0 = jnp.sum(r * after, axis=0)
    dp1 = jnp.sum(r * ((after - head_r[2][None]) / d), axis=0)
    carry0 = (
        arrived_back,
        dp0 * head_r[5],
        dp1 * head_r[6],
        dp0 * head_r[3],
        dp1 * head_r[4],
    )

    def last_pass(n, carry):
        state, a1, a2, b1, b2 = carry
        i = chunks - 1 - n
        d = dec[...]
        for s in reversed(range(SUBS)):
            t = i * 8 + s
            dproduct = dp[t] + jnp.sum(state, axis=0)
            state = d * state
            a0 = dproduct * vm[t]
            b0 = dproduct * km[t]
            put_row(3, i, s, tap(1, 0) * a0 + tap(1, 1) * a1 + tap(1, 2) * a2)
            put_row(4, i, s, tap(2, 0) * b0 + tap(2, 1) * b1 + tap(2, 2) * b2)
            a1, a2, b1, b2 = a0, a1, b0, b1
        return state, a1, a2, b1, b2

    lax.fori_loop(0, chunks, last_pass, carry0)
    from_tiles(3, 3, kgrad_hbm)
    from_tiles(4, 4, vgrad_hbm)

    @pl.when(me < n_seq - 1)
    def _():
        halo_copy().wait_send()

    @pl.when(me > 0)
    def _():
        head_copy().wait_send()

    sent(1, fs.at[0])
    sent(2, ax.at[0])
    sent(4, fs.at[1])
    sent(5, ax.at[1])
    pltpu.make_async_copy(peers, peers, send_sem.at[3]).wait()
    for copy in stores:
        copy.wait()


def solution(mesh):
    n_seq, n_tp = mesh.shape["seq"], mesh.shape["tp"]

    def body(q, k, v, stream, taps, rate, residue, gain, cotangent):
        length, channels = q.shape
        modes = rate.shape[0]
        assert channels == SUBS * LANES and modes * 2 == n_seq and length == LANES
        hbm = pl.BlockSpec(memory_space=pl.ANY)
        vmem = pl.BlockSpec(memory_space=pltpu.VMEM)
        out = jax.ShapeDtypeStruct((length, channels), jnp.bfloat16)
        tiles = pltpu.VMEM((length, SUBS, LANES), f32)
        per_mode = pltpu.VMEM((modes, SUBS, LANES), f32)
        slices = (n_seq, 4, LANES)
        return pl.pallas_call(
            functools.partial(kernel, n_seq, n_tp),
            out_shape=(out,) * 5,
            in_specs=[hbm] * 5 + [vmem] * 4,
            out_specs=(hbm,) * 5,
            scratch_shapes=[
                pltpu.VMEM((5, length, channels), jnp.bfloat16),
                pltpu.VMEM((5, length * SUBS, LANES), f32),
                pltpu.VMEM((modes * SUBS, LANES), f32),
                pltpu.VMEM((3 * 64, LANES), f32),
                per_mode,
                per_mode,
            ]
            + [tiles] * 11
            + [
                pltpu.VMEM((2, length, LANES), f32),
                pltpu.VMEM((5, length, channels), jnp.bfloat16),
                pltpu.VMEM((6, SUBS, LANES), f32),
                pltpu.VMEM((6, SUBS, LANES), f32),
                pltpu.VMEM((7, SUBS, LANES), f32),
                pltpu.VMEM((7, SUBS, LANES), f32),
                pltpu.VMEM((2, modes, SUBS, LANES), f32),
                pltpu.VMEM((3,) + slices, f32),
                pltpu.VMEM((2,) + slices, f32),
                pltpu.VMEM((2,) + slices, f32),
                pltpu.VMEM((2,) + slices, f32),
                pltpu.VMEM((2, LANES), f32),
                pltpu.VMEM((n_tp, 2, LANES), f32),
                pltpu.SemaphoreType.DMA((5,)),
                pltpu.SemaphoreType.DMA((5,)),
                pltpu.SemaphoreType.DMA((7,)),
                pltpu.SemaphoreType.DMA((7,)),
            ],
            compiler_params=pltpu.CompilerParams(
                collective_id=0, has_side_effects=True, vmem_limit_bytes=40 * 1024 * 1024
            ),
        )(q, k, v, stream, cotangent, taps, rate, residue, gain.reshape(SUBS, LANES))

    seq_tp = P("seq", "tp")
    return jax.shard_map(
        body,
        mesh=mesh,
        in_specs=(
            seq_tp,
            seq_tp,
            seq_tp,
            seq_tp,
            P(None, None, "tp"),
            P(None, "tp"),
            P(None, "tp"),
            P("tp"),
            seq_tp,
        ),
        out_specs=(seq_tp,) * 5,
        check_vma=False,
    )
```

```python
import functools

import jax
import jax.numpy as jnp
from jax import lax
from jax.experimental import pallas as pl
from jax.experimental.pallas import tpu as pltpu
from jax.sharding import PartitionSpec as P

MESH = pl.DeviceIdType.MESH
f32 = jnp.float32
epsilon = 1e-05
LANES = 128
SUBS = 8


def kernel(
    n_seq,
    n_tp,
    q_hbm,
    k_hbm,
    v_hbm,
    s_hbm,
    c_hbm,
    taps_hbm,
    rate_hbm,
    res_hbm,
    gain_hbm,
    normed_ref,
    sgrad_ref,
    qgrad_ref,
    kgrad_ref,
    vgrad_ref,
    inb,
    taps_ref,
    rate_ref,
    res_ref,
    gain_ref,
    nat,
    par,
    tapn,
    dec,
    res,
    km,
    vm,
    qm,
    pr,
    cv,
    st,
    sc,
    mx,
    dm,
    dc,
    dp,
    rows,
    halo_s,
    halo_r,
    head_s,
    head_r,
    big,
    fs,
    rx,
    ax,
    ar,
    pss,
    psr,
    in_sem,
    send_sem,
    recv_sem,
):
    me = lax.axis_index("seq")
    mt = lax.axis_index("tp")
    length = km.shape[0]
    modes = rate_ref.shape[0]
    chunks = length // SUBS
    width = float(n_tp * SUBS * LANES)

    barrier = pltpu.get_barrier_semaphore()

    def greet_seq(k, carry):
        other = lax.rem(me + 1 + k, n_seq)
        pl.semaphore_signal(barrier, inc=1, device_id={"seq": other}, device_id_type=MESH)
        return carry

    def greet_tp(k, carry):
        other = lax.rem(mt + 1 + k, n_tp)
        pl.semaphore_signal(barrier, inc=1, device_id={"tp": other}, device_id_type=MESH)
        return carry

    lax.fori_loop(0, n_seq - 1, greet_seq, 0)
    lax.fori_loop(0, n_tp - 1, greet_tp, 0)

    loads = []
    for a, (src, into) in enumerate(
        (
            (k_hbm, inb.at[0]),
            (v_hbm, inb.at[1]),
            (q_hbm, inb.at[2]),
            (taps_hbm, taps_ref),
            (rate_hbm, rate_ref),
            (s_hbm, inb.at[3]),
            (c_hbm, inb.at[4]),
            (res_hbm, res_ref),
            (gain_hbm, gain_ref),
        )
    ):
        copy = pltpu.make_async_copy(src, into, in_sem.at[a])
        copy.start()
        loads.append(copy)
    at_load = (0, 1, 2, 5, 6)


    def per_mode(source, into):
        for i in range(modes // SUBS):
            for j in range(SUBS):
                par[pl.ds(i * 64 + j * 8, 8), :] = source[
                    pl.ds(i * 8, 8), pl.ds(j * LANES, LANES)
                ]
        for m in range(modes):
            into[m] = par[pl.ds((m // 8) * 64 + m % 8, 8, stride=8), :]

    def tap_rows():
        for a in range(3):
            for j in range(SUBS):
                tapn[pl.ds((a * 8 + j) * 8, 3), :] = taps_ref[a, :, pl.ds(j * LANES, LANES)]

    def tap(a, b):
        return tapn[pl.ds(a * 64 + b, 8, stride=8), :]

    def to_tiles(a, first, last):
        def step(i, carry):
            block = inb[a, pl.ds(pl.multiple_of(i * 16, 16), 16), :].astype(f32)
            for h in range(2):
                for j in range(SUBS):
                    nat[a, pl.ds(pl.multiple_of(i * 128 + h * 64 + j * 8, 8), 8), :] = block[
                        h * 8 : h * 8 + 8, j * LANES : (j + 1) * LANES
                    ]
            return carry

        lax.fori_loop(first, last, step, 0)

    def row(a, i, s):
        return nat[a, pl.ds(i * 64 + s, 8, stride=8), :]

    def put_row(a, i, s, value):
        nat[a, pl.ds(i * 64 + s, 8, stride=8), :] = value

    zero = jnp.zeros((SUBS, LANES), f32)
    blocks = length // 16
    for a in range(3):
        loads[a].wait()
        to_tiles(a, blocks - 1, blocks)
        halo_s[2 * a] = row(a, chunks - 1, 6)
        halo_s[2 * a + 1] = row(a, chunks - 1, 7)

    pl.semaphore_wait(barrier, n_seq - 1 + n_tp - 1)

    def halo_copy():
        return pltpu.make_async_remote_copy(
            src_ref=halo_s,
            dst_ref=halo_r,
            send_sem=send_sem.at[0],
            recv_sem=recv_sem.at[0],
            device_id={"seq": me + 1},
            device_id_type=MESH,
        )

    @pl.when(me < n_seq - 1)
    def _():
        halo_copy().start()

    loads[3].wait()
    tap_rows()
    loads[4].wait()
    per_mode(rate_ref, dec)
    rate = dec[...]
    big[0] = jnp.exp(rate * (-float(length)))
    big[1] = jnp.exp(rate * (-float(length - 2)))
    dec[...] = jnp.exp(-rate)

    to_tiles(0, 0, blocks - 1)
    to_tiles(1, 0, blocks - 1)

    def first_pass(i, carry):
        state, k1, k2, v1, v2 = carry
        d = dec[...]
        for s in range(SUBS):
            k0, v0 = row(0, i, s), row(1, i, s)
            kmix = tap(1, 0) * k0 + tap(1, 1) * k1 + tap(1, 2) * k2
            vmix = tap(2, 0) * v0 + tap(2, 1) * v1 + tap(2, 2) * v2
            prod = kmix * vmix
            km[i * 8 + s] = kmix
            vm[i * 8 + s] = vmix
            pr[i * 8 + s] = prod
            state = d * state + prod[None]
            k1, k2, v1, v2 = k0, k1, v0, v1
        return state, k1, k2, v1, v2

    state0 = jnp.zeros((modes, SUBS, LANES), f32)
    final, k1, k2, v1, v2 = lax.fori_loop(0, chunks, first_pass, (state0, zero, zero, zero, zero))
    dp[pl.ds(0, modes)] = final

    @pl.when(me == 0)
    def _():
        halo_r[...] = jnp.zeros_like(halo_r)

    @pl.when(me > 0)
    def _():
        halo_copy().wait_recv()

    d = dec[...]
    hk2, hk1, hv2, hv1 = halo_r[0], halo_r[1], halo_r[2], halo_r[3]
    old0, old1 = pr[0], pr[1]
    km0 = km[0] + tap(1, 1) * hk1 + tap(1, 2) * hk2
    km1 = km[1] + tap(1, 2) * hk1
    vm0 = vm[0] + tap(2, 1) * hv1 + tap(2, 2) * hv2
    vm1 = vm[1] + tap(2, 2) * hv1
    km[0], km[1], vm[0], vm[1] = km0, km1, vm0, vm1
    pr0, pr1 = km0 * vm0, km1 * vm1
    pr[0], pr[1] = pr0, pr1
    lift = (d * (pr0 - old0)[None] + (pr1 - old1)[None]) * big[1]
    final = dp[pl.ds(0, modes)] + lift

    def exchange(which, source, into):
        def send(k, carry):
            sign = 1 - 2 * lax.rem(k, 2)
            offset = n_seq // 2 + sign * ((k + 1) // 2)
            other = lax.rem(me + offset, n_seq)
            pltpu.make_async_remote_copy(
                src_ref=source.at[other],
                dst_ref=into.at[me],
                send_sem=send_sem.at[which],
                recv_sem=recv_sem.at[which],
                device_id={"seq": other},
                device_id_type=MESH,
            ).start()
            return carry

        lax.fori_loop(0, n_seq - 1, send, 0)
        into[me] = source[me]

    def landed(which, into):
        others = into.at[pl.ds(0, n_seq - 1)]
        pltpu.make_async_copy(others, others, recv_sem.at[which]).wait()

    def sent(which, source):
        others = source.at[pl.ds(0, n_seq - 1)]
        pltpu.make_async_copy(others, others, send_sem.at[which]).wait()

    def put_state(slot, value):
        for m in range(modes):
            fs[slot, 2 * m] = value[m, 0:4]
            fs[slot, 2 * m + 1] = value[m, 4:8]

    def get_state(slot):
        return ar[slot].reshape(modes, SUBS, LANES)

    for m in range(modes):
        fs[2, 2 * m] = big[0, m, 0:4]
        fs[2, 2 * m + 1] = big[0, m, 4:8]

    put_state(0, final)
    exchange(1, fs.at[0], rx.at[0])

    for a in range(3, 5):
        loads[at_load[a]].wait()
        to_tiles(a, 0, blocks)
    to_tiles(2, 0, blocks - 1)
    loads[7].wait()
    per_mode(res_ref, res)
    loads[8].wait()
    hq2, hq1 = halo_r[4], halo_r[5]
    gain = gain_ref[...]

    def middle_pass(i, carry):
        q1, q2 = carry
        for s in range(SUBS):
            q0 = row(2, i, s)
            qm[i * 8 + s] = tap(0, 0) * q0 + tap(0, 1) * q1 + tap(0, 2) * q2
            st[i * 8 + s] = row(3, i, s)
            sc[i * 8 + s] = gain * row(4, i, s)
            q1, q2 = q0, q1
        return q1, q2

    landed(1, rx.at[0])
    step_decay = fs[2, me]

    def scan_forward(p, state):
        ax[0, p] = state
        return step_decay * state + rx[0, p]

    lax.fori_loop(0, n_seq, scan_forward, jnp.zeros((4, LANES), f32))
    exchange(2, ax.at[0], ar.at[0])

    lax.fori_loop(0, chunks, middle_pass, (hq1, hq2))

    def local_pass(i, state):
        d, r = dec[...], res[...]
        block = pr[pl.ds(i * 8, 8)]
        for s in range(SUBS):
            state = d * state + block[s][None]
            cv[i * 8 + s] = jnp.sum(r * state, axis=0)
        return state

    lax.fori_loop(0, chunks, local_pass, state0)

    landed(2, ar.at[0])
    arrived = res[...] * dec[...] * get_state(0)

    def join_pass(i, state):
        d = dec[...]
        for s in range(SUBS):
            t = i * 8 + s
            conv = cv[t] + jnp.sum(state, axis=0)
            state = d * state
            mixed = st[t] + qm[t] * conv
            cv[t] = conv
            mx[t] = mixed
            put_row(0, i, s, mixed * mixed)
            put_row(1, i, s, sc[t] * mixed)
        return state

    lax.fori_loop(0, chunks, join_pass, arrived)

    for a in range(2):
        for i in range(chunks):
            total = nat[a, pl.ds(i * 64, 8), :]
            for j in range(1, SUBS):
                total = total + nat[a, pl.ds(i * 64 + j * 8, 8), :]
            rows[a, pl.ds(i * 8, 8), :] = total
        pss[pl.ds(a, 1), :] = jnp.sum(rows[a].T, axis=0, keepdims=True)

    def share(k, carry):
        other = lax.rem(mt + 1 + k, n_tp)
        pltpu.make_async_remote_copy(
            src_ref=pss,
            dst_ref=psr.at[mt],
            send_sem=send_sem.at[3],
            recv_sem=recv_sem.at[3],
            device_id={"tp": other},
            device_id_type=MESH,
        ).start()
        return carry

    lax.fori_loop(0, n_tp - 1, share, 0)
    psr[mt] = pss[...]
    peers = psr.at[pl.ds(0, n_tp - 1)]
    pltpu.make_async_copy(peers, peers, recv_sem.at[3]).wait()
    totals = jnp.sum(psr[...], axis=0)
    inverse = lax.rsqrt(totals[0:1] / width + epsilon)
    factor = inverse * inverse * inverse * totals[1:2] / width
    rows[0] = jnp.broadcast_to(inverse, (length, LANES)).T
    rows[1] = jnp.broadcast_to(factor, (length, LANES)).T

    def spread(a, t):
        return jnp.broadcast_to(rows[a, pl.ds(t, 1), :], (SUBS, LANES))

    def back_pass(n, state):
        i = chunks - 1 - n
        d = dec[...]
        for s in reversed(range(SUBS)):
            t = i * 8 + s
            dmixed = spread(0, t) * sc[t] - mx[t] * spread(1, t)
            dconv = dmixed * qm[t]
            dm[t] = dmixed
            dc[t] = dconv
            state = d * state + dconv[None]
        return state

    final_back = lax.fori_loop(0, chunks, back_pass, state0)
    put_state(1, final_back)
    exchange(4, fs.at[1], rx.at[1])

    head_s[0] = dm[0] * cv[0]
    head_s[1] = dm[1] * cv[1]
    head_s[2] = dc[0]
    head_s[3], head_s[4] = km[0], km[1]
    head_s[5], head_s[6] = vm[0], vm[1]

    def head_copy():
        return pltpu.make_async_remote_copy(
            src_ref=head_s,
            dst_ref=head_r,
            send_sem=send_sem.at[6],
            recv_sem=recv_sem.at[6],
            device_id={"seq": me - 1},
            device_id_type=MESH,
        )

    @pl.when(me > 0)
    def _():
        head_copy().start()

    @pl.when(me == n_seq - 1)
    def _():
        head_r[...] = jnp.zeros_like(head_r)

    landed(4, rx.at[1])

    def scan_backward(n, state):
        p = n_seq - 1 - n
        ax[1, p] = state
        return step_decay * state + rx[1, p]

    lax.fori_loop(0, n_seq, scan_backward, jnp.zeros((4, LANES), f32))
    exchange(5, ax.at[1], ar.at[1])

    def adjoint_pass(n, state):
        i = chunks - 1 - n
        d, r = dec[...], res[...]
        for s in reversed(range(SUBS)):
            state = d * state + dc[i * 8 + s][None]
            dp[i * 8 + s] = jnp.sum(r * state, axis=0)
        return state

    lax.fori_loop(0, chunks, adjoint_pass, state0)

    @pl.when(me < n_seq - 1)
    def _():
        head_copy().wait_recv()

    def query_pass(n, carry):
        g1, g2 = carry
        i = chunks - 1 - n
        for s in reversed(range(SUBS)):
            t = i * 8 + s
            dmixed = dm[t]
            g0 = dmixed * cv[t]
            put_row(0, i, s, mx[t] * spread(0, t) * gain)
            put_row(1, i, s, dmixed)
            put_row(2, i, s, tap(0, 0) * g0 + tap(0, 1) * g1 + tap(0, 2) * g2)
            g1, g2 = g0, g1
        return g1, g2

    lax.fori_loop(0, chunks, query_pass, (head_r[0], head_r[1]))

    def from_tiles(a, target):
        def step(i, carry):
            for j in range(SUBS):
                block = jnp.concatenate(
                    [
                        nat[a, pl.ds(pl.multiple_of(i * 128 + j * 8, 8), 8), :],
                        nat[a, pl.ds(pl.multiple_of(i * 128 + 64 + j * 8, 8), 8), :],
                    ],
                    axis=0,
                )
                target[pl.ds(pl.multiple_of(i * 16, 16), 16), pl.ds(j * LANES, LANES)] = (
                    block.astype(jnp.bfloat16)
                )
            return carry

        lax.fori_loop(0, length // 16, step, 0)

    from_tiles(0, normed_ref)
    from_tiles(1, sgrad_ref)
    from_tiles(2, qgrad_ref)

    landed(5, ar.at[1])
    d, r = dec[...], res[...]
    after = get_state(1)
    arrived_back = r * d * after
    dp0 = jnp.sum(r * after, axis=0)
    dp1 = jnp.sum(r * ((after - head_r[2][None]) / d), axis=0)
    carry0 = (
        arrived_back,
        dp0 * head_r[5],
        dp1 * head_r[6],
        dp0 * head_r[3],
        dp1 * head_r[4],
    )

    def last_pass(n, carry):
        state, a1, a2, b1, b2 = carry
        i = chunks - 1 - n
        d = dec[...]
        for s in reversed(range(SUBS)):
            t = i * 8 + s
            dproduct = dp[t] + jnp.sum(state, axis=0)
            state = d * state
            a0 = dproduct * vm[t]
            b0 = dproduct * km[t]
            put_row(3, i, s, tap(1, 0) * a0 + tap(1, 1) * a1 + tap(1, 2) * a2)
            put_row(4, i, s, tap(2, 0) * b0 + tap(2, 1) * b1 + tap(2, 2) * b2)
            a1, a2, b1, b2 = a0, a1, b0, b1
        return state, a1, a2, b1, b2

    lax.fori_loop(0, chunks, last_pass, carry0)
    from_tiles(3, kgrad_ref)
    from_tiles(4, vgrad_ref)

    @pl.when(me < n_seq - 1)
    def _():
        halo_copy().wait_send()

    @pl.when(me > 0)
    def _():
        head_copy().wait_send()

    sent(1, fs.at[0])
    sent(2, ax.at[0])
    sent(4, fs.at[1])
    sent(5, ax.at[1])
    pltpu.make_async_copy(peers, peers, send_sem.at[3]).wait()


def write_out(*refs):
    sem = refs[-1]
    half = (len(refs) - 1) // 2
    copies = [
        pltpu.make_async_copy(refs[a], refs[half + a], sem.at[a]) for a in range(half)
    ]
    for copy in copies:
        copy.start()
    for copy in copies:
        copy.wait()


def solution(mesh):
    n_seq, n_tp = mesh.shape["seq"], mesh.shape["tp"]

    def body(q, k, v, stream, taps, rate, residue, gain, cotangent):
        length, channels = q.shape
        modes = rate.shape[0]
        assert channels == SUBS * LANES and modes * 2 == n_seq and length == LANES
        hbm = pl.BlockSpec(memory_space=pl.ANY)
        vmem = pl.BlockSpec(memory_space=pltpu.VMEM)
        out = jax.ShapeDtypeStruct((length, channels), jnp.bfloat16)
        tiles = pltpu.VMEM((length, SUBS, LANES), f32)
        per_mode = pltpu.VMEM((modes, SUBS, LANES), f32)
        slices = (n_seq, 4, LANES)
        operands = (q, k, v, stream, cotangent, taps, rate, residue, gain.reshape(SUBS, LANES))
        results = pl.pallas_call(
            functools.partial(kernel, n_seq, n_tp),
            out_shape=(out,) * 5,
            in_specs=[hbm] * 9,
            out_specs=(vmem,) * 5,
            scratch_shapes=[
                pltpu.VMEM((5, length, channels), jnp.bfloat16),
                pltpu.VMEM(taps.shape, f32),
                pltpu.VMEM(rate.shape, f32),
                pltpu.VMEM(rate.shape, f32),
                pltpu.VMEM((SUBS, LANES), f32),
                pltpu.VMEM((5, length * SUBS, LANES), f32),
                pltpu.VMEM((modes * SUBS, LANES), f32),
                pltpu.VMEM((3 * 64, LANES), f32),
                per_mode,
                per_mode,
            ]
            + [tiles] * 11
            + [
                pltpu.VMEM((2, length, LANES), f32),
                pltpu.VMEM((6, SUBS, LANES), f32),
                pltpu.VMEM((6, SUBS, LANES), f32),
                pltpu.VMEM((7, SUBS, LANES), f32),
                pltpu.VMEM((7, SUBS, LANES), f32),
                pltpu.VMEM((2, modes, SUBS, LANES), f32),
                pltpu.VMEM((3,) + slices, f32),
                pltpu.VMEM((2,) + slices, f32),
                pltpu.VMEM((2,) + slices, f32),
                pltpu.VMEM((2,) + slices, f32),
                pltpu.VMEM((2, LANES), f32),
                pltpu.VMEM((n_tp, 2, LANES), f32),
                pltpu.SemaphoreType.DMA((9,)),
                pltpu.SemaphoreType.DMA((7,)),
                pltpu.SemaphoreType.DMA((7,)),
            ],
            compiler_params=pltpu.CompilerParams(
                collective_id=0, has_side_effects=True, vmem_limit_bytes=40 * 1024 * 1024
            ),
        )(*[pltpu.with_memory_space_constraint(x, pltpu.HBM) for x in operands])
        return pl.pallas_call(
            write_out,
            out_shape=(out,) * 5,
            in_specs=[hbm] * 5,
            out_specs=(pl.BlockSpec(memory_space=pltpu.HBM),) * 5,
            scratch_shapes=[pltpu.SemaphoreType.DMA((5,))],
            compiler_params=pltpu.CompilerParams(vmem_limit_bytes=1024 * 1024),
        )(*results)

    seq_tp = P("seq", "tp")
    return jax.shard_map(
        body,
        mesh=mesh,
        in_specs=(
            seq_tp,
            seq_tp,
            seq_tp,
            seq_tp,
            P(None, None, "tp"),
            P(None, "tp"),
            P(None, "tp"),
            P("tp"),
            seq_tp,
        ),
        out_specs=(seq_tp,) * 5,
        check_vma=False,
    )
```

```python
import functools

import jax
import jax.numpy as jnp
from jax import lax
from jax.experimental import pallas as pl
from jax.experimental.pallas import tpu as pltpu
from jax.sharding import PartitionSpec as P

MESH = pl.DeviceIdType.MESH
f32 = jnp.float32
epsilon = 1e-05
LANES = 128
SUBS = 8


def swap_blocks(x, bits):
    low, high = bits
    y0 = jnp.where(low, pltpu.roll(x[1], 32, 1), x[0])
    y1 = jnp.where(low, x[1], pltpu.roll(x[0], 96, 1))
    y2 = jnp.where(low, pltpu.roll(x[3], 32, 1), x[2])
    y3 = jnp.where(low, x[3], pltpu.roll(x[2], 96, 1))
    return (
        jnp.where(high, pltpu.roll(y2, 64, 1), y0),
        jnp.where(high, pltpu.roll(y3, 64, 1), y1),
        jnp.where(high, y2, pltpu.roll(y0, 64, 1)),
        jnp.where(high, y3, pltpu.roll(y1, 64, 1)),
    )


def kernel(
    n_seq,
    n_tp,
    q_hbm,
    k_hbm,
    v_hbm,
    s_hbm,
    c_hbm,
    taps_hbm,
    rate_hbm,
    res_hbm,
    gain_hbm,
    normed_ref,
    sgrad_ref,
    qgrad_ref,
    kgrad_ref,
    vgrad_ref,
    inb,
    taps_ref,
    rate_ref,
    res_ref,
    gain_ref,
    nat,
    par,
    tapn,
    dec,
    res,
    km,
    vm,
    qm,
    pr,
    cv,
    st,
    sc,
    mx,
    dm,
    dc,
    dp,
    rows,
    halo_s,
    halo_r,
    head_s,
    head_r,
    fsf,
    fsb,
    rxf,
    rxb,
    dsl,
    lift,
    ax,
    ar,
    pss,
    psr,
    in_sem,
    send_sem,
    recv_sem,
):
    me = lax.axis_index("seq")
    mt = lax.axis_index("tp")
    length = km.shape[0]
    modes = rate_ref.shape[0]
    chunks = length // SUBS
    width = float(n_tp * SUBS * LANES)

    barrier = pltpu.get_barrier_semaphore()

    def partner(k):
        sign = 1 - 2 * lax.rem(k, 2)
        return lax.rem(me + n_seq // 2 + sign * ((k + 1) // 2), n_seq)

    def greet_seq(k, carry):
        other = partner(k)
        pl.semaphore_signal(barrier, inc=1, device_id={"seq": other}, device_id_type=MESH)
        return carry

    def greet_tp(k, carry):
        other = lax.rem(mt + 1 + k, n_tp)
        pl.semaphore_signal(barrier, inc=1, device_id={"tp": other}, device_id_type=MESH)
        return carry

    lax.fori_loop(0, n_seq - 1, greet_seq, 0)
    lax.fori_loop(0, n_tp - 1, greet_tp, 0)

    loads = []
    for a, (src, into) in enumerate(
        (
            (k_hbm, inb.at[0]),
            (v_hbm, inb.at[1]),
            (q_hbm, inb.at[2]),
            (taps_hbm, taps_ref),
            (rate_hbm, rate_ref),
            (s_hbm, inb.at[3]),
            (c_hbm, inb.at[4]),
            (res_hbm, res_ref),
            (gain_hbm, gain_ref),
        )
    ):
        copy = pltpu.make_async_copy(src, into, in_sem.at[a])
        copy.start()
        loads.append(copy)
    at_load = (0, 1, 2, 5, 6)


    def per_mode(source, into):
        for i in range(modes // SUBS):
            for j in range(SUBS):
                par[pl.ds(i * 64 + j * 8, 8), :] = source[
                    pl.ds(i * 8, 8), pl.ds(j * LANES, LANES)
                ]
        for m in range(modes):
            into[m] = par[pl.ds((m // 8) * 64 + m % 8, 8, stride=8), :]

    def tap_rows():
        for a in range(3):
            for j in range(SUBS):
                tapn[pl.ds((a * 8 + j) * 8, 3), :] = taps_ref[a, :, pl.ds(j * LANES, LANES)]

    def tap(a, b):
        return tapn[pl.ds(a * 64 + b, 8, stride=8), :]

    def to_tiles(a, first, last):
        def step(i, carry):
            block = inb[a, pl.ds(pl.multiple_of(i * 16, 16), 16), :].astype(f32)
            for h in range(2):
                for j in range(SUBS):
                    nat[a, pl.ds(pl.multiple_of(i * 128 + h * 64 + j * 8, 8), 8), :] = block[
                        h * 8 : h * 8 + 8, j * LANES : (j + 1) * LANES
                    ]
            return carry

        lax.fori_loop(first, last, step, 0)

    def row(a, i, s):
        return nat[a, pl.ds(i * 64 + s, 8, stride=8), :]

    def put_row(a, i, s, value):
        nat[a, pl.ds(i * 64 + s, 8, stride=8), :] = value

    zero = jnp.zeros((SUBS, LANES), f32)
    blocks = length // 16
    for a in range(2):
        loads[a].wait()
        to_tiles(a, 0, blocks)
    loads[3].wait()
    tap_rows()
    loads[4].wait()
    per_mode(rate_ref, dec)
    dec[...] = jnp.exp(-dec[...])

    def first_pass(i, carry):
        state, k1, k2, v1, v2 = carry
        d = dec[...]
        for s in range(SUBS):
            k0, v0 = row(0, i, s), row(1, i, s)
            kmix = tap(1, 0) * k0 + tap(1, 1) * k1 + tap(1, 2) * k2
            vmix = tap(2, 0) * v0 + tap(2, 1) * v1 + tap(2, 2) * v2
            prod = kmix * vmix
            km[i * 8 + s] = kmix
            vm[i * 8 + s] = vmix
            pr[i * 8 + s] = prod
            state = d * state + prod[None]
            k1, k2, v1, v2 = k0, k1, v0, v1
        return state, k1, k2, v1, v2

    state0 = jnp.zeros((modes, SUBS, LANES), f32)
    final, k1, k2, v1, v2 = lax.fori_loop(0, chunks, first_pass, (state0, zero, zero, zero, zero))
    lane = lax.broadcasted_iota(jnp.int32, (SUBS, LANES), 1)
    bits = ((lane // 32) % 2 == 1, lane // 64 == 1)

    def put_slices(into, value):
        for a in range(modes // 4):
            tiles = swap_blocks([value[4 * a + b] for b in range(4)], bits)
            for q in range(4):
                into[pl.ds(q * 8, 8), a, :] = tiles[q]

    def get_state(slot):
        out = []
        for a in range(modes // 4):
            out += swap_blocks([ar[slot, pl.ds(q * 8, 8), a, :] for q in range(4)], bits)
        return jnp.stack(out)

    kt0, kt1 = tap(1, 1) * k1 + tap(1, 2) * k2, tap(1, 2) * k1
    vt0, vt1 = tap(2, 1) * v1 + tap(2, 2) * v2, tap(2, 2) * v1
    put_slices(fsf, final)
    edges = ([km[0], km[1], kt0, kt1], [vm[0], vm[1], vt0, vt1])
    for a in range(2):
        tiles = swap_blocks(edges[a], bits)
        for q in range(4):
            fsf[pl.ds(q * 8, 8), modes // 4 + a, :] = tiles[q]

    pl.semaphore_wait(barrier, n_seq - 1 + n_tp - 1)

    def exchange(which, source, into, shift=0):
        def send(k, carry):
            other = partner(k)
            pltpu.make_async_remote_copy(
                src_ref=source.at[other],
                dst_ref=into.at[me + shift],
                send_sem=send_sem.at[which],
                recv_sem=recv_sem.at[which],
                device_id={"seq": other},
                device_id_type=MESH,
            ).start()
            return carry

        lax.fori_loop(0, n_seq - 1, send, 0)
        into[me + shift] = source[me]

    def landed(which, into):
        others = into.at[pl.ds(0, n_seq - 1)]
        pltpu.make_async_copy(others, others, recv_sem.at[which]).wait()

    def sent(which, source):
        others = source.at[pl.ds(0, n_seq - 1)]
        pltpu.make_async_copy(others, others, send_sem.at[which]).wait()

    exchange(1, fsf, rxf, 1)

    def halo_copy():
        return pltpu.make_async_remote_copy(
            src_ref=halo_s,
            dst_ref=halo_r,
            send_sem=send_sem.at[0],
            recv_sem=recv_sem.at[0],
            device_id={"seq": me + 1},
            device_id_type=MESH,
        )

    loads[2].wait()
    to_tiles(2, 0, blocks)
    q1, q2 = row(2, chunks - 1, 7), row(2, chunks - 1, 6)
    halo_s[0], halo_s[1], halo_s[2], halo_s[3] = kt0, kt1, vt0, vt1
    halo_s[4] = tap(0, 1) * q1 + tap(0, 2) * q2
    halo_s[5] = tap(0, 2) * q1

    @pl.when(me < n_seq - 1)
    def _():
        halo_copy().start()

    @pl.when(me == 0)
    def _():
        halo_r[...] = jnp.zeros_like(halo_r)

    per_mode(rate_ref, res)
    rate = res[...]
    put_slices(dsl.at[0], jnp.exp(rate * (-float(length))))
    put_slices(dsl.at[1], jnp.exp(rate * (-float(length - 2))))
    put_slices(dsl.at[2], dec[...])
    for a in range(3, 5):
        loads[at_load[a]].wait()
        to_tiles(a, 0, blocks)
    loads[7].wait()
    per_mode(res_ref, res)
    loads[8].wait()
    gain = gain_ref[...]

    def middle_pass(i, carry):
        q1, q2 = carry
        for s in range(SUBS):
            q0 = row(2, i, s)
            qm[i * 8 + s] = tap(0, 0) * q0 + tap(0, 1) * q1 + tap(0, 2) * q2
            st[i * 8 + s] = row(3, i, s)
            sc[i * 8 + s] = gain * row(4, i, s)
            q1, q2 = q0, q1
        return q1, q2

    lax.fori_loop(0, chunks, middle_pass, (zero, zero))

    @pl.when(me > 0)
    def _():
        halo_copy().wait_recv()

    for t in range(2):
        km[t] = km[t] + halo_r[t]
        vm[t] = vm[t] + halo_r[2 + t]
        qm[t] = qm[t] + halo_r[4 + t]
        pr[t] = km[t] * vm[t]

    rxf[0] = jnp.zeros((modes // 4 + 2, LANES), f32)
    landed(1, rxf)
    edge = modes // 4
    kh, vh = rxf[pl.ds(1, n_seq), edge, :], rxf[pl.ds(1, n_seq), edge + 1, :]
    kmix = kh + pltpu.roll(rxf[pl.ds(0, n_seq), edge, :], 64, 1)
    vmix = vh + pltpu.roll(rxf[pl.ds(0, n_seq), edge + 1, :], 64, 1)
    extra = kmix * vmix - kh * vh
    quarter = lax.broadcasted_iota(jnp.int32, (n_seq, LANES), 1) // 32
    for b in range(2):
        part = jnp.where(quarter == b, extra, 0.0)
        part = part + pltpu.roll(part, 64, 1)
        lift[b] = part + pltpu.roll(part, 32, 1)
    step_decay, lift_decay, one_decay = dsl[0, me], dsl[1, me], dsl[2, me]

    def scan_forward(p, state):
        ax[0, p] = state
        added = one_decay * lift[0, pl.ds(p, 1), :] + lift[1, pl.ds(p, 1), :]
        return step_decay * state + (rxf[p + 1, 0 : modes // 4, :] + lift_decay * added)

    lax.fori_loop(0, n_seq, scan_forward, jnp.zeros((4, LANES), f32))
    exchange(2, ax.at[0], ar.at[0])

    def local_pass(i, state):
        d, r = dec[...], res[...]
        block = pr[pl.ds(i * 8, 8)]
        for s in range(SUBS):
            state = d * state + block[s][None]
            cv[i * 8 + s] = jnp.sum(r * state, axis=0)
        return state

    lax.fori_loop(0, chunks, local_pass, state0)

    landed(2, ar.at[0])
    arrived = res[...] * dec[...] * get_state(0)

    def join_pass(i, state):
        d = dec[...]
        for s in range(SUBS):
            t = i * 8 + s
            conv = cv[t] + jnp.sum(state, axis=0)
            state = d * state
            mixed = st[t] + qm[t] * conv
            cv[t] = conv
            mx[t] = mixed
            put_row(0, i, s, mixed * mixed)
            put_row(1, i, s, sc[t] * mixed)
        return state

    lax.fori_loop(0, chunks, join_pass, arrived)

    for a in range(2):
        for i in range(chunks):
            total = nat[a, pl.ds(i * 64, 8), :]
            for j in range(1, SUBS):
                total = total + nat[a, pl.ds(i * 64 + j * 8, 8), :]
            rows[a, pl.ds(i * 8, 8), :] = total
        pss[pl.ds(a, 1), :] = jnp.sum(rows[a].T, axis=0, keepdims=True)

    def share(k, carry):
        other = lax.rem(mt + 1 + k, n_tp)
        pltpu.make_async_remote_copy(
            src_ref=pss,
            dst_ref=psr.at[mt],
            send_sem=send_sem.at[3],
            recv_sem=recv_sem.at[3],
            device_id={"tp": other},
            device_id_type=MESH,
        ).start()
        return carry

    lax.fori_loop(0, n_tp - 1, share, 0)
    psr[mt] = pss[...]
    peers = psr.at[pl.ds(0, n_tp - 1)]
    pltpu.make_async_copy(peers, peers, recv_sem.at[3]).wait()
    totals = jnp.sum(psr[...], axis=0)
    inverse = lax.rsqrt(totals[0:1] / width + epsilon)
    factor = inverse * inverse * inverse * totals[1:2] / width
    rows[0] = jnp.broadcast_to(inverse, (length, LANES)).T
    rows[1] = jnp.broadcast_to(factor, (length, LANES)).T

    def spread(a, t):
        return jnp.broadcast_to(rows[a, pl.ds(t, 1), :], (SUBS, LANES))

    def back_pass(n, state):
        i = chunks - 1 - n
        d = dec[...]
        for s in reversed(range(SUBS)):
            t = i * 8 + s
            dmixed = spread(0, t) * sc[t] - mx[t] * spread(1, t)
            dconv = dmixed * qm[t]
            dm[t] = dmixed
            dc[t] = dconv
            state = d * state + dconv[None]
        return state

    final_back = lax.fori_loop(0, chunks, back_pass, state0)
    put_slices(fsb, final_back)
    exchange(4, fsb, rxb)

    head_s[0] = dm[0] * cv[0]
    head_s[1] = dm[1] * cv[1]
    head_s[2] = dc[0]
    head_s[3], head_s[4] = km[0], km[1]
    head_s[5], head_s[6] = vm[0], vm[1]

    def head_copy():
        return pltpu.make_async_remote_copy(
            src_ref=head_s,
            dst_ref=head_r,
            send_sem=send_sem.at[6],
            recv_sem=recv_sem.at[6],
            device_id={"seq": me - 1},
            device_id_type=MESH,
        )

    @pl.when(me > 0)
    def _():
        head_copy().start()

    @pl.when(me == n_seq - 1)
    def _():
        head_r[...] = jnp.zeros_like(head_r)

    landed(4, rxb)

    def scan_backward(n, state):
        p = n_seq - 1 - n
        ax[1, p] = state
        return step_decay * state + rxb[p]

    lax.fori_loop(0, n_seq, scan_backward, jnp.zeros((4, LANES), f32))
    exchange(5, ax.at[1], ar.at[1])

    def adjoint_pass(n, state):
        i = chunks - 1 - n
        d, r = dec[...], res[...]
        for s in reversed(range(SUBS)):
            state = d * state + dc[i * 8 + s][None]
            dp[i * 8 + s] = jnp.sum(r * state, axis=0)
        return state

    lax.fori_loop(0, chunks, adjoint_pass, state0)

    @pl.when(me < n_seq - 1)
    def _():
        head_copy().wait_recv()

    def query_pass(n, carry):
        g1, g2 = carry
        i = chunks - 1 - n
        for s in reversed(range(SUBS)):
            t = i * 8 + s
            dmixed = dm[t]
            g0 = dmixed * cv[t]
            put_row(0, i, s, mx[t] * spread(0, t) * gain)
            put_row(1, i, s, dmixed)
            put_row(2, i, s, tap(0, 0) * g0 + tap(0, 1) * g1 + tap(0, 2) * g2)
            g1, g2 = g0, g1
        return g1, g2

    lax.fori_loop(0, chunks, query_pass, (head_r[0], head_r[1]))

    def from_tiles(a, target):
        def step(i, carry):
            for j in range(SUBS):
                block = jnp.concatenate(
                    [
                        nat[a, pl.ds(pl.multiple_of(i * 128 + j * 8, 8), 8), :],
                        nat[a, pl.ds(pl.multiple_of(i * 128 + 64 + j * 8, 8), 8), :],
                    ],
                    axis=0,
                )
                target[pl.ds(pl.multiple_of(i * 16, 16), 16), pl.ds(j * LANES, LANES)] = (
                    block.astype(jnp.bfloat16)
                )
            return carry

        lax.fori_loop(0, length // 16, step, 0)

    from_tiles(0, normed_ref)
    from_tiles(1, sgrad_ref)
    from_tiles(2, qgrad_ref)

    landed(5, ar.at[1])
    d, r = dec[...], res[...]
    after = get_state(1)
    arrived_back = r * d * after
    dp0 = jnp.sum(r * after, axis=0)
    dp1 = jnp.sum(r * ((after - head_r[2][None]) / d), axis=0)
    carry0 = (
        arrived_back,
        dp0 * head_r[5],
        dp1 * head_r[6],
        dp0 * head_r[3],
        dp1 * head_r[4],
    )

    def last_pass(n, carry):
        state, a1, a2, b1, b2 = carry
        i = chunks - 1 - n
        d = dec[...]
        for s in reversed(range(SUBS)):
            t = i * 8 + s
            dproduct = dp[t] + jnp.sum(state, axis=0)
            state = d * state
            a0 = dproduct * vm[t]
            b0 = dproduct * km[t]
            put_row(3, i, s, tap(1, 0) * a0 + tap(1, 1) * a1 + tap(1, 2) * a2)
            put_row(4, i, s, tap(2, 0) * b0 + tap(2, 1) * b1 + tap(2, 2) * b2)
            a1, a2, b1, b2 = a0, a1, b0, b1
        return state, a1, a2, b1, b2

    lax.fori_loop(0, chunks, last_pass, carry0)
    from_tiles(3, kgrad_ref)
    from_tiles(4, vgrad_ref)

    @pl.when(me < n_seq - 1)
    def _():
        halo_copy().wait_send()

    @pl.when(me > 0)
    def _():
        head_copy().wait_send()

    sent(1, fsf)
    sent(2, ax.at[0])
    sent(4, fsb)
    sent(5, ax.at[1])
    pltpu.make_async_copy(peers, peers, send_sem.at[3]).wait()


def write_out(*refs):
    sem = refs[-1]
    half = (len(refs) - 1) // 2
    copies = [
        pltpu.make_async_copy(refs[a], refs[half + a], sem.at[a]) for a in range(half)
    ]
    for copy in copies:
        copy.start()
    for copy in copies:
        copy.wait()


def solution(mesh):
    n_seq, n_tp = mesh.shape["seq"], mesh.shape["tp"]

    def body(q, k, v, stream, taps, rate, residue, gain, cotangent):
        length, channels = q.shape
        modes = rate.shape[0]
        assert channels == SUBS * LANES and modes * 2 == n_seq and length == LANES
        hbm = pl.BlockSpec(memory_space=pl.ANY)
        vmem = pl.BlockSpec(memory_space=pltpu.VMEM)
        out = jax.ShapeDtypeStruct((length, channels), jnp.bfloat16)
        tiles = pltpu.VMEM((length, SUBS, LANES), f32)
        per_mode = pltpu.VMEM((modes, SUBS, LANES), f32)
        slices = (n_seq, modes // 4, LANES)
        edged = modes // 4 + 2
        operands = (q, k, v, stream, cotangent, taps, rate, residue, gain.reshape(SUBS, LANES))
        results = pl.pallas_call(
            functools.partial(kernel, n_seq, n_tp),
            out_shape=(out,) * 5,
            in_specs=[hbm] * 9,
            out_specs=(vmem,) * 5,
            scratch_shapes=[
                pltpu.VMEM((5, length, channels), jnp.bfloat16),
                pltpu.VMEM(taps.shape, f32),
                pltpu.VMEM(rate.shape, f32),
                pltpu.VMEM(rate.shape, f32),
                pltpu.VMEM((SUBS, LANES), f32),
                pltpu.VMEM((5, length * SUBS, LANES), f32),
                pltpu.VMEM((modes * SUBS, LANES), f32),
                pltpu.VMEM((3 * 64, LANES), f32),
                per_mode,
                per_mode,
            ]
            + [tiles] * 11
            + [
                pltpu.VMEM((2, length, LANES), f32),
                pltpu.VMEM((6, SUBS, LANES), f32),
                pltpu.VMEM((6, SUBS, LANES), f32),
                pltpu.VMEM((7, SUBS, LANES), f32),
                pltpu.VMEM((7, SUBS, LANES), f32),
                pltpu.VMEM((n_seq, edged, LANES), f32),
                pltpu.VMEM(slices, f32),
                pltpu.VMEM((n_seq + 1, edged, LANES), f32),
                pltpu.VMEM(slices, f32),
                pltpu.VMEM((3,) + slices, f32),
                pltpu.VMEM((2, n_seq, LANES), f32),
                pltpu.VMEM((2,) + slices, f32),
                pltpu.VMEM((2,) + slices, f32),
                pltpu.VMEM((2, LANES), f32),
                pltpu.VMEM((n_tp, 2, LANES), f32),
                pltpu.SemaphoreType.DMA((9,)),
                pltpu.SemaphoreType.DMA((7,)),
                pltpu.SemaphoreType.DMA((7,)),
            ],
            compiler_params=pltpu.CompilerParams(
                collective_id=0, has_side_effects=True, vmem_limit_bytes=40 * 1024 * 1024
            ),
        )(*[pltpu.with_memory_space_constraint(x, pltpu.HBM) for x in operands])
        return pl.pallas_call(
            write_out,
            out_shape=(out,) * 5,
            in_specs=[hbm] * 5,
            out_specs=(pl.BlockSpec(memory_space=pltpu.HBM),) * 5,
            scratch_shapes=[pltpu.SemaphoreType.DMA((5,))],
            compiler_params=pltpu.CompilerParams(vmem_limit_bytes=1024 * 1024),
        )(*results)

    seq_tp = P("seq", "tp")
    return jax.shard_map(
        body,
        mesh=mesh,
        in_specs=(
            seq_tp,
            seq_tp,
            seq_tp,
            seq_tp,
            P(None, None, "tp"),
            P(None, "tp"),
            P(None, "tp"),
            P("tp"),
            seq_tp,
        ),
        out_specs=(seq_tp,) * 5,
        check_vma=False,
    )
```

```python
import functools

import jax
import jax.numpy as jnp
from jax import lax
from jax.experimental import pallas as pl
from jax.experimental.pallas import tpu as pltpu
from jax.sharding import PartitionSpec as P

MESH = pl.DeviceIdType.MESH
f32 = jnp.float32
epsilon = 1e-05
LANES = 128
SUBS = 8


def swap_halves(first, second, upper):
    return (
        jnp.where(upper, pltpu.roll(second, 64, 1), first),
        jnp.where(upper, second, pltpu.roll(first, 64, 1)),
    )


def kernel(
    n_seq,
    n_tp,
    q_hbm,
    k_hbm,
    v_hbm,
    s_hbm,
    c_hbm,
    taps_hbm,
    rate_hbm,
    res_hbm,
    gain_hbm,
    normed_ref,
    sgrad_ref,
    qgrad_ref,
    kgrad_ref,
    vgrad_ref,
    inb,
    taps_ref,
    rate_ref,
    res_ref,
    gain_ref,
    nat,
    par,
    tapn,
    dec,
    res,
    km,
    vm,
    qm,
    pr,
    cv,
    st,
    sc,
    mx,
    dm,
    dc,
    dp,
    rows,
    halo_s,
    halo_r,
    head_s,
    head_r,
    fsf,
    fsb,
    rxf,
    rxb,
    dsl,
    lift,
    powers,
    ax,
    ar,
    total,
    across,
    bump,
    growth,
    pss,
    psr,
    in_sem,
    send_sem,
    recv_sem,
    ready,
):
    me = lax.axis_index("seq")
    mt = lax.axis_index("tp")
    n_half = n_seq // 2
    half, place = me // n_half, lax.rem(me, n_half)
    base = half * n_half
    length = km.shape[0]
    modes = rate_ref.shape[0]
    chunks = length // SUBS
    width = float(n_tp * SUBS * LANES)

    barrier = pltpu.get_barrier_semaphore()

    def partner(k):
        sign = 1 - 2 * lax.rem(k, 2)
        return lax.rem(place + n_half // 2 + sign * ((k + 1) // 2), n_half)

    def greet(device):
        pl.semaphore_signal(barrier, inc=1, device_id={"seq": device}, device_id_type=MESH)

    def greet_half(k, carry):
        greet(base + partner(k))
        return carry

    def greet_later(k, carry):
        greet(n_half + k)
        return carry

    def greet_tp(k, carry):
        other = lax.rem(mt + 1 + k, n_tp)
        pl.semaphore_signal(barrier, inc=1, device_id={"tp": other}, device_id_type=MESH)
        return carry

    @pl.when(me == n_half)
    def _():
        greet(me - 1)

    lax.fori_loop(0, n_half - 1, greet_half, 0)
    lax.fori_loop(0, n_tp - 1, greet_tp, 0)

    @pl.when(half == 0)
    def _():
        lax.fori_loop(0, n_half, greet_later, 0)


    loads = []
    for a, (src, into) in enumerate(
        (
            (k_hbm, inb.at[0]),
            (v_hbm, inb.at[1]),
            (q_hbm, inb.at[2]),
            (taps_hbm, taps_ref),
            (rate_hbm, rate_ref),
            (s_hbm, inb.at[3]),
            (c_hbm, inb.at[4]),
            (res_hbm, res_ref),
            (gain_hbm, gain_ref),
        )
    ):
        copy = pltpu.make_async_copy(src, into, in_sem.at[a])
        copy.start()
        loads.append(copy)
    at_load = (0, 1, 2, 5, 6)


    def per_mode(source, into):
        for i in range(modes // SUBS):
            for j in range(SUBS):
                par[pl.ds(i * 64 + j * 8, 8), :] = source[
                    pl.ds(i * 8, 8), pl.ds(j * LANES, LANES)
                ]
        for m in range(modes):
            into[m] = par[pl.ds((m // 8) * 64 + m % 8, 8, stride=8), :]

    def tap_rows():
        for a in range(3):
            for j in range(SUBS):
                tapn[pl.ds((a * 8 + j) * 8, 3), :] = taps_ref[a, :, pl.ds(j * LANES, LANES)]

    def tap(a, b):
        return tapn[pl.ds(a * 64 + b, 8, stride=8), :]

    def to_tiles(a, first, last):
        def step(i, carry):
            block = inb[a, pl.ds(pl.multiple_of(i * 16, 16), 16), :].astype(f32)
            for h in range(2):
                for j in range(SUBS):
                    nat[a, pl.ds(pl.multiple_of(i * 128 + h * 64 + j * 8, 8), 8), :] = block[
                        h * 8 : h * 8 + 8, j * LANES : (j + 1) * LANES
                    ]
            return carry

        lax.fori_loop(first, last, step, 0)

    def row(a, i, s):
        return nat[a, pl.ds(i * 64 + s, 8, stride=8), :]

    def put_row(a, i, s, value):
        nat[a, pl.ds(i * 64 + s, 8, stride=8), :] = value

    zero = jnp.zeros((SUBS, LANES), f32)
    blocks = length // 16
    for a in range(2):
        loads[a].wait()
        to_tiles(a, 0, blocks)
    loads[3].wait()
    tap_rows()
    loads[4].wait()
    per_mode(rate_ref, dec)
    dec[...] = jnp.exp(-dec[...])

    def first_pass(i, carry):
        state, k1, k2, v1, v2 = carry
        d = dec[...]
        for s in range(SUBS):
            k0, v0 = row(0, i, s), row(1, i, s)
            kmix = tap(1, 0) * k0 + tap(1, 1) * k1 + tap(1, 2) * k2
            vmix = tap(2, 0) * v0 + tap(2, 1) * v1 + tap(2, 2) * v2
            prod = kmix * vmix
            km[i * 8 + s] = kmix
            vm[i * 8 + s] = vmix
            pr[i * 8 + s] = prod
            state = d * state + prod[None]
            k1, k2, v1, v2 = k0, k1, v0, v1
        return state, k1, k2, v1, v2

    state0 = jnp.zeros((modes, SUBS, LANES), f32)
    final, k1, k2, v1, v2 = lax.fori_loop(0, chunks, first_pass, (state0, zero, zero, zero, zero))
    upper = lax.broadcasted_iota(jnp.int32, (SUBS, LANES), 1) >= 64
    groups = modes // 2

    def put_slices(into, values, row0=0):
        for a in range(len(values) // 2):
            tiles = swap_halves(values[2 * a], values[2 * a + 1], upper)
            for q in range(2):
                into[pl.ds(q * 8, 8), row0 + a, :] = tiles[q]

    def get_state(source):
        out = []
        for a in range(groups):
            out += swap_halves(source[pl.ds(0, 8), a, :], source[pl.ds(8, 8), a, :], upper)
        return jnp.stack(out)

    def each(value):
        return [value[m] for m in range(modes)]

    kt0, kt1 = tap(1, 1) * k1 + tap(1, 2) * k2, tap(1, 2) * k1
    vt0, vt1 = tap(2, 1) * v1 + tap(2, 2) * v2, tap(2, 2) * v1
    halo_s[0], halo_s[1], halo_s[2], halo_s[3] = kt0, kt1, vt0, vt1

    put_slices(fsf, each(final))
    edges = (km[0], km[1], kt0, kt1, vm[0], vm[1], vt0, vt1)
    put_slices(fsf, edges, groups)
    loads[2].wait()
    to_tiles(2, 0, blocks)
    q1, q2 = row(2, chunks - 1, 7), row(2, chunks - 1, 6)
    halo_s[4] = tap(0, 1) * q1 + tap(0, 2) * q2
    halo_s[5] = tap(0, 2) * q1
    per_mode(rate_ref, res)

    first_of_later = (1 - half) * ((me + 1) // n_half)
    pl.semaphore_wait(barrier, n_half - 1 + n_tp - 1 + half * n_half + first_of_later)

    def halo_copy():
        return pltpu.make_async_remote_copy(
            src_ref=halo_s,
            dst_ref=halo_r,
            send_sem=send_sem.at[0],
            recv_sem=recv_sem.at[0],
            device_id={"seq": me + 1},
            device_id_type=MESH,
        )

    @pl.when(me < n_seq - 1)
    def _():
        halo_copy().start()

    @pl.when(me == 0)
    def _():
        halo_r[...] = jnp.zeros_like(halo_r)

    def first_rows():
        for t in range(2):
            km[t] = km[t] + halo_r[t]
            vm[t] = vm[t] + halo_r[2 + t]
            pr[t] = km[t] * vm[t]

    def exchange(which, source, into, shift=0):
        def send(k, carry):
            other = partner(k)
            pltpu.make_async_remote_copy(
                src_ref=source.at[other],
                dst_ref=into.at[place + shift],
                send_sem=send_sem.at[which],
                recv_sem=recv_sem.at[which],
                device_id={"seq": base + other},
                device_id_type=MESH,
            ).start()
            return carry

        lax.fori_loop(0, n_half - 1, send, 0)
        into[place + shift] = source[place]

    def landed(which, into):
        others = into.at[pl.ds(0, n_half - 1)]
        pltpu.make_async_copy(others, others, recv_sem.at[which]).wait()

    def sent(which, source):
        others = source.at[pl.ds(0, n_half - 1)]
        pltpu.make_async_copy(others, others, send_sem.at[which]).wait()

    def send_across(which, slot, target):
        def send(k, carry):
            pltpu.make_async_remote_copy(
                src_ref=total.at[slot],
                dst_ref=across.at[slot, place],
                send_sem=send_sem.at[which],
                recv_sem=recv_sem.at[which],
                device_id={"seq": target + lax.rem(place + n_half // 2 + k, n_half)},
                device_id_type=MESH,
            ).start()
            return carry

        lax.fori_loop(0, n_half, send, 0)

    def wait_across(sem, slot):
        pltpu.make_async_copy(across.at[slot], across.at[slot], sem).wait()

    exchange(1, fsf, rxf, 1)

    def tell(k, carry):
        pl.semaphore_signal(ready, inc=1, device_id={"seq": k}, device_id_type=MESH)
        return carry

    @pl.when(half == 1)
    def _():
        lax.fori_loop(0, n_half, tell, 0)
        across[1] = jnp.zeros(across.shape[1:], f32)

    @pl.when(half == 0)
    def _():
        across[0] = jnp.zeros(across.shape[1:], f32)

    rate = res[...]
    put_slices(dsl.at[0], each(jnp.exp(rate * (-float(length)))))
    put_slices(dsl.at[1], each(jnp.exp(rate * (-float(length - 2)))))
    put_slices(dsl.at[2], [dec[m] for m in range(modes)])
    before = (place * length).astype(f32)
    after = ((n_half - 1 - place) * length).astype(f32)
    powers[0] = jnp.exp(rate * -before)
    powers[1] = jnp.exp(rate * -after)
    growth[0] = jnp.exp(rate)
    growth[1] = jnp.exp(rate * 2.0)
    for a in range(3, 5):
        loads[at_load[a]].wait()
        to_tiles(a, 0, blocks)
    loads[7].wait()
    per_mode(res_ref, res)
    loads[8].wait()
    gain = gain_ref[...]

    def middle_pass(i, carry):
        q1, q2 = carry
        for s in range(SUBS):
            q0 = row(2, i, s)
            qm[i * 8 + s] = tap(0, 0) * q0 + tap(0, 1) * q1 + tap(0, 2) * q2
            st[i * 8 + s] = row(3, i, s)
            sc[i * 8 + s] = gain * row(4, i, s)
            q1, q2 = q0, q1
        return q1, q2

    lax.fori_loop(0, chunks, middle_pass, (zero, zero))

    @pl.when(me > 0)
    def _():
        halo_copy().wait_recv()

    old0, old1 = pr[0], pr[1]
    first_rows()
    bump[0, 0], bump[0, 1] = pr[0] - old0, pr[1] - old1

    def bump_copy(other):
        return pltpu.make_async_remote_copy(
            src_ref=bump.at[0],
            dst_ref=bump.at[1],
            send_sem=send_sem.at[9],
            recv_sem=recv_sem.at[9],
            device_id={"seq": other},
            device_id_type=MESH,
        )

    def tell_bump(k, carry):
        bump_copy(n_half + 1 + k).start()
        return carry

    @pl.when(me == n_half)
    def _():
        lax.fori_loop(0, n_half - 1, tell_bump, 0)

    @pl.when(me <= n_half)
    def _():
        bump[1] = jnp.zeros(bump.shape[1:], f32)

    qm[0] = qm[0] + halo_r[4]
    qm[1] = qm[1] + halo_r[5]

    rxf[0] = jnp.zeros(rxf.shape[1:], f32)
    landed(1, rxf)
    kh, vh = rxf[pl.ds(1, n_half), groups, :], rxf[pl.ds(1, n_half), groups + 2, :]
    kmix = kh + rxf[pl.ds(0, n_half), groups + 1, :]
    vmix = vh + rxf[pl.ds(0, n_half), groups + 3, :]
    extra = kmix * vmix - kh * vh
    turned = pltpu.roll(extra, 64, 1)
    high = lax.broadcasted_iota(jnp.int32, (n_half, LANES), 1) >= 64
    lift[0] = jnp.where(high, turned, extra)
    lift[1] = jnp.where(high, extra, turned)
    step_decay, lift_decay, one_decay = dsl[0, place], dsl[1, place], dsl[2, place]

    def scan_forward(p, state):
        ax[0, p] = state
        added = one_decay * lift[0, pl.ds(p, 1), :] + lift[1, pl.ds(p, 1), :]
        return step_decay * state + (rxf[p + 1, 0:groups, :] + lift_decay * added)

    total[0] = lax.fori_loop(0, n_half, scan_forward, jnp.zeros((groups, LANES), f32))
    exchange(2, ax.at[0], ar.at[0])

    @pl.when(half == 0)
    def _():
        pl.semaphore_wait(ready, n_half)
        send_across(7, 0, n_half)

    def local_pass(i, state):
        d, r = dec[...], res[...]
        block = pr[pl.ds(i * 8, 8)]
        for s in range(SUBS):
            state = d * state + block[s][None]
            cv[i * 8 + s] = jnp.sum(r * state, axis=0)
        return state

    lax.fori_loop(0, chunks, local_pass, state0)

    landed(2, ar.at[0])

    @pl.when(half == 1)
    def _():
        wait_across(recv_sem.at[7], 0)

    @pl.when(me > n_half)
    def _():
        bump_copy(me).wait_recv()

    crossed = get_state(across.at[0]) + growth[0] * bump[1, 0] + growth[1] * bump[1, 1]
    arrived = res[...] * dec[...] * (get_state(ar.at[0]) + powers[0] * crossed)

    def join_pass(i, state):
        d = dec[...]
        for s in range(SUBS):
            t = i * 8 + s
            conv = cv[t] + jnp.sum(state, axis=0)
            state = d * state
            mixed = st[t] + qm[t] * conv
            cv[t] = conv
            mx[t] = mixed
            put_row(0, i, s, mixed * mixed)
            put_row(1, i, s, sc[t] * mixed)
        return state

    lax.fori_loop(0, chunks, join_pass, arrived)

    for a in range(2):
        for i in range(chunks):
            partial = nat[a, pl.ds(i * 64, 8), :]
            for j in range(1, SUBS):
                partial = partial + nat[a, pl.ds(i * 64 + j * 8, 8), :]
            rows[a, pl.ds(i * 8, 8), :] = partial
        pss[pl.ds(a, 1), :] = jnp.sum(rows[a].T, axis=0, keepdims=True)

    def share(k, carry):
        other = lax.rem(mt + 1 + k, n_tp)
        pltpu.make_async_remote_copy(
            src_ref=pss,
            dst_ref=psr.at[mt],
            send_sem=send_sem.at[3],
            recv_sem=recv_sem.at[3],
            device_id={"tp": other},
            device_id_type=MESH,
        ).start()
        return carry

    lax.fori_loop(0, n_tp - 1, share, 0)
    psr[mt] = pss[...]
    peers = psr.at[pl.ds(0, n_tp - 1)]
    pltpu.make_async_copy(peers, peers, recv_sem.at[3]).wait()
    totals = jnp.sum(psr[...], axis=0)
    inverse = lax.rsqrt(totals[0:1] / width + epsilon)
    factor = inverse * inverse * inverse * totals[1:2] / width
    rows[0] = jnp.broadcast_to(inverse, (length, LANES)).T
    rows[1] = jnp.broadcast_to(factor, (length, LANES)).T

    def spread(a, t):
        return jnp.broadcast_to(rows[a, pl.ds(t, 1), :], (SUBS, LANES))

    def back_pass(n, state):
        i = chunks - 1 - n
        d = dec[...]
        for s in reversed(range(SUBS)):
            t = i * 8 + s
            dmixed = spread(0, t) * sc[t] - mx[t] * spread(1, t)
            dconv = dmixed * qm[t]
            dm[t] = dmixed
            dc[t] = dconv
            state = d * state + dconv[None]
        return state

    final_back = lax.fori_loop(0, chunks, back_pass, state0)
    put_slices(fsb, each(final_back))
    exchange(4, fsb, rxb)

    head_s[0] = dm[0] * cv[0]
    head_s[1] = dm[1] * cv[1]
    head_s[2] = dc[0]
    head_s[3], head_s[4] = km[0], km[1]
    head_s[5], head_s[6] = vm[0], vm[1]

    def head_copy():
        return pltpu.make_async_remote_copy(
            src_ref=head_s,
            dst_ref=head_r,
            send_sem=send_sem.at[6],
            recv_sem=recv_sem.at[6],
            device_id={"seq": me - 1},
            device_id_type=MESH,
        )

    @pl.when(me > 0)
    def _():
        head_copy().start()

    @pl.when(me == n_seq - 1)
    def _():
        head_r[...] = jnp.zeros_like(head_r)

    landed(4, rxb)

    def scan_backward(n, state):
        p = n_half - 1 - n
        ax[1, p] = state
        return step_decay * state + rxb[p]

    total[1] = lax.fori_loop(0, n_half, scan_backward, jnp.zeros((groups, LANES), f32))

    @pl.when(half == 1)
    def _():
        send_across(8, 1, 0)

    exchange(5, ax.at[1], ar.at[1])

    def adjoint_pass(n, state):
        i = chunks - 1 - n
        d, r = dec[...], res[...]
        for s in reversed(range(SUBS)):
            state = d * state + dc[i * 8 + s][None]
            dp[i * 8 + s] = jnp.sum(r * state, axis=0)
        return state

    lax.fori_loop(0, chunks, adjoint_pass, state0)

    @pl.when(me < n_seq - 1)
    def _():
        head_copy().wait_recv()

    def query_pass(n, carry):
        g1, g2 = carry
        i = chunks - 1 - n
        for s in reversed(range(SUBS)):
            t = i * 8 + s
            dmixed = dm[t]
            g0 = dmixed * cv[t]
            put_row(0, i, s, mx[t] * spread(0, t) * gain)
            put_row(1, i, s, dmixed)
            put_row(2, i, s, tap(0, 0) * g0 + tap(0, 1) * g1 + tap(0, 2) * g2)
            g1, g2 = g0, g1
        return g1, g2

    lax.fori_loop(0, chunks, query_pass, (head_r[0], head_r[1]))

    def from_tiles(a, target):
        def step(i, carry):
            for j in range(SUBS):
                block = jnp.concatenate(
                    [
                        nat[a, pl.ds(pl.multiple_of(i * 128 + j * 8, 8), 8), :],
                        nat[a, pl.ds(pl.multiple_of(i * 128 + 64 + j * 8, 8), 8), :],
                    ],
                    axis=0,
                )
                target[pl.ds(pl.multiple_of(i * 16, 16), 16), pl.ds(j * LANES, LANES)] = (
                    block.astype(jnp.bfloat16)
                )
            return carry

        lax.fori_loop(0, length // 16, step, 0)

    from_tiles(0, normed_ref)
    from_tiles(1, sgrad_ref)
    from_tiles(2, qgrad_ref)

    landed(5, ar.at[1])

    @pl.when(half == 0)
    def _():
        wait_across(recv_sem.at[8], 1)

    d, r = dec[...], res[...]
    after = get_state(ar.at[1]) + powers[1] * get_state(across.at[1])
    arrived_back = r * d * after
    dp0 = jnp.sum(r * after, axis=0)
    dp1 = jnp.sum(r * ((after - head_r[2][None]) / d), axis=0)
    carry0 = (
        arrived_back,
        dp0 * head_r[5],
        dp1 * head_r[6],
        dp0 * head_r[3],
        dp1 * head_r[4],
    )

    def last_pass(n, carry):
        state, a1, a2, b1, b2 = carry
        i = chunks - 1 - n
        d = dec[...]
        for s in reversed(range(SUBS)):
            t = i * 8 + s
            dproduct = dp[t] + jnp.sum(state, axis=0)
            state = d * state
            a0 = dproduct * vm[t]
            b0 = dproduct * km[t]
            put_row(3, i, s, tap(1, 0) * a0 + tap(1, 1) * a1 + tap(1, 2) * a2)
            put_row(4, i, s, tap(2, 0) * b0 + tap(2, 1) * b1 + tap(2, 2) * b2)
            a1, a2, b1, b2 = a0, a1, b0, b1
        return state, a1, a2, b1, b2

    lax.fori_loop(0, chunks, last_pass, carry0)
    from_tiles(3, kgrad_ref)
    from_tiles(4, vgrad_ref)

    @pl.when(me < n_seq - 1)
    def _():
        halo_copy().wait_send()

    @pl.when(me > 0)
    def _():
        head_copy().wait_send()

    @pl.when(me == n_half)
    def _():
        as_many = km.at[pl.ds(0, 2 * (n_half - 1))]
        pltpu.make_async_copy(as_many, as_many, send_sem.at[9]).wait()

    @pl.when(half == 0)
    def _():
        wait_across(send_sem.at[7], 0)

    @pl.when(half == 1)
    def _():
        wait_across(send_sem.at[8], 1)

    sent(1, fsf)
    sent(2, ax.at[0])
    sent(4, fsb)
    sent(5, ax.at[1])
    pltpu.make_async_copy(peers, peers, send_sem.at[3]).wait()


def write_out(*refs):
    sem = refs[-1]
    half = (len(refs) - 1) // 2
    copies = [
        pltpu.make_async_copy(refs[a], refs[half + a], sem.at[a]) for a in range(half)
    ]
    for copy in copies:
        copy.start()
    for copy in copies:
        copy.wait()


def solution(mesh):
    n_seq, n_tp = mesh.shape["seq"], mesh.shape["tp"]

    def body(q, k, v, stream, taps, rate, residue, gain, cotangent):
        length, channels = q.shape
        modes = rate.shape[0]
        assert channels == SUBS * LANES and n_seq == 32 and modes == 16 and length == LANES
        hbm = pl.BlockSpec(memory_space=pl.ANY)
        vmem = pl.BlockSpec(memory_space=pltpu.VMEM)
        out = jax.ShapeDtypeStruct((length, channels), jnp.bfloat16)
        tiles = pltpu.VMEM((length, SUBS, LANES), f32)
        per_mode = pltpu.VMEM((modes, SUBS, LANES), f32)
        n_half, groups = n_seq // 2, modes // 2
        slices = (n_half, groups, LANES)
        operands = (q, k, v, stream, cotangent, taps, rate, residue, gain.reshape(SUBS, LANES))
        results = pl.pallas_call(
            functools.partial(kernel, n_seq, n_tp),
            out_shape=(out,) * 5,
            in_specs=[hbm] * 9,
            out_specs=(vmem,) * 5,
            scratch_shapes=[
                pltpu.VMEM((5, length, channels), jnp.bfloat16),
                pltpu.VMEM(taps.shape, f32),
                pltpu.VMEM(rate.shape, f32),
                pltpu.VMEM(rate.shape, f32),
                pltpu.VMEM((SUBS, LANES), f32),
                pltpu.VMEM((5, length * SUBS, LANES), f32),
                pltpu.VMEM((modes * SUBS, LANES), f32),
                pltpu.VMEM((3 * 64, LANES), f32),
                per_mode,
                per_mode,
            ]
            + [tiles] * 11
            + [
                pltpu.VMEM((2, length, LANES), f32),
                pltpu.VMEM((6, SUBS, LANES), f32),
                pltpu.VMEM((6, SUBS, LANES), f32),
                pltpu.VMEM((7, SUBS, LANES), f32),
                pltpu.VMEM((7, SUBS, LANES), f32),
                pltpu.VMEM((n_half, groups + 4, LANES), f32),
                pltpu.VMEM(slices, f32),
                pltpu.VMEM((n_half + 1, groups + 4, LANES), f32),
                pltpu.VMEM(slices, f32),
                pltpu.VMEM((3,) + slices, f32),
                pltpu.VMEM((2, n_half, LANES), f32),
                pltpu.VMEM((2, modes, SUBS, LANES), f32),
                pltpu.VMEM((2,) + slices, f32),
                pltpu.VMEM((2,) + slices, f32),
                pltpu.VMEM((2, groups, LANES), f32),
                pltpu.VMEM((2,) + slices, f32),
                pltpu.VMEM((2, 2, SUBS, LANES), f32),
                pltpu.VMEM((2, modes, SUBS, LANES), f32),
                pltpu.VMEM((2, LANES), f32),
                pltpu.VMEM((n_tp, 2, LANES), f32),
                pltpu.SemaphoreType.DMA((9,)),
                pltpu.SemaphoreType.DMA((10,)),
                pltpu.SemaphoreType.DMA((10,)),
                pltpu.SemaphoreType.REGULAR,
            ],
            compiler_params=pltpu.CompilerParams(
                collective_id=0, has_side_effects=True, vmem_limit_bytes=40 * 1024 * 1024
            ),
        )(*[pltpu.with_memory_space_constraint(x, pltpu.HBM) for x in operands])
        return pl.pallas_call(
            write_out,
            out_shape=(out,) * 5,
            in_specs=[hbm] * 5,
            out_specs=(pl.BlockSpec(memory_space=pltpu.HBM),) * 5,
            scratch_shapes=[pltpu.SemaphoreType.DMA((5,))],
            compiler_params=pltpu.CompilerParams(vmem_limit_bytes=1024 * 1024),
        )(*results)

    seq_tp = P("seq", "tp")
    return jax.shard_map(
        body,
        mesh=mesh,
        in_specs=(
            seq_tp,
            seq_tp,
            seq_tp,
            seq_tp,
            P(None, None, "tp"),
            P(None, "tp"),
            P(None, "tp"),
            P("tp"),
            seq_tp,
        ),
        out_specs=(seq_tp,) * 5,
        check_vma=False,
    )
```

```python
import functools

import jax
import jax.numpy as jnp
from jax import lax
from jax.experimental import pallas as pl
from jax.experimental.pallas import tpu as pltpu
from jax.sharding import PartitionSpec as P

MESH = pl.DeviceIdType.MESH
f32 = jnp.float32
epsilon = 1e-05
LANES = 128
SUBS = 8


def swap_halves(first, second, upper):
    return (
        jnp.where(upper, pltpu.roll(second, 64, 1), first),
        jnp.where(upper, second, pltpu.roll(first, 64, 1)),
    )


def kernel(
    n_seq,
    n_tp,
    q_hbm,
    k_hbm,
    v_hbm,
    s_hbm,
    c_hbm,
    taps_hbm,
    rate_hbm,
    res_hbm,
    gain_hbm,
    normed_ref,
    sgrad_ref,
    qgrad_ref,
    kgrad_ref,
    vgrad_ref,
    inb,
    taps_ref,
    rate_ref,
    res_ref,
    gain_ref,
    nat,
    par,
    tapn,
    dec,
    res,
    km,
    vm,
    qm,
    pr,
    cv,
    st,
    sc,
    mx,
    dm,
    dc,
    dp,
    rows,
    halo_s,
    halo_r,
    head_s,
    head_r,
    fsf,
    fsb,
    rxf,
    rxb,
    dsl,
    lift,
    powers,
    ax,
    ar,
    total,
    across,
    bump,
    growth,
    pss,
    psr,
    in_sem,
    send_sem,
    recv_sem,
    ready,
):
    me = lax.axis_index("seq")
    mt = lax.axis_index("tp")
    n_half = n_seq // 2
    half, place = me // n_half, lax.rem(me, n_half)
    base = half * n_half
    length = km.shape[0]
    modes = rate_ref.shape[0]
    chunks = length // SUBS
    width = float(n_tp * SUBS * LANES)

    barrier = pltpu.get_barrier_semaphore()

    def partner(k):
        sign = 1 - 2 * lax.rem(k, 2)
        return lax.rem(place + n_half // 2 + sign * ((k + 1) // 2), n_half)

    def greet(device):
        pl.semaphore_signal(barrier, inc=1, device_id={"seq": device}, device_id_type=MESH)

    def greet_half(k, carry):
        greet(base + partner(k))
        return carry

    def greet_later(k, carry):
        greet(n_half + k)
        return carry

    def greet_tp(k, carry):
        other = lax.rem(mt + 1 + k, n_tp)
        pl.semaphore_signal(barrier, inc=1, device_id={"tp": other}, device_id_type=MESH)
        return carry

    @pl.when(me == n_half)
    def _():
        greet(me - 1)

    lax.fori_loop(0, n_half - 1, greet_half, 0)
    lax.fori_loop(0, n_tp - 1, greet_tp, 0)

    @pl.when(half == 0)
    def _():
        lax.fori_loop(0, n_half, greet_later, 0)


    loads = []
    for a, (src, into) in enumerate(
        (
            (k_hbm, inb.at[0]),
            (v_hbm, inb.at[1]),
            (q_hbm, inb.at[2]),
            (taps_hbm, taps_ref),
            (rate_hbm, rate_ref),
            (s_hbm, inb.at[3]),
            (c_hbm, inb.at[4]),
            (res_hbm, res_ref),
            (gain_hbm, gain_ref),
        )
    ):
        copy = pltpu.make_async_copy(src, into, in_sem.at[a])
        copy.start()
        loads.append(copy)
    at_load = (0, 1, 2, 5, 6)


    def per_mode(source, into):
        for i in range(modes // SUBS):
            for j in range(SUBS):
                par[pl.ds(i * 64 + j * 8, 8), :] = source[
                    pl.ds(i * 8, 8), pl.ds(j * LANES, LANES)
                ]
        for m in range(modes):
            into[m] = par[pl.ds((m // 8) * 64 + m % 8, 8, stride=8), :]

    def tap_rows():
        for a in range(3):
            for j in range(SUBS):
                tapn[pl.ds((a * 8 + j) * 8, 3), :] = taps_ref[a, :, pl.ds(j * LANES, LANES)]

    def tap(a, b):
        return tapn[pl.ds(a * 64 + b, 8, stride=8), :]

    def to_tiles(a, first, last):
        def step(i, carry):
            block = inb[a, pl.ds(pl.multiple_of(i * 16, 16), 16), :].astype(f32)
            for h in range(2):
                for j in range(SUBS):
                    nat[a, pl.ds(pl.multiple_of(i * 128 + h * 64 + j * 8, 8), 8), :] = block[
                        h * 8 : h * 8 + 8, j * LANES : (j + 1) * LANES
                    ]
            return carry

        lax.fori_loop(first, last, step, 0)

    def row(a, i, s):
        return nat[a, pl.ds(i * 64 + s, 8, stride=8), :]

    def put_row(a, i, s, value):
        nat[a, pl.ds(i * 64 + s, 8, stride=8), :] = value

    zero = jnp.zeros((SUBS, LANES), f32)
    blocks = length // 16
    for a in range(2):
        loads[a].wait()
        to_tiles(a, 0, blocks)
    loads[3].wait()
    tap_rows()
    loads[4].wait()
    per_mode(rate_ref, dec)
    dec[...] = jnp.exp(-dec[...])

    def first_pass(i, carry):
        state, k1, k2, v1, v2 = carry
        d = dec[...]
        for s in range(SUBS):
            k0, v0 = row(0, i, s), row(1, i, s)
            kmix = tap(1, 0) * k0 + tap(1, 1) * k1 + tap(1, 2) * k2
            vmix = tap(2, 0) * v0 + tap(2, 1) * v1 + tap(2, 2) * v2
            prod = kmix * vmix
            km[i * 8 + s] = kmix
            vm[i * 8 + s] = vmix
            pr[i * 8 + s] = prod
            state = d * state + prod[None]
            k1, k2, v1, v2 = k0, k1, v0, v1
        return state, k1, k2, v1, v2

    state0 = jnp.zeros((modes, SUBS, LANES), f32)
    final, k1, k2, v1, v2 = lax.fori_loop(0, chunks, first_pass, (state0, zero, zero, zero, zero))
    upper = lax.broadcasted_iota(jnp.int32, (SUBS, LANES), 1) >= 64
    groups = modes // 2

    def put_slices(into, values, row0=0):
        for a in range(len(values) // 2):
            tiles = swap_halves(values[2 * a], values[2 * a + 1], upper)
            for q in range(2):
                into[pl.ds(q * 8, 8), row0 + a, :] = tiles[q]

    def get_state(source):
        out = []
        for a in range(groups):
            out += swap_halves(source[pl.ds(0, 8), a, :], source[pl.ds(8, 8), a, :], upper)
        return jnp.stack(out)

    def each(value):
        return [value[m] for m in range(modes)]

    kt0, kt1 = tap(1, 1) * k1 + tap(1, 2) * k2, tap(1, 2) * k1
    vt0, vt1 = tap(2, 1) * v1 + tap(2, 2) * v2, tap(2, 2) * v1
    halo_s[0], halo_s[1], halo_s[2], halo_s[3] = kt0, kt1, vt0, vt1

    put_slices(fsf, each(final))
    edges = (km[0], km[1], kt0, kt1, vm[0], vm[1], vt0, vt1)
    put_slices(fsf, edges, groups)
    loads[2].wait()
    to_tiles(2, 0, blocks)
    q1, q2 = row(2, chunks - 1, 7), row(2, chunks - 1, 6)
    halo_s[4] = tap(0, 1) * q1 + tap(0, 2) * q2
    halo_s[5] = tap(0, 2) * q1
    per_mode(rate_ref, res)

    first_of_later = (1 - half) * ((me + 1) // n_half)
    pl.semaphore_wait(barrier, n_half - 1 + n_tp - 1 + half * n_half + first_of_later)

    def halo_copy():
        return pltpu.make_async_remote_copy(
            src_ref=halo_s,
            dst_ref=halo_r,
            send_sem=send_sem.at[0],
            recv_sem=recv_sem.at[0],
            device_id={"seq": me + 1},
            device_id_type=MESH,
        )

    @pl.when(me < n_seq - 1)
    def _():
        halo_copy().start()

    @pl.when(me == 0)
    def _():
        halo_r[...] = jnp.zeros_like(halo_r)

    def first_rows():
        for t in range(2):
            km[t] = km[t] + halo_r[t]
            vm[t] = vm[t] + halo_r[2 + t]
            pr[t] = km[t] * vm[t]

    in_half = [(3, 2), (1, 2), (2, 2), (3, 1), (3, 3), (1, 1), (1, 3), (2, 1), (2, 3)]
    in_half += [(3, 0), (1, 0), (2, 0), (0, 2), (0, 1), (0, 3)]
    to_other = [(dz, dy) for dz in (0, 1, 3, 2) for dy in (2, 1, 3, 0)]

    def at_step(step):
        dz, dy = step
        return lax.rem(place // 4 + dz, n_half // 4) * 4 + lax.rem(place + dy, 4)

    def exchange(which, source, into, shift=0):
        for step in in_half:
            other = at_step(step)
            pltpu.make_async_remote_copy(
                src_ref=source.at[other],
                dst_ref=into.at[place + shift],
                send_sem=send_sem.at[which],
                recv_sem=recv_sem.at[which],
                device_id={"seq": base + other},
                device_id_type=MESH,
            ).start()
        into[place + shift] = source[place]

    def landed(which, into):
        others = into.at[pl.ds(0, n_half - 1)]
        pltpu.make_async_copy(others, others, recv_sem.at[which]).wait()

    def sent(which, source):
        others = source.at[pl.ds(0, n_half - 1)]
        pltpu.make_async_copy(others, others, send_sem.at[which]).wait()

    def send_across(which, slot, target):
        for step in to_other:
            pltpu.make_async_remote_copy(
                src_ref=total.at[slot],
                dst_ref=across.at[slot, place],
                send_sem=send_sem.at[which],
                recv_sem=recv_sem.at[which],
                device_id={"seq": target + at_step(step)},
                device_id_type=MESH,
            ).start()

    def wait_across(sem, slot):
        pltpu.make_async_copy(across.at[slot], across.at[slot], sem).wait()

    exchange(1, fsf, rxf, 1)

    def tell(k, carry):
        pl.semaphore_signal(ready, inc=1, device_id={"seq": k}, device_id_type=MESH)
        return carry

    @pl.when(half == 1)
    def _():
        lax.fori_loop(0, n_half, tell, 0)
        across[1] = jnp.zeros(across.shape[1:], f32)

    @pl.when(half == 0)
    def _():
        across[0] = jnp.zeros(across.shape[1:], f32)

    rate = res[...]
    put_slices(dsl.at[0], each(jnp.exp(rate * (-float(length)))))
    put_slices(dsl.at[1], each(jnp.exp(rate * (-float(length - 2)))))
    put_slices(dsl.at[2], [dec[m] for m in range(modes)])
    before = (place * length).astype(f32)
    after = ((n_half - 1 - place) * length).astype(f32)
    powers[0] = jnp.exp(rate * -before)
    powers[1] = jnp.exp(rate * -after)
    growth[0] = jnp.exp(rate)
    growth[1] = jnp.exp(rate * 2.0)
    for a in range(3, 5):
        loads[at_load[a]].wait()
        to_tiles(a, 0, blocks)
    loads[7].wait()
    per_mode(res_ref, res)
    loads[8].wait()
    gain = gain_ref[...]

    def middle_pass(i, carry):
        q1, q2 = carry
        for s in range(SUBS):
            q0 = row(2, i, s)
            qm[i * 8 + s] = tap(0, 0) * q0 + tap(0, 1) * q1 + tap(0, 2) * q2
            st[i * 8 + s] = row(3, i, s)
            sc[i * 8 + s] = gain * row(4, i, s)
            q1, q2 = q0, q1
        return q1, q2

    lax.fori_loop(0, chunks, middle_pass, (zero, zero))

    @pl.when(me > 0)
    def _():
        halo_copy().wait_recv()

    old0, old1 = pr[0], pr[1]
    first_rows()
    bump[0, 0], bump[0, 1] = pr[0] - old0, pr[1] - old1

    def bump_copy(other):
        return pltpu.make_async_remote_copy(
            src_ref=bump.at[0],
            dst_ref=bump.at[1],
            send_sem=send_sem.at[9],
            recv_sem=recv_sem.at[9],
            device_id={"seq": other},
            device_id_type=MESH,
        )

    def tell_bump(k, carry):
        bump_copy(n_half + 1 + k).start()
        return carry

    @pl.when(me == n_half)
    def _():
        lax.fori_loop(0, n_half - 1, tell_bump, 0)

    @pl.when(me <= n_half)
    def _():
        bump[1] = jnp.zeros(bump.shape[1:], f32)

    qm[0] = qm[0] + halo_r[4]
    qm[1] = qm[1] + halo_r[5]

    rxf[0] = jnp.zeros(rxf.shape[1:], f32)
    landed(1, rxf)
    kh, vh = rxf[pl.ds(1, n_half), groups, :], rxf[pl.ds(1, n_half), groups + 2, :]
    kmix = kh + rxf[pl.ds(0, n_half), groups + 1, :]
    vmix = vh + rxf[pl.ds(0, n_half), groups + 3, :]
    extra = kmix * vmix - kh * vh
    turned = pltpu.roll(extra, 64, 1)
    high = lax.broadcasted_iota(jnp.int32, (n_half, LANES), 1) >= 64
    lift[0] = jnp.where(high, turned, extra)
    lift[1] = jnp.where(high, extra, turned)
    step_decay, lift_decay, one_decay = dsl[0, place], dsl[1, place], dsl[2, place]

    def scan_forward(p, state):
        ax[0, p] = state
        added = one_decay * lift[0, pl.ds(p, 1), :] + lift[1, pl.ds(p, 1), :]
        return step_decay * state + (rxf[p + 1, 0:groups, :] + lift_decay * added)

    total[0] = lax.fori_loop(0, n_half, scan_forward, jnp.zeros((groups, LANES), f32))
    exchange(2, ax.at[0], ar.at[0])

    @pl.when(half == 0)
    def _():
        pl.semaphore_wait(ready, n_half)
        send_across(7, 0, n_half)

    def local_pass(i, state):
        d, r = dec[...], res[...]
        block = pr[pl.ds(i * 8, 8)]
        for s in range(SUBS):
            state = d * state + block[s][None]
            cv[i * 8 + s] = jnp.sum(r * state, axis=0)
        return state

    lax.fori_loop(0, chunks, local_pass, state0)

    landed(2, ar.at[0])

    @pl.when(half == 1)
    def _():
        wait_across(recv_sem.at[7], 0)

    @pl.when(me > n_half)
    def _():
        bump_copy(me).wait_recv()

    crossed = get_state(across.at[0]) + growth[0] * bump[1, 0] + growth[1] * bump[1, 1]
    arrived = res[...] * dec[...] * (get_state(ar.at[0]) + powers[0] * crossed)

    def join_pass(i, state):
        d = dec[...]
        for s in range(SUBS):
            t = i * 8 + s
            conv = cv[t] + jnp.sum(state, axis=0)
            state = d * state
            mixed = st[t] + qm[t] * conv
            cv[t] = conv
            mx[t] = mixed
            put_row(0, i, s, mixed * mixed)
            put_row(1, i, s, sc[t] * mixed)
        return state

    lax.fori_loop(0, chunks, join_pass, arrived)

    for a in range(2):
        for i in range(chunks):
            partial = nat[a, pl.ds(i * 64, 8), :]
            for j in range(1, SUBS):
                partial = partial + nat[a, pl.ds(i * 64 + j * 8, 8), :]
            rows[a, pl.ds(i * 8, 8), :] = partial
        pss[pl.ds(a, 1), :] = jnp.sum(rows[a].T, axis=0, keepdims=True)

    def share(k, carry):
        other = lax.rem(mt + 1 + k, n_tp)
        pltpu.make_async_remote_copy(
            src_ref=pss,
            dst_ref=psr.at[mt],
            send_sem=send_sem.at[3],
            recv_sem=recv_sem.at[3],
            device_id={"tp": other},
            device_id_type=MESH,
        ).start()
        return carry

    lax.fori_loop(0, n_tp - 1, share, 0)
    psr[mt] = pss[...]
    peers = psr.at[pl.ds(0, n_tp - 1)]
    pltpu.make_async_copy(peers, peers, recv_sem.at[3]).wait()
    totals = jnp.sum(psr[...], axis=0)
    inverse = lax.rsqrt(totals[0:1] / width + epsilon)
    factor = inverse * inverse * inverse * totals[1:2] / width
    rows[0] = jnp.broadcast_to(inverse, (length, LANES)).T
    rows[1] = jnp.broadcast_to(factor, (length, LANES)).T

    def spread(a, t):
        return jnp.broadcast_to(rows[a, pl.ds(t, 1), :], (SUBS, LANES))

    def back_pass(n, state):
        i = chunks - 1 - n
        d = dec[...]
        for s in reversed(range(SUBS)):
            t = i * 8 + s
            dmixed = spread(0, t) * sc[t] - mx[t] * spread(1, t)
            dconv = dmixed * qm[t]
            dm[t] = dmixed
            dc[t] = dconv
            state = d * state + dconv[None]
        return state

    final_back = lax.fori_loop(0, chunks, back_pass, state0)
    put_slices(fsb, each(final_back))
    exchange(4, fsb, rxb)

    head_s[0] = dm[0] * cv[0]
    head_s[1] = dm[1] * cv[1]
    head_s[2] = dc[0]
    head_s[3], head_s[4] = km[0], km[1]
    head_s[5], head_s[6] = vm[0], vm[1]

    def head_copy():
        return pltpu.make_async_remote_copy(
            src_ref=head_s,
            dst_ref=head_r,
            send_sem=send_sem.at[6],
            recv_sem=recv_sem.at[6],
            device_id={"seq": me - 1},
            device_id_type=MESH,
        )

    @pl.when(me > 0)
    def _():
        head_copy().start()

    @pl.when(me == n_seq - 1)
    def _():
        head_r[...] = jnp.zeros_like(head_r)

    landed(4, rxb)

    def scan_backward(n, state):
        p = n_half - 1 - n
        ax[1, p] = state
        return step_decay * state + rxb[p]

    total[1] = lax.fori_loop(0, n_half, scan_backward, jnp.zeros((groups, LANES), f32))

    @pl.when(half == 1)
    def _():
        send_across(8, 1, 0)

    exchange(5, ax.at[1], ar.at[1])

    def adjoint_pass(n, state):
        i = chunks - 1 - n
        d, r = dec[...], res[...]
        for s in reversed(range(SUBS)):
            state = d * state + dc[i * 8 + s][None]
            dp[i * 8 + s] = jnp.sum(r * state, axis=0)
        return state

    lax.fori_loop(0, chunks, adjoint_pass, state0)

    @pl.when(me < n_seq - 1)
    def _():
        head_copy().wait_recv()

    def query_pass(n, carry):
        g1, g2 = carry
        i = chunks - 1 - n
        for s in reversed(range(SUBS)):
            t = i * 8 + s
            dmixed = dm[t]
            g0 = dmixed * cv[t]
            put_row(0, i, s, mx[t] * spread(0, t) * gain)
            put_row(1, i, s, dmixed)
            put_row(2, i, s, tap(0, 0) * g0 + tap(0, 1) * g1 + tap(0, 2) * g2)
            g1, g2 = g0, g1
        return g1, g2

    lax.fori_loop(0, chunks, query_pass, (head_r[0], head_r[1]))

    def from_tiles(a, target):
        def step(i, carry):
            for j in range(SUBS):
                block = jnp.concatenate(
                    [
                        nat[a, pl.ds(pl.multiple_of(i * 128 + j * 8, 8), 8), :],
                        nat[a, pl.ds(pl.multiple_of(i * 128 + 64 + j * 8, 8), 8), :],
                    ],
                    axis=0,
                )
                target[pl.ds(pl.multiple_of(i * 16, 16), 16), pl.ds(j * LANES, LANES)] = (
                    block.astype(jnp.bfloat16)
                )
            return carry

        lax.fori_loop(0, length // 16, step, 0)

    from_tiles(0, normed_ref)
    from_tiles(1, sgrad_ref)
    from_tiles(2, qgrad_ref)

    landed(5, ar.at[1])

    @pl.when(half == 0)
    def _():
        wait_across(recv_sem.at[8], 1)

    d, r = dec[...], res[...]
    after = get_state(ar.at[1]) + powers[1] * get_state(across.at[1])
    arrived_back = r * d * after
    dp0 = jnp.sum(r * after, axis=0)
    dp1 = jnp.sum(r * ((after - head_r[2][None]) / d), axis=0)
    carry0 = (
        arrived_back,
        dp0 * head_r[5],
        dp1 * head_r[6],
        dp0 * head_r[3],
        dp1 * head_r[4],
    )

    def last_pass(n, carry):
        state, a1, a2, b1, b2 = carry
        i = chunks - 1 - n
        d = dec[...]
        for s in reversed(range(SUBS)):
            t = i * 8 + s
            dproduct = dp[t] + jnp.sum(state, axis=0)
            state = d * state
            a0 = dproduct * vm[t]
            b0 = dproduct * km[t]
            put_row(3, i, s, tap(1, 0) * a0 + tap(1, 1) * a1 + tap(1, 2) * a2)
            put_row(4, i, s, tap(2, 0) * b0 + tap(2, 1) * b1 + tap(2, 2) * b2)
            a1, a2, b1, b2 = a0, a1, b0, b1
        return state, a1, a2, b1, b2

    lax.fori_loop(0, chunks, last_pass, carry0)
    from_tiles(3, kgrad_ref)
    from_tiles(4, vgrad_ref)

    @pl.when(me < n_seq - 1)
    def _():
        halo_copy().wait_send()

    @pl.when(me > 0)
    def _():
        head_copy().wait_send()

    @pl.when(me == n_half)
    def _():
        as_many = km.at[pl.ds(0, 2 * (n_half - 1))]
        pltpu.make_async_copy(as_many, as_many, send_sem.at[9]).wait()

    @pl.when(half == 0)
    def _():
        wait_across(send_sem.at[7], 0)

    @pl.when(half == 1)
    def _():
        wait_across(send_sem.at[8], 1)

    sent(1, fsf)
    sent(2, ax.at[0])
    sent(4, fsb)
    sent(5, ax.at[1])
    pltpu.make_async_copy(peers, peers, send_sem.at[3]).wait()


def write_out(*refs):
    sem = refs[-1]
    half = (len(refs) - 1) // 2
    copies = [
        pltpu.make_async_copy(refs[a], refs[half + a], sem.at[a]) for a in range(half)
    ]
    for copy in copies:
        copy.start()
    for copy in copies:
        copy.wait()


def solution(mesh):
    n_seq, n_tp = mesh.shape["seq"], mesh.shape["tp"]

    def body(q, k, v, stream, taps, rate, residue, gain, cotangent):
        length, channels = q.shape
        modes = rate.shape[0]
        assert channels == SUBS * LANES and n_seq == 32 and modes == 16 and length == LANES
        hbm = pl.BlockSpec(memory_space=pl.ANY)
        vmem = pl.BlockSpec(memory_space=pltpu.VMEM)
        out = jax.ShapeDtypeStruct((length, channels), jnp.bfloat16)
        tiles = pltpu.VMEM((length, SUBS, LANES), f32)
        per_mode = pltpu.VMEM((modes, SUBS, LANES), f32)
        n_half, groups = n_seq // 2, modes // 2
        slices = (n_half, groups, LANES)
        operands = (q, k, v, stream, cotangent, taps, rate, residue, gain.reshape(SUBS, LANES))
        results = pl.pallas_call(
            functools.partial(kernel, n_seq, n_tp),
            out_shape=(out,) * 5,
            in_specs=[hbm] * 9,
            out_specs=(vmem,) * 5,
            scratch_shapes=[
                pltpu.VMEM((5, length, channels), jnp.bfloat16),
                pltpu.VMEM(taps.shape, f32),
                pltpu.VMEM(rate.shape, f32),
                pltpu.VMEM(rate.shape, f32),
                pltpu.VMEM((SUBS, LANES), f32),
                pltpu.VMEM((5, length * SUBS, LANES), f32),
                pltpu.VMEM((modes * SUBS, LANES), f32),
                pltpu.VMEM((3 * 64, LANES), f32),
                per_mode,
                per_mode,
            ]
            + [tiles] * 11
            + [
                pltpu.VMEM((2, length, LANES), f32),
                pltpu.VMEM((6, SUBS, LANES), f32),
                pltpu.VMEM((6, SUBS, LANES), f32),
                pltpu.VMEM((7, SUBS, LANES), f32),
                pltpu.VMEM((7, SUBS, LANES), f32),
                pltpu.VMEM((n_half, groups + 4, LANES), f32),
                pltpu.VMEM(slices, f32),
                pltpu.VMEM((n_half + 1, groups + 4, LANES), f32),
                pltpu.VMEM(slices, f32),
                pltpu.VMEM((3,) + slices, f32),
                pltpu.VMEM((2, n_half, LANES), f32),
                pltpu.VMEM((2, modes, SUBS, LANES), f32),
                pltpu.VMEM((2,) + slices, f32),
                pltpu.VMEM((2,) + slices, f32),
                pltpu.VMEM((2, groups, LANES), f32),
                pltpu.VMEM((2,) + slices, f32),
                pltpu.VMEM((2, 2, SUBS, LANES), f32),
                pltpu.VMEM((2, modes, SUBS, LANES), f32),
                pltpu.VMEM((2, LANES), f32),
                pltpu.VMEM((n_tp, 2, LANES), f32),
                pltpu.SemaphoreType.DMA((9,)),
                pltpu.SemaphoreType.DMA((10,)),
                pltpu.SemaphoreType.DMA((10,)),
                pltpu.SemaphoreType.REGULAR,
            ],
            compiler_params=pltpu.CompilerParams(
                collective_id=0, has_side_effects=True, vmem_limit_bytes=40 * 1024 * 1024
            ),
        )(*[pltpu.with_memory_space_constraint(x, pltpu.HBM) for x in operands])
        return pl.pallas_call(
            write_out,
            out_shape=(out,) * 5,
            in_specs=[hbm] * 5,
            out_specs=(pl.BlockSpec(memory_space=pltpu.HBM),) * 5,
            scratch_shapes=[pltpu.SemaphoreType.DMA((5,))],
            compiler_params=pltpu.CompilerParams(vmem_limit_bytes=1024 * 1024),
        )(*results)

    seq_tp = P("seq", "tp")
    return jax.shard_map(
        body,
        mesh=mesh,
        in_specs=(
            seq_tp,
            seq_tp,
            seq_tp,
            seq_tp,
            P(None, None, "tp"),
            P(None, "tp"),
            P(None, "tp"),
            P("tp"),
            seq_tp,
        ),
        out_specs=(seq_tp,) * 5,
        check_vma=False,
    )
```

```python
import functools

import jax
import jax.numpy as jnp
from jax import lax
from jax.experimental import pallas as pl
from jax.experimental.pallas import tpu as pltpu
from jax.sharding import PartitionSpec as P

MESH = pl.DeviceIdType.MESH
f32 = jnp.float32
epsilon = 1e-05
LANES = 128
SUBS = 8
PARTS = 2


def swap_halves(first, second, upper):
    return (
        jnp.where(upper, pltpu.roll(second, 64, 1), first),
        jnp.where(upper, second, pltpu.roll(first, 64, 1)),
    )


def kernel(
    n_seq,
    n_tp,
    q_hbm,
    k_hbm,
    v_hbm,
    s_hbm,
    c_hbm,
    taps_hbm,
    rate_hbm,
    res_hbm,
    gain_hbm,
    normed_ref,
    sgrad_ref,
    qgrad_ref,
    km,
    vm,
    dp,
    dec,
    tapn,
    tail,
    inb,
    taps_ref,
    rate_ref,
    res_ref,
    gain_ref,
    nat,
    par,
    res,
    qm,
    pr,
    cv,
    st,
    sc,
    mx,
    dm,
    dc,
    rows,
    halo_s,
    halo_r,
    head_s,
    head_r,
    fsf,
    fsb,
    rxf,
    rxb,
    dsl,
    lift,
    powers,
    ax,
    ar,
    total,
    across,
    bump,
    growth,
    starts,
    pss,
    psr,
    in_sem,
    send_sem,
    recv_sem,
    ready,
):
    me = lax.axis_index("seq")
    mt = lax.axis_index("tp")
    n_half = n_seq // 2
    half, place = me // n_half, lax.rem(me, n_half)
    base = half * n_half
    length = km.shape[0]
    modes = rate_ref.shape[0]
    chunks = length // SUBS
    width = float(n_tp * SUBS * LANES)

    barrier = pltpu.get_barrier_semaphore()

    in_half = [(3, 2), (1, 2), (2, 2), (3, 1), (3, 3), (1, 1), (1, 3), (2, 1), (2, 3)]
    in_half += [(3, 0), (1, 0), (2, 0), (0, 2), (0, 1), (0, 3)]
    to_other = [(dz, dy) for dz in (0, 1, 3, 2) for dy in (2, 1, 3, 0)]
    along_tp = (4, 5, 3, 2, 6, 7, 1)

    def at_step(step):
        dz, dy = step
        return lax.rem(place // 4 + dz, n_half // 4) * 4 + lax.rem(place + dy, 4)

    def greet(device):
        pl.semaphore_signal(barrier, inc=1, device_id={"seq": device}, device_id_type=MESH)

    def greet_later(k, carry):
        greet(n_half + k)
        return carry

    @pl.when(me == n_half)
    def _():
        greet(me - 1)

    for step in in_half:
        greet(base + at_step(step))
    for step in along_tp:
        other = lax.rem(mt + step, n_tp)
        pl.semaphore_signal(barrier, inc=1, device_id={"tp": other}, device_id_type=MESH)

    @pl.when(half == 0)
    def _():
        lax.fori_loop(0, n_half, greet_later, 0)


    loads = []
    for a, (src, into) in enumerate(
        (
            (k_hbm, inb.at[0]),
            (v_hbm, inb.at[1]),
            (q_hbm, inb.at[2]),
            (taps_hbm, taps_ref),
            (rate_hbm, rate_ref),
            (s_hbm, inb.at[3]),
            (c_hbm, inb.at[4]),
            (res_hbm, res_ref),
            (gain_hbm, gain_ref),
        )
    ):
        copy = pltpu.make_async_copy(src, into, in_sem.at[a])
        copy.start()
        loads.append(copy)
    at_load = (0, 1, 2, 5, 6)


    def per_mode(source, into):
        for i in range(modes // SUBS):
            for j in range(SUBS):
                par[pl.ds(i * 64 + j * 8, 8), :] = source[
                    pl.ds(i * 8, 8), pl.ds(j * LANES, LANES)
                ]
        for m in range(modes):
            into[m] = par[pl.ds((m // 8) * 64 + m % 8, 8, stride=8), :]

    def tap_rows():
        for a in range(3):
            for j in range(SUBS):
                tapn[pl.ds((a * 8 + j) * 8, 3), :] = taps_ref[a, :, pl.ds(j * LANES, LANES)]

    def tap(a, b):
        return tapn[pl.ds(a * 64 + b, 8, stride=8), :]

    def to_tiles(a, first, last):
        def step(i, carry):
            block = inb[a, pl.ds(pl.multiple_of(i * 16, 16), 16), :].astype(f32)
            for h in range(2):
                for j in range(SUBS):
                    nat[a, pl.ds(pl.multiple_of(i * 128 + h * 64 + j * 8, 8), 8), :] = block[
                        h * 8 : h * 8 + 8, j * LANES : (j + 1) * LANES
                    ]
            return carry

        lax.fori_loop(first, last, step, 0)

    def row(a, i, s):
        return nat[a, pl.ds(i * 64 + s, 8, stride=8), :]

    def put_row(a, i, s, value):
        nat[a, pl.ds(i * 64 + s, 8, stride=8), :] = value

    zero = jnp.zeros((SUBS, LANES), f32)
    blocks = length // 16
    for a in range(2):
        loads[a].wait()
        to_tiles(a, 0, blocks)
    loads[3].wait()
    tap_rows()
    loads[4].wait()
    per_mode(rate_ref, dec)
    dec[...] = jnp.exp(-dec[...])

    def first_pass(i, carry):
        state, k1, k2, v1, v2 = carry
        d = dec[...]
        for s in range(SUBS):
            k0, v0 = row(0, i, s), row(1, i, s)
            kmix = tap(1, 0) * k0 + tap(1, 1) * k1 + tap(1, 2) * k2
            vmix = tap(2, 0) * v0 + tap(2, 1) * v1 + tap(2, 2) * v2
            prod = kmix * vmix
            km[i * 8 + s] = kmix
            vm[i * 8 + s] = vmix
            pr[i * 8 + s] = prod
            state = d * state + prod[None]
            k1, k2, v1, v2 = k0, k1, v0, v1
        return state, k1, k2, v1, v2

    state0 = jnp.zeros((modes, SUBS, LANES), f32)
    final, k1, k2, v1, v2 = lax.fori_loop(0, chunks, first_pass, (state0, zero, zero, zero, zero))
    upper = lax.broadcasted_iota(jnp.int32, (SUBS, LANES), 1) >= 64
    groups = modes // 2

    def put_slices(into, values, row0=0):
        for a in range(len(values) // 2):
            tiles = swap_halves(values[2 * a], values[2 * a + 1], upper)
            for q in range(2):
                into[pl.ds(q * 8, 8), row0 + a, :] = tiles[q]

    def get_state(source):
        out = []
        for a in range(groups):
            out += swap_halves(source[pl.ds(0, 8), a, :], source[pl.ds(8, 8), a, :], upper)
        return jnp.stack(out)

    def each(value):
        return [value[m] for m in range(modes)]

    kt0, kt1 = tap(1, 1) * k1 + tap(1, 2) * k2, tap(1, 2) * k1
    vt0, vt1 = tap(2, 1) * v1 + tap(2, 2) * v2, tap(2, 2) * v1
    halo_s[0], halo_s[1], halo_s[2], halo_s[3] = kt0, kt1, vt0, vt1

    put_slices(fsf, each(final))
    edges = (km[0], km[1], kt0, kt1, vm[0], vm[1], vt0, vt1)
    put_slices(fsf, edges, groups)
    loads[2].wait()
    to_tiles(2, 0, blocks)
    q1, q2 = row(2, chunks - 1, 7), row(2, chunks - 1, 6)
    halo_s[4] = tap(0, 1) * q1 + tap(0, 2) * q2
    halo_s[5] = tap(0, 2) * q1
    per_mode(rate_ref, res)

    first_of_later = (1 - half) * ((me + 1) // n_half)
    pl.semaphore_wait(barrier, n_half - 1 + n_tp - 1 + half * n_half + first_of_later)

    def halo_copy():
        return pltpu.make_async_remote_copy(
            src_ref=halo_s,
            dst_ref=halo_r,
            send_sem=send_sem.at[0],
            recv_sem=recv_sem.at[0],
            device_id={"seq": me + 1},
            device_id_type=MESH,
        )

    @pl.when(me < n_seq - 1)
    def _():
        halo_copy().start()

    @pl.when(me == 0)
    def _():
        halo_r[...] = jnp.zeros_like(halo_r)

    def first_rows():
        for t in range(2):
            km[t] = km[t] + halo_r[t]
            vm[t] = vm[t] + halo_r[2 + t]
            pr[t] = km[t] * vm[t]

    def exchange(which, source, into, shift=0):
        for step in in_half:
            other = at_step(step)
            pltpu.make_async_remote_copy(
                src_ref=source.at[other],
                dst_ref=into.at[place + shift],
                send_sem=send_sem.at[which],
                recv_sem=recv_sem.at[which],
                device_id={"seq": base + other},
                device_id_type=MESH,
            ).start()
        into[place + shift] = source[place]

    def landed(which, into):
        others = into.at[pl.ds(0, n_half - 1)]
        pltpu.make_async_copy(others, others, recv_sem.at[which]).wait()

    def sent(which, source):
        others = source.at[pl.ds(0, n_half - 1)]
        pltpu.make_async_copy(others, others, send_sem.at[which]).wait()

    def send_across(which, slot, target):
        for step in to_other:
            pltpu.make_async_remote_copy(
                src_ref=total.at[slot],
                dst_ref=across.at[slot, place],
                send_sem=send_sem.at[which],
                recv_sem=recv_sem.at[which],
                device_id={"seq": target + at_step(step)},
                device_id_type=MESH,
            ).start()

    def wait_across(sem, slot):
        pltpu.make_async_copy(across.at[slot], across.at[slot], sem).wait()

    exchange(1, fsf, rxf, 1)

    def tell(k, carry):
        pl.semaphore_signal(ready, inc=1, device_id={"seq": k}, device_id_type=MESH)
        return carry

    @pl.when(half == 1)
    def _():
        lax.fori_loop(0, n_half, tell, 0)
        across[1] = jnp.zeros(across.shape[1:], f32)

    @pl.when(half == 0)
    def _():
        across[0] = jnp.zeros(across.shape[1:], f32)

    rate = res[...]
    put_slices(dsl.at[0], each(jnp.exp(rate * (-float(length)))))
    put_slices(dsl.at[1], each(jnp.exp(rate * (-float(length - 2)))))
    put_slices(dsl.at[2], [dec[m] for m in range(modes)])
    before = (place * length).astype(f32)
    after = ((n_half - 1 - place) * length).astype(f32)
    powers[0] = jnp.exp(rate * -before)
    powers[1] = jnp.exp(rate * -after)
    growth[0] = jnp.exp(rate)
    growth[1] = jnp.exp(rate * 2.0)
    for part in range(1, PARTS):
        starts[part] = jnp.exp(rate * (-float(part * (length // PARTS))))
    pss[...] = jnp.zeros_like(pss)
    for a in range(3, 5):
        loads[at_load[a]].wait()
        to_tiles(a, 0, blocks)
    loads[7].wait()
    per_mode(res_ref, res)
    loads[8].wait()
    gain = gain_ref[...]

    def middle_pass(i, carry):
        q1, q2 = carry
        for s in range(SUBS):
            q0 = row(2, i, s)
            qm[i * 8 + s] = tap(0, 0) * q0 + tap(0, 1) * q1 + tap(0, 2) * q2
            st[i * 8 + s] = row(3, i, s)
            sc[i * 8 + s] = gain * row(4, i, s)
            q1, q2 = q0, q1
        return q1, q2

    lax.fori_loop(0, chunks, middle_pass, (zero, zero))

    @pl.when(me > 0)
    def _():
        halo_copy().wait_recv()

    old0, old1 = pr[0], pr[1]
    first_rows()
    bump[0, 0], bump[0, 1] = pr[0] - old0, pr[1] - old1

    def bump_copy(other):
        return pltpu.make_async_remote_copy(
            src_ref=bump.at[0],
            dst_ref=bump.at[1],
            send_sem=send_sem.at[9],
            recv_sem=recv_sem.at[9],
            device_id={"seq": other},
            device_id_type=MESH,
        )

    def tell_bump(k, carry):
        bump_copy(n_half + 1 + k).start()
        return carry

    @pl.when(me == n_half)
    def _():
        lax.fori_loop(0, n_half - 1, tell_bump, 0)

    @pl.when(me <= n_half)
    def _():
        bump[1] = jnp.zeros(bump.shape[1:], f32)

    qm[0] = qm[0] + halo_r[4]
    qm[1] = qm[1] + halo_r[5]

    rxf[0] = jnp.zeros(rxf.shape[1:], f32)
    landed(1, rxf)
    kh, vh = rxf[pl.ds(1, n_half), groups, :], rxf[pl.ds(1, n_half), groups + 2, :]
    kmix = kh + rxf[pl.ds(0, n_half), groups + 1, :]
    vmix = vh + rxf[pl.ds(0, n_half), groups + 3, :]
    extra = kmix * vmix - kh * vh
    turned = pltpu.roll(extra, 64, 1)
    high = lax.broadcasted_iota(jnp.int32, (n_half, LANES), 1) >= 64
    lift[0] = jnp.where(high, turned, extra)
    lift[1] = jnp.where(high, extra, turned)
    step_decay, lift_decay, one_decay = dsl[0, place], dsl[1, place], dsl[2, place]

    def scan_forward(p, state):
        ax[0, p] = state
        added = one_decay * lift[0, pl.ds(p, 1), :] + lift[1, pl.ds(p, 1), :]
        return step_decay * state + (rxf[p + 1, 0:groups, :] + lift_decay * added)

    total[0] = lax.fori_loop(0, n_half, scan_forward, jnp.zeros((groups, LANES), f32))
    exchange(2, ax.at[0], ar.at[0])

    @pl.when(half == 0)
    def _():
        pl.semaphore_wait(ready, n_half)
        send_across(7, 0, n_half)

    def local_pass(i, state):
        d, r = dec[...], res[...]
        block = pr[pl.ds(i * 8, 8)]
        for s in range(SUBS):
            state = d * state + block[s][None]
            cv[i * 8 + s] = jnp.sum(r * state, axis=0)
        return state

    lax.fori_loop(0, chunks, local_pass, state0)

    landed(2, ar.at[0])

    @pl.when(half == 1)
    def _():
        wait_across(recv_sem.at[7], 0)

    @pl.when(me > n_half)
    def _():
        bump_copy(me).wait_recv()

    crossed = get_state(across.at[0]) + growth[0] * bump[1, 0] + growth[1] * bump[1, 1]
    arrived = res[...] * dec[...] * (get_state(ar.at[0]) + powers[0] * crossed)

    def join_pass(i, state):
        d = dec[...]
        for s in range(SUBS):
            t = i * 8 + s
            conv = cv[t] + jnp.sum(state, axis=0)
            state = d * state
            mixed = st[t] + qm[t] * conv
            cv[t] = conv
            mx[t] = mixed
            put_row(0, i, s, mixed * mixed)
            put_row(1, i, s, sc[t] * mixed)
        return state

    span = length // PARTS
    step_chunks = chunks // PARTS
    order = list(reversed(range(PARTS)))

    for part in order:
        first = part * step_chunks
        start = arrived if part == 0 else arrived * starts[part]
        lax.fori_loop(first, first + step_chunks, join_pass, start)
        for a in range(2):
            for i in range(first, first + step_chunks):
                partial = nat[a, pl.ds(i * 64, 8), :]
                for j in range(1, SUBS):
                    partial = partial + nat[a, pl.ds(i * 64 + j * 8, 8), :]
                rows[a, pl.ds(i * 8, 8), :] = partial
            summed = rows[a, pl.ds(part * span, span), :].T
            pss[part, pl.ds(a, 1), pl.ds(0, span)] = jnp.sum(summed, axis=0, keepdims=True)
        for step in along_tp:
            pltpu.make_async_remote_copy(
                src_ref=pss.at[part],
                dst_ref=psr.at[part, mt],
                send_sem=send_sem.at[10 + part],
                recv_sem=recv_sem.at[10 + part],
                device_id={"tp": lax.rem(mt + step, n_tp)},
                device_id_type=MESH,
            ).start()
        psr[part, mt] = pss[part]

    def peers(part):
        return psr.at[part, pl.ds(0, n_tp - 1)]

    def spread(a, t):
        return jnp.broadcast_to(rows[a, pl.ds(t, 1), :], (SUBS, LANES))

    def back_pass(n, state):
        i = chunks - 1 - n
        d = dec[...]
        for s in reversed(range(SUBS)):
            t = i * 8 + s
            dmixed = spread(0, t) * sc[t] - mx[t] * spread(1, t)
            dconv = dmixed * qm[t]
            dm[t] = dmixed
            dc[t] = dconv
            state = d * state + dconv[None]
        return state

    final_back = state0
    for turn, part in enumerate(order):
        pltpu.make_async_copy(peers(part), peers(part), recv_sem.at[10 + part]).wait()
        totals = jnp.sum(psr[part], axis=0)
        inverse = lax.rsqrt(totals[0:1, 0:span] / width + epsilon)
        factor = inverse * inverse * inverse * totals[1:2, 0:span] / width
        rows[0, pl.ds(part * span, span), :] = jnp.broadcast_to(inverse, (LANES, span)).T
        rows[1, pl.ds(part * span, span), :] = jnp.broadcast_to(factor, (LANES, span)).T
        final_back = lax.fori_loop(
            turn * step_chunks, (turn + 1) * step_chunks, back_pass, final_back
        )
    put_slices(fsb, each(final_back))
    exchange(4, fsb, rxb)

    head_s[0] = dm[0] * cv[0]
    head_s[1] = dm[1] * cv[1]
    head_s[2] = dc[0]
    head_s[3], head_s[4] = km[0], km[1]
    head_s[5], head_s[6] = vm[0], vm[1]

    def head_copy():
        return pltpu.make_async_remote_copy(
            src_ref=head_s,
            dst_ref=head_r,
            send_sem=send_sem.at[6],
            recv_sem=recv_sem.at[6],
            device_id={"seq": me - 1},
            device_id_type=MESH,
        )

    @pl.when(me > 0)
    def _():
        head_copy().start()

    @pl.when(me == n_seq - 1)
    def _():
        head_r[...] = jnp.zeros_like(head_r)

    landed(4, rxb)

    def scan_backward(n, state):
        p = n_half - 1 - n
        ax[1, p] = state
        return step_decay * state + rxb[p]

    total[1] = lax.fori_loop(0, n_half, scan_backward, jnp.zeros((groups, LANES), f32))

    @pl.when(half == 1)
    def _():
        send_across(8, 1, 0)

    exchange(5, ax.at[1], ar.at[1])

    def adjoint_pass(n, state):
        i = chunks - 1 - n
        d, r = dec[...], res[...]
        for s in reversed(range(SUBS)):
            state = d * state + dc[i * 8 + s][None]
            dp[i * 8 + s] = jnp.sum(r * state, axis=0)
        return state

    lax.fori_loop(0, chunks, adjoint_pass, state0)

    @pl.when(me < n_seq - 1)
    def _():
        head_copy().wait_recv()

    def query_pass(n, carry):
        g1, g2 = carry
        i = chunks - 1 - n
        for s in reversed(range(SUBS)):
            t = i * 8 + s
            dmixed = dm[t]
            g0 = dmixed * cv[t]
            put_row(0, i, s, mx[t] * spread(0, t) * gain)
            put_row(1, i, s, dmixed)
            put_row(2, i, s, tap(0, 0) * g0 + tap(0, 1) * g1 + tap(0, 2) * g2)
            g1, g2 = g0, g1
        return g1, g2

    lax.fori_loop(0, chunks, query_pass, (head_r[0], head_r[1]))

    def from_tiles(a, target):
        def step(i, carry):
            for j in range(SUBS):
                block = jnp.concatenate(
                    [
                        nat[a, pl.ds(pl.multiple_of(i * 128 + j * 8, 8), 8), :],
                        nat[a, pl.ds(pl.multiple_of(i * 128 + 64 + j * 8, 8), 8), :],
                    ],
                    axis=0,
                )
                target[pl.ds(pl.multiple_of(i * 16, 16), 16), pl.ds(j * LANES, LANES)] = (
                    block.astype(jnp.bfloat16)
                )
            return carry

        lax.fori_loop(0, length // 16, step, 0)

    from_tiles(0, normed_ref)
    from_tiles(1, sgrad_ref)
    from_tiles(2, qgrad_ref)

    landed(5, ar.at[1])

    @pl.when(half == 0)
    def _():
        wait_across(recv_sem.at[8], 1)

    d, r = dec[...], res[...]
    after = get_state(ar.at[1]) + powers[1] * get_state(across.at[1])
    arrived_back = r * d * after
    dp0 = jnp.sum(r * after, axis=0)
    dp1 = jnp.sum(r * ((after - head_r[2][None]) / d), axis=0)
    tail[pl.ds(0, modes)] = arrived_back
    tail[modes], tail[modes + 1] = dp0 * head_r[5], dp1 * head_r[6]
    tail[modes + 2], tail[modes + 3] = dp0 * head_r[3], dp1 * head_r[4]

    @pl.when(me < n_seq - 1)
    def _():
        halo_copy().wait_send()

    @pl.when(me > 0)
    def _():
        head_copy().wait_send()

    @pl.when(me == n_half)
    def _():
        as_many = km.at[pl.ds(0, 2 * (n_half - 1))]
        pltpu.make_async_copy(as_many, as_many, send_sem.at[9]).wait()

    @pl.when(half == 0)
    def _():
        wait_across(send_sem.at[7], 0)

    @pl.when(half == 1)
    def _():
        wait_across(send_sem.at[8], 1)

    sent(1, fsf)
    sent(2, ax.at[0])
    sent(4, fsb)
    sent(5, ax.at[1])
    for part in order:
        pltpu.make_async_copy(peers(part), peers(part), send_sem.at[10 + part]).wait()


def finish(
    normed_ref,
    sgrad_ref,
    qgrad_ref,
    km,
    vm,
    dp,
    dec,
    tapn,
    tail,
    normed_hbm,
    sgrad_hbm,
    qgrad_hbm,
    kgrad_hbm,
    vgrad_hbm,
    nat,
    outb,
    sem,
):
    early = [
        pltpu.make_async_copy(source, target, sem.at[2 + a])
        for a, (source, target) in enumerate(
            ((normed_ref, normed_hbm), (sgrad_ref, sgrad_hbm), (qgrad_ref, qgrad_hbm))
        )
    ]
    for copy in early:
        copy.start()
    modes = dec.shape[0]
    blocks = km.shape[0] // 16

    def tap(a, b):
        return tapn[pl.ds(a * 64 + b, 8, stride=8), :]

    def late(a, first, count):
        target = (kgrad_hbm, vgrad_hbm)[a]
        return pltpu.make_async_copy(
            outb.at[a, pl.ds(first, count), :], target.at[pl.ds(first, count), :], sem.at[a]
        )

    def last_pass(n, carry):
        state, a1, a2, b1, b2 = carry
        block = blocks - 1 - n
        d = dec[...]
        for s in reversed(range(16)):
            t = block * 16 + s
            at = block * 128 + (s // 8) * 64 + s % 8
            dproduct = dp[t] + jnp.sum(state, axis=0)
            state = d * state
            a0 = dproduct * vm[t]
            b0 = dproduct * km[t]
            nat[0, pl.ds(at, 8, stride=8), :] = tap(1, 0) * a0 + tap(1, 1) * a1 + tap(1, 2) * a2
            nat[1, pl.ds(at, 8, stride=8), :] = tap(2, 0) * b0 + tap(2, 1) * b1 + tap(2, 2) * b2
            a1, a2, b1, b2 = a0, a1, b0, b1
        first = pl.multiple_of(block * 16, 16)
        for a in range(2):
            for j in range(SUBS):
                rows = [
                    nat[a, pl.ds(pl.multiple_of(block * 128 + h * 64 + j * 8, 8), 8), :]
                    for h in range(2)
                ]
                outb[a, pl.ds(first, 16), pl.ds(j * LANES, LANES)] = jnp.concatenate(
                    rows, axis=0
                ).astype(jnp.bfloat16)
            late(a, first, 16).start()
        return state, a1, a2, b1, b2

    edges = tuple(tail[modes + a] for a in range(4))
    lax.fori_loop(0, blocks, last_pass, (tail[pl.ds(0, modes)],) + edges)
    for a in range(2):
        late(a, 0, blocks * 16).wait()
    for copy in early:
        copy.wait()


def solution(mesh):
    n_seq, n_tp = mesh.shape["seq"], mesh.shape["tp"]

    def body(q, k, v, stream, taps, rate, residue, gain, cotangent):
        length, channels = q.shape
        modes = rate.shape[0]
        assert channels == SUBS * LANES and n_seq == 32 and modes == 16 and length == LANES
        hbm = pl.BlockSpec(memory_space=pl.ANY)
        vmem = pl.BlockSpec(memory_space=pltpu.VMEM)
        out = jax.ShapeDtypeStruct((length, channels), jnp.bfloat16)
        tiles = pltpu.VMEM((length, SUBS, LANES), f32)
        per_mode = pltpu.VMEM((modes, SUBS, LANES), f32)
        n_half, groups = n_seq // 2, modes // 2
        slices = (n_half, groups, LANES)
        operands = (q, k, v, stream, cotangent, taps, rate, residue, gain.reshape(SUBS, LANES))
        results = pl.pallas_call(
            functools.partial(kernel, n_seq, n_tp),
            out_shape=(out,) * 3
            + (jax.ShapeDtypeStruct((length, SUBS, LANES), f32),) * 3
            + (
                jax.ShapeDtypeStruct((modes, SUBS, LANES), f32),
                jax.ShapeDtypeStruct((3 * 64, LANES), f32),
                jax.ShapeDtypeStruct((modes + 4, SUBS, LANES), f32),
            ),
            in_specs=[hbm] * 9,
            out_specs=(vmem,) * 9,
            scratch_shapes=[
                pltpu.VMEM((5, length, channels), jnp.bfloat16),
                pltpu.VMEM(taps.shape, f32),
                pltpu.VMEM(rate.shape, f32),
                pltpu.VMEM(rate.shape, f32),
                pltpu.VMEM((SUBS, LANES), f32),
                pltpu.VMEM((5, length * SUBS, LANES), f32),
                pltpu.VMEM((modes * SUBS, LANES), f32),
                per_mode,
            ]
            + [tiles] * 8
            + [
                pltpu.VMEM((2, length, LANES), f32),
                pltpu.VMEM((6, SUBS, LANES), f32),
                pltpu.VMEM((6, SUBS, LANES), f32),
                pltpu.VMEM((7, SUBS, LANES), f32),
                pltpu.VMEM((7, SUBS, LANES), f32),
                pltpu.VMEM((n_half, groups + 4, LANES), f32),
                pltpu.VMEM(slices, f32),
                pltpu.VMEM((n_half + 1, groups + 4, LANES), f32),
                pltpu.VMEM(slices, f32),
                pltpu.VMEM((3,) + slices, f32),
                pltpu.VMEM((2, n_half, LANES), f32),
                pltpu.VMEM((2, modes, SUBS, LANES), f32),
                pltpu.VMEM((2,) + slices, f32),
                pltpu.VMEM((2,) + slices, f32),
                pltpu.VMEM((2, groups, LANES), f32),
                pltpu.VMEM((2,) + slices, f32),
                pltpu.VMEM((2, 2, SUBS, LANES), f32),
                pltpu.VMEM((2, modes, SUBS, LANES), f32),
                pltpu.VMEM((PARTS, modes, SUBS, LANES), f32),
                pltpu.VMEM((PARTS, 2, LANES), f32),
                pltpu.VMEM((PARTS, n_tp, 2, LANES), f32),
                pltpu.SemaphoreType.DMA((9,)),
                pltpu.SemaphoreType.DMA((10 + PARTS,)),
                pltpu.SemaphoreType.DMA((10 + PARTS,)),
                pltpu.SemaphoreType.REGULAR,
            ],
            compiler_params=pltpu.CompilerParams(
                collective_id=0, has_side_effects=True, vmem_limit_bytes=40 * 1024 * 1024
            ),
        )(*[pltpu.with_memory_space_constraint(x, pltpu.HBM) for x in operands])
        return pl.pallas_call(
            finish,
            out_shape=(out,) * 5,
            in_specs=[vmem] * 9,
            out_specs=(pl.BlockSpec(memory_space=pltpu.HBM),) * 5,
            scratch_shapes=[
                pltpu.VMEM((2, length * SUBS, LANES), f32),
                pltpu.VMEM((2, length, channels), jnp.bfloat16),
                pltpu.SemaphoreType.DMA((5,)),
            ],
            compiler_params=pltpu.CompilerParams(vmem_limit_bytes=8 * 1024 * 1024),
        )(*results)

    seq_tp = P("seq", "tp")
    return jax.shard_map(
        body,
        mesh=mesh,
        in_specs=(
            seq_tp,
            seq_tp,
            seq_tp,
            seq_tp,
            P(None, None, "tp"),
            P(None, "tp"),
            P(None, "tp"),
            P("tp"),
            seq_tp,
        ),
        out_specs=(seq_tp,) * 5,
        check_vma=False,
    )
```

```python
import functools

import jax
import jax.numpy as jnp
from jax import lax
from jax.experimental import pallas as pl
from jax.experimental.pallas import tpu as pltpu
from jax.sharding import PartitionSpec as P

MESH = pl.DeviceIdType.MESH
f32 = jnp.float32
epsilon = 1e-05
LANES = 128
SUBS = 8
PARTS = 2
ROWS = 16


def swap_halves(first, second, upper):
    return (
        jnp.where(upper, pltpu.roll(second, 64, 1), first),
        jnp.where(upper, second, pltpu.roll(first, 64, 1)),
    )


def kernel(
    n_seq,
    n_tp,
    q_hbm,
    k_hbm,
    v_hbm,
    s_hbm,
    c_hbm,
    taps_hbm,
    rate_hbm,
    res_hbm,
    gain_hbm,
    normed_ref,
    sgrad_ref,
    qgrad_ref,
    km,
    vm,
    dp,
    dec,
    tapn,
    tail,
    inb,
    taps_ref,
    rate_ref,
    res_ref,
    gain_ref,
    nat,
    par,
    res,
    qm,
    pr,
    cv,
    st,
    sc,
    mx,
    dm,
    dc,
    rows,
    halo_s,
    halo_r,
    head_s,
    head_r,
    fsf,
    fsb,
    rxf,
    rxb,
    dsl,
    lift,
    powers,
    ax,
    ar,
    total,
    across,
    bump,
    growth,
    starts,
    pss,
    psr,
    in_sem,
    send_sem,
    recv_sem,
    ready,
):
    me = lax.axis_index("seq")
    mt = lax.axis_index("tp")
    n_half = n_seq // 2
    half, place = me // n_half, lax.rem(me, n_half)
    base = half * n_half
    length = km.shape[0]
    modes = rate_ref.shape[0]
    chunks = length // SUBS
    width = float(n_tp * SUBS * LANES)

    barrier = pltpu.get_barrier_semaphore()

    in_half = [(3, 2), (1, 2), (2, 2), (3, 1), (3, 3), (1, 1), (1, 3), (2, 1), (2, 3)]
    in_half += [(3, 0), (1, 0), (2, 0), (0, 2), (0, 1), (0, 3)]
    to_other = [(dz, dy) for dz in (0, 1, 3, 2) for dy in (2, 1, 3, 0)]
    along_tp = (4, 5, 3, 2, 6, 7, 1)

    def at_step(step):
        dz, dy = step
        return lax.rem(place // 4 + dz, n_half // 4) * 4 + lax.rem(place + dy, 4)

    def greet(device):
        pl.semaphore_signal(barrier, inc=1, device_id={"seq": device}, device_id_type=MESH)

    def greet_later(k, carry):
        greet(n_half + k)
        return carry

    @pl.when(me == n_half)
    def _():
        greet(me - 1)

    for step in in_half:
        greet(base + at_step(step))
    for step in along_tp:
        other = lax.rem(mt + step, n_tp)
        pl.semaphore_signal(barrier, inc=1, device_id={"tp": other}, device_id_type=MESH)

    @pl.when(half == 0)
    def _():
        lax.fori_loop(0, n_half, greet_later, 0)


    loads = []
    for a, (src, into) in enumerate(
        (
            (k_hbm, inb.at[0]),
            (v_hbm, inb.at[1]),
            (q_hbm, inb.at[2]),
            (taps_hbm, taps_ref),
            (rate_hbm, rate_ref),
            (s_hbm, inb.at[3]),
            (c_hbm, inb.at[4]),
            (res_hbm, res_ref),
            (gain_hbm, gain_ref),
        )
    ):
        copy = pltpu.make_async_copy(src, into, in_sem.at[a])
        copy.start()
        loads.append(copy)
    at_load = (0, 1, 2, 5, 6)


    def per_mode(source, into):
        for i in range(modes // SUBS):
            for j in range(SUBS):
                par[pl.ds(i * 64 + j * 8, 8), :] = source[
                    pl.ds(i * 8, 8), pl.ds(j * LANES, LANES)
                ]
        for m in range(modes):
            into[m] = par[pl.ds((m // 8) * 64 + m % 8, 8, stride=8), :]

    def tap_rows():
        for a in range(3):
            for j in range(SUBS):
                tapn[pl.ds((a * 8 + j) * 8, 3), :] = taps_ref[a, :, pl.ds(j * LANES, LANES)]

    def tap(a, b):
        return tapn[pl.ds(a * 64 + b, 8, stride=8), :]

    def to_tiles(a, first, last):
        def step(i, carry):
            block = inb[a, pl.ds(pl.multiple_of(i * 16, 16), 16), :].astype(f32)
            for h in range(2):
                for j in range(SUBS):
                    nat[a, pl.ds(pl.multiple_of(i * 128 + h * 64 + j * 8, 8), 8), :] = block[
                        h * 8 : h * 8 + 8, j * LANES : (j + 1) * LANES
                    ]
            return carry

        lax.fori_loop(first, last, step, 0)

    def row(a, i, s):
        return nat[a, pl.ds(i * 64 + s, 8, stride=8), :]

    def put_row(a, i, s, value):
        nat[a, pl.ds(i * 64 + s, 8, stride=8), :] = value

    zero = jnp.zeros((SUBS, LANES), f32)
    blocks = length // 16
    for a in range(2):
        loads[a].wait()
        to_tiles(a, 0, blocks)
    loads[3].wait()
    tap_rows()
    loads[4].wait()
    per_mode(rate_ref, dec)
    dec[...] = jnp.exp(-dec[...])

    def first_pass(i, carry):
        state, k1, k2, v1, v2 = carry
        d = dec[...]
        for s in range(SUBS):
            k0, v0 = row(0, i, s), row(1, i, s)
            kmix = tap(1, 0) * k0 + tap(1, 1) * k1 + tap(1, 2) * k2
            vmix = tap(2, 0) * v0 + tap(2, 1) * v1 + tap(2, 2) * v2
            prod = kmix * vmix
            km[i * 8 + s] = kmix
            vm[i * 8 + s] = vmix
            pr[i * 8 + s] = prod
            state = d * state + prod[None]
            k1, k2, v1, v2 = k0, k1, v0, v1
        return state, k1, k2, v1, v2

    state0 = jnp.zeros((modes, SUBS, LANES), f32)
    final, k1, k2, v1, v2 = lax.fori_loop(0, chunks, first_pass, (state0, zero, zero, zero, zero))
    upper = lax.broadcasted_iota(jnp.int32, (SUBS, LANES), 1) >= 64
    groups = modes // 2

    def put_slices(into, values, row0=0):
        for a in range(len(values) // 2):
            tiles = swap_halves(values[2 * a], values[2 * a + 1], upper)
            for q in range(2):
                into[pl.ds(q * 8, 8), row0 + a, :] = tiles[q]

    def get_state(source):
        out = []
        for a in range(groups):
            out += swap_halves(source[pl.ds(0, 8), a, :], source[pl.ds(8, 8), a, :], upper)
        return jnp.stack(out)

    def each(value):
        return [value[m] for m in range(modes)]

    kt0, kt1 = tap(1, 1) * k1 + tap(1, 2) * k2, tap(1, 2) * k1
    vt0, vt1 = tap(2, 1) * v1 + tap(2, 2) * v2, tap(2, 2) * v1
    halo_s[0], halo_s[1], halo_s[2], halo_s[3] = kt0, kt1, vt0, vt1

    put_slices(fsf, each(final))
    edges = (km[0], km[1], kt0, kt1, vm[0], vm[1], vt0, vt1)
    put_slices(fsf, edges, groups)
    loads[2].wait()
    to_tiles(2, 0, blocks)
    q1, q2 = row(2, chunks - 1, 7), row(2, chunks - 1, 6)
    halo_s[4] = tap(0, 1) * q1 + tap(0, 2) * q2
    halo_s[5] = tap(0, 2) * q1
    per_mode(rate_ref, res)

    first_of_later = (1 - half) * ((me + 1) // n_half)
    pl.semaphore_wait(barrier, n_half - 1 + n_tp - 1 + half * n_half + first_of_later)

    def halo_copy():
        return pltpu.make_async_remote_copy(
            src_ref=halo_s,
            dst_ref=halo_r,
            send_sem=send_sem.at[0],
            recv_sem=recv_sem.at[0],
            device_id={"seq": me + 1},
            device_id_type=MESH,
        )

    @pl.when(me == 0)
    def _():
        halo_r[...] = jnp.zeros_like(halo_r)

    def first_rows():
        for t in range(2):
            km[t] = km[t] + halo_r[t]
            vm[t] = vm[t] + halo_r[2 + t]
            pr[t] = km[t] * vm[t]

    def exchange(which, source, into, shift=0):
        for step in in_half:
            other = at_step(step)
            pltpu.make_async_remote_copy(
                src_ref=source.at[other],
                dst_ref=into.at[place + shift],
                send_sem=send_sem.at[which],
                recv_sem=recv_sem.at[which],
                device_id={"seq": base + other},
                device_id_type=MESH,
            ).start()
        into[place + shift] = source[place]

    def landed(which, into):
        others = into.at[pl.ds(0, n_half - 1)]
        pltpu.make_async_copy(others, others, recv_sem.at[which]).wait()

    def sent(which, source):
        others = source.at[pl.ds(0, n_half - 1)]
        pltpu.make_async_copy(others, others, send_sem.at[which]).wait()

    def send_across(which, slot, target):
        for step in to_other:
            pltpu.make_async_remote_copy(
                src_ref=total.at[slot],
                dst_ref=across.at[slot, place],
                send_sem=send_sem.at[which],
                recv_sem=recv_sem.at[which],
                device_id={"seq": target + at_step(step)},
                device_id_type=MESH,
            ).start()

    def wait_across(sem, slot):
        pltpu.make_async_copy(across.at[slot], across.at[slot], sem).wait()

    exchange(1, fsf, rxf, 1)

    @pl.when(me < n_seq - 1)
    def _():
        halo_copy().start()

    def tell(k, carry):
        pl.semaphore_signal(ready, inc=1, device_id={"seq": k}, device_id_type=MESH)
        return carry

    @pl.when(half == 1)
    def _():
        lax.fori_loop(0, n_half, tell, 0)
        across[1] = jnp.zeros(across.shape[1:], f32)

    @pl.when(half == 0)
    def _():
        across[0] = jnp.zeros(across.shape[1:], f32)

    rate = res[...]
    put_slices(dsl.at[0], each(jnp.exp(rate * (-float(length)))))
    put_slices(dsl.at[1], each(jnp.exp(rate * (-float(length - 2)))))
    put_slices(dsl.at[2], [dec[m] for m in range(modes)])
    before = (place * length).astype(f32)
    after = ((n_half - 1 - place) * length).astype(f32)
    powers[0] = jnp.exp(rate * -before)
    powers[1] = jnp.exp(rate * -after)
    growth[0] = jnp.exp(rate)
    growth[1] = jnp.exp(rate * 2.0)
    for part in range(1, PARTS):
        starts[part] = jnp.exp(rate * (-float(part * (length // PARTS))))
    pss[...] = jnp.zeros_like(pss)
    for a in range(3, 5):
        loads[at_load[a]].wait()
        to_tiles(a, 0, blocks)
    loads[7].wait()
    per_mode(res_ref, res)
    loads[8].wait()
    gain = gain_ref[...]

    def middle_pass(i, carry):
        q1, q2 = carry
        for s in range(SUBS):
            q0 = row(2, i, s)
            qm[i * 8 + s] = tap(0, 0) * q0 + tap(0, 1) * q1 + tap(0, 2) * q2
            st[i * 8 + s] = row(3, i, s)
            sc[i * 8 + s] = gain * row(4, i, s)
            q1, q2 = q0, q1
        return q1, q2

    lax.fori_loop(0, chunks, middle_pass, (zero, zero))

    @pl.when(me > 0)
    def _():
        halo_copy().wait_recv()

    old0, old1 = pr[0], pr[1]
    first_rows()
    bump[0, 0], bump[0, 1] = pr[0] - old0, pr[1] - old1

    def bump_copy(other):
        return pltpu.make_async_remote_copy(
            src_ref=bump.at[0],
            dst_ref=bump.at[1],
            send_sem=send_sem.at[9],
            recv_sem=recv_sem.at[9],
            device_id={"seq": other},
            device_id_type=MESH,
        )

    def tell_bump(k, carry):
        bump_copy(n_half + 1 + k).start()
        return carry

    @pl.when(me == n_half)
    def _():
        lax.fori_loop(0, n_half - 1, tell_bump, 0)

    @pl.when(me <= n_half)
    def _():
        bump[1] = jnp.zeros(bump.shape[1:], f32)

    qm[0] = qm[0] + halo_r[4]
    qm[1] = qm[1] + halo_r[5]

    rxf[0] = jnp.zeros(rxf.shape[1:], f32)
    landed(1, rxf)
    kh, vh = rxf[pl.ds(1, n_half), groups, :], rxf[pl.ds(1, n_half), groups + 2, :]
    kmix = kh + rxf[pl.ds(0, n_half), groups + 1, :]
    vmix = vh + rxf[pl.ds(0, n_half), groups + 3, :]
    extra = kmix * vmix - kh * vh
    turned = pltpu.roll(extra, 64, 1)
    high = lax.broadcasted_iota(jnp.int32, (n_half, LANES), 1) >= 64
    lift[0] = jnp.where(high, turned, extra)
    lift[1] = jnp.where(high, extra, turned)
    step_decay, lift_decay, one_decay = dsl[0, place], dsl[1, place], dsl[2, place]

    def scan_forward(p, state):
        ax[0, p] = state
        added = one_decay * lift[0, pl.ds(p, 1), :] + lift[1, pl.ds(p, 1), :]
        return step_decay * state + (rxf[p + 1, 0:groups, :] + lift_decay * added)

    passed = jnp.zeros((groups, LANES), f32)
    for p in range(n_half):
        passed = scan_forward(p, passed)
    total[0] = passed
    exchange(2, ax.at[0], ar.at[0])

    @pl.when(half == 0)
    def _():
        pl.semaphore_wait(ready, n_half)
        send_across(7, 0, n_half)

    def local_pass(i, state):
        d, r = dec[...], res[...]
        block = pr[pl.ds(i * 8, 8)]
        for s in range(SUBS):
            state = d * state + block[s][None]
            cv[i * 8 + s] = jnp.sum(r * state, axis=0)
        return state

    lax.fori_loop(0, chunks, local_pass, state0)

    landed(2, ar.at[0])

    @pl.when(half == 1)
    def _():
        wait_across(recv_sem.at[7], 0)

    @pl.when(me > n_half)
    def _():
        bump_copy(me).wait_recv()

    crossed = get_state(across.at[0]) + growth[0] * bump[1, 0] + growth[1] * bump[1, 1]
    arrived = res[...] * dec[...] * (get_state(ar.at[0]) + powers[0] * crossed)

    def join_pass(i, state):
        d = dec[...]
        for s in range(ROWS):
            t = i * ROWS + s
            conv = cv[t] + jnp.sum(state, axis=0)
            state = d * state
            mixed = st[t] + qm[t] * conv
            cv[t] = conv
            mx[t] = mixed
            put_row(0, i * (ROWS // 8) + s // 8, s % 8, mixed * mixed)
            put_row(1, i * (ROWS // 8) + s // 8, s % 8, sc[t] * mixed)
        return state

    span = length // PARTS
    step_chunks = chunks // PARTS
    order = list(reversed(range(PARTS)))

    for part in order:
        first = part * step_chunks
        start = arrived if part == 0 else arrived * starts[part]
        lax.fori_loop(part * span // ROWS, (part + 1) * span // ROWS, join_pass, start)
        for a in range(2):
            for i in range(first, first + step_chunks):
                partial = nat[a, pl.ds(i * 64, 8), :]
                for j in range(1, SUBS):
                    partial = partial + nat[a, pl.ds(i * 64 + j * 8, 8), :]
                rows[a, pl.ds(i * 8, 8), :] = partial
            summed = rows[a, pl.ds(part * span, span), :].T
            pss[part, pl.ds(a, 1), pl.ds(0, span)] = jnp.sum(summed, axis=0, keepdims=True)
        for step in along_tp:
            pltpu.make_async_remote_copy(
                src_ref=pss.at[part],
                dst_ref=psr.at[part, mt],
                send_sem=send_sem.at[10 + part],
                recv_sem=recv_sem.at[10 + part],
                device_id={"tp": lax.rem(mt + step, n_tp)},
                device_id_type=MESH,
            ).start()
        psr[part, mt] = pss[part]

    def peers(part):
        return psr.at[part, pl.ds(0, n_tp - 1)]

    def spread(a, t):
        return jnp.broadcast_to(rows[a, pl.ds(t, 1), :], (SUBS, LANES))

    def back_pass(n, state):
        i = length // ROWS - 1 - n
        d = dec[...]
        for s in reversed(range(ROWS)):
            t = i * ROWS + s
            dmixed = spread(0, t) * sc[t] - mx[t] * spread(1, t)
            dconv = dmixed * qm[t]
            dm[t] = dmixed
            dc[t] = dconv
            state = d * state + dconv[None]
        return state

    final_back = state0
    for turn, part in enumerate(order):
        pltpu.make_async_copy(peers(part), peers(part), recv_sem.at[10 + part]).wait()
        totals = jnp.sum(psr[part], axis=0)
        inverse = lax.rsqrt(totals[0:1, 0:span] / width + epsilon)
        factor = inverse * inverse * inverse * totals[1:2, 0:span] / width
        rows[0, pl.ds(part * span, span), :] = jnp.broadcast_to(inverse, (LANES, span)).T
        rows[1, pl.ds(part * span, span), :] = jnp.broadcast_to(factor, (LANES, span)).T
        final_back = lax.fori_loop(
            turn * span // ROWS, (turn + 1) * span // ROWS, back_pass, final_back
        )
    put_slices(fsb, each(final_back))
    exchange(4, fsb, rxb)

    head_s[0] = dm[0] * cv[0]
    head_s[1] = dm[1] * cv[1]
    head_s[2] = dc[0]
    head_s[3], head_s[4] = km[0], km[1]
    head_s[5], head_s[6] = vm[0], vm[1]

    def head_copy():
        return pltpu.make_async_remote_copy(
            src_ref=head_s,
            dst_ref=head_r,
            send_sem=send_sem.at[6],
            recv_sem=recv_sem.at[6],
            device_id={"seq": me - 1},
            device_id_type=MESH,
        )

    @pl.when(me > 0)
    def _():
        head_copy().start()

    @pl.when(me == n_seq - 1)
    def _():
        head_r[...] = jnp.zeros_like(head_r)

    landed(4, rxb)

    def scan_backward(n, state):
        p = n_half - 1 - n
        ax[1, p] = state
        return step_decay * state + rxb[p]

    passed = jnp.zeros((groups, LANES), f32)
    for n in range(n_half):
        passed = scan_backward(n, passed)
    total[1] = passed

    @pl.when(half == 1)
    def _():
        send_across(8, 1, 0)

    exchange(5, ax.at[1], ar.at[1])

    def adjoint_pass(n, state):
        i = chunks - 1 - n
        d, r = dec[...], res[...]
        for s in reversed(range(SUBS)):
            state = d * state + dc[i * 8 + s][None]
            dp[i * 8 + s] = jnp.sum(r * state, axis=0)
        return state

    lax.fori_loop(0, chunks, adjoint_pass, state0)

    @pl.when(me < n_seq - 1)
    def _():
        head_copy().wait_recv()

    def query_pass(n, carry):
        g1, g2 = carry
        i = chunks - 1 - n
        for s in reversed(range(SUBS)):
            t = i * 8 + s
            dmixed = dm[t]
            g0 = dmixed * cv[t]
            put_row(0, i, s, mx[t] * spread(0, t) * gain)
            put_row(1, i, s, dmixed)
            put_row(2, i, s, tap(0, 0) * g0 + tap(0, 1) * g1 + tap(0, 2) * g2)
            g1, g2 = g0, g1
        return g1, g2

    lax.fori_loop(0, chunks, query_pass, (head_r[0], head_r[1]))

    def from_tiles(a, target):
        def step(i, carry):
            for j in range(SUBS):
                block = jnp.concatenate(
                    [
                        nat[a, pl.ds(pl.multiple_of(i * 128 + j * 8, 8), 8), :],
                        nat[a, pl.ds(pl.multiple_of(i * 128 + 64 + j * 8, 8), 8), :],
                    ],
                    axis=0,
                )
                target[pl.ds(pl.multiple_of(i * 16, 16), 16), pl.ds(j * LANES, LANES)] = (
                    block.astype(jnp.bfloat16)
                )
            return carry

        lax.fori_loop(0, length // 16, step, 0)

    from_tiles(0, normed_ref)
    from_tiles(1, sgrad_ref)
    from_tiles(2, qgrad_ref)

    landed(5, ar.at[1])

    @pl.when(half == 0)
    def _():
        wait_across(recv_sem.at[8], 1)

    d, r = dec[...], res[...]
    after = get_state(ar.at[1]) + powers[1] * get_state(across.at[1])
    arrived_back = r * d * after
    dp0 = jnp.sum(r * after, axis=0)
    dp1 = jnp.sum(r * ((after - head_r[2][None]) / d), axis=0)
    tail[pl.ds(0, modes)] = arrived_back
    tail[modes], tail[modes + 1] = dp0 * head_r[5], dp1 * head_r[6]
    tail[modes + 2], tail[modes + 3] = dp0 * head_r[3], dp1 * head_r[4]

    @pl.when(me < n_seq - 1)
    def _():
        halo_copy().wait_send()

    @pl.when(me > 0)
    def _():
        head_copy().wait_send()

    @pl.when(me == n_half)
    def _():
        as_many = km.at[pl.ds(0, 2 * (n_half - 1))]
        pltpu.make_async_copy(as_many, as_many, send_sem.at[9]).wait()

    @pl.when(half == 0)
    def _():
        wait_across(send_sem.at[7], 0)

    @pl.when(half == 1)
    def _():
        wait_across(send_sem.at[8], 1)

    sent(1, fsf)
    sent(2, ax.at[0])
    sent(4, fsb)
    sent(5, ax.at[1])
    for part in order:
        pltpu.make_async_copy(peers(part), peers(part), send_sem.at[10 + part]).wait()


def finish(
    normed_ref,
    sgrad_ref,
    qgrad_ref,
    km,
    vm,
    dp,
    dec,
    tapn,
    tail,
    normed_hbm,
    sgrad_hbm,
    qgrad_hbm,
    kgrad_hbm,
    vgrad_hbm,
    nat,
    outb,
    sem,
):
    early = [
        pltpu.make_async_copy(source, target, sem.at[2 + a])
        for a, (source, target) in enumerate(
            ((normed_ref, normed_hbm), (sgrad_ref, sgrad_hbm), (qgrad_ref, qgrad_hbm))
        )
    ]
    for copy in early:
        copy.start()
    modes = dec.shape[0]
    blocks = km.shape[0] // 16

    def tap(a, b):
        return tapn[pl.ds(a * 64 + b, 8, stride=8), :]

    def late(a, first, count):
        target = (kgrad_hbm, vgrad_hbm)[a]
        return pltpu.make_async_copy(
            outb.at[a, pl.ds(first, count), :], target.at[pl.ds(first, count), :], sem.at[a]
        )

    def last_pass(n, carry):
        state, a1, a2, b1, b2 = carry
        block = blocks - 1 - n
        d = dec[...]
        for s in reversed(range(16)):
            t = block * 16 + s
            at = block * 128 + (s // 8) * 64 + s % 8
            dproduct = dp[t] + jnp.sum(state, axis=0)
            state = d * state
            a0 = dproduct * vm[t]
            b0 = dproduct * km[t]
            nat[0, pl.ds(at, 8, stride=8), :] = tap(1, 0) * a0 + tap(1, 1) * a1 + tap(1, 2) * a2
            nat[1, pl.ds(at, 8, stride=8), :] = tap(2, 0) * b0 + tap(2, 1) * b1 + tap(2, 2) * b2
            a1, a2, b1, b2 = a0, a1, b0, b1
        first = pl.multiple_of(block * 16, 16)
        for a in range(2):
            for j in range(SUBS):
                rows = [
                    nat[a, pl.ds(pl.multiple_of(block * 128 + h * 64 + j * 8, 8), 8), :]
                    for h in range(2)
                ]
                outb[a, pl.ds(first, 16), pl.ds(j * LANES, LANES)] = jnp.concatenate(
                    rows, axis=0
                ).astype(jnp.bfloat16)
            late(a, first, 16).start()
        return state, a1, a2, b1, b2

    edges = tuple(tail[modes + a] for a in range(4))
    lax.fori_loop(0, blocks, last_pass, (tail[pl.ds(0, modes)],) + edges)
    for a in range(2):
        late(a, 0, blocks * 16).wait()
    for copy in early:
        copy.wait()


def solution(mesh):
    n_seq, n_tp = mesh.shape["seq"], mesh.shape["tp"]

    def body(q, k, v, stream, taps, rate, residue, gain, cotangent):
        length, channels = q.shape
        modes = rate.shape[0]
        assert channels == SUBS * LANES and n_seq == 32 and modes == 16 and length == LANES
        hbm = pl.BlockSpec(memory_space=pl.ANY)
        vmem = pl.BlockSpec(memory_space=pltpu.VMEM)
        out = jax.ShapeDtypeStruct((length, channels), jnp.bfloat16)
        tiles = pltpu.VMEM((length, SUBS, LANES), f32)
        per_mode = pltpu.VMEM((modes, SUBS, LANES), f32)
        n_half, groups = n_seq // 2, modes // 2
        slices = (n_half, groups, LANES)
        operands = (q, k, v, stream, cotangent, taps, rate, residue, gain.reshape(SUBS, LANES))
        results = pl.pallas_call(
            functools.partial(kernel, n_seq, n_tp),
            out_shape=(out,) * 3
            + (jax.ShapeDtypeStruct((length, SUBS, LANES), f32),) * 3
            + (
                jax.ShapeDtypeStruct((modes, SUBS, LANES), f32),
                jax.ShapeDtypeStruct((3 * 64, LANES), f32),
                jax.ShapeDtypeStruct((modes + 4, SUBS, LANES), f32),
            ),
            in_specs=[hbm] * 9,
            out_specs=(vmem,) * 9,
            scratch_shapes=[
                pltpu.VMEM((5, length, channels), jnp.bfloat16),
                pltpu.VMEM(taps.shape, f32),
                pltpu.VMEM(rate.shape, f32),
                pltpu.VMEM(rate.shape, f32),
                pltpu.VMEM((SUBS, LANES), f32),
                pltpu.VMEM((5, length * SUBS, LANES), f32),
                pltpu.VMEM((modes * SUBS, LANES), f32),
                per_mode,
            ]
            + [tiles] * 8
            + [
                pltpu.VMEM((2, length, LANES), f32),
                pltpu.VMEM((6, SUBS, LANES), f32),
                pltpu.VMEM((6, SUBS, LANES), f32),
                pltpu.VMEM((7, SUBS, LANES), f32),
                pltpu.VMEM((7, SUBS, LANES), f32),
                pltpu.VMEM((n_half, groups + 4, LANES), f32),
                pltpu.VMEM(slices, f32),
                pltpu.VMEM((n_half + 1, groups + 4, LANES), f32),
                pltpu.VMEM(slices, f32),
                pltpu.VMEM((3,) + slices, f32),
                pltpu.VMEM((2, n_half, LANES), f32),
                pltpu.VMEM((2, modes, SUBS, LANES), f32),
                pltpu.VMEM((2,) + slices, f32),
                pltpu.VMEM((2,) + slices, f32),
                pltpu.VMEM((2, groups, LANES), f32),
                pltpu.VMEM((2,) + slices, f32),
                pltpu.VMEM((2, 2, SUBS, LANES), f32),
                pltpu.VMEM((2, modes, SUBS, LANES), f32),
                pltpu.VMEM((PARTS, modes, SUBS, LANES), f32),
                pltpu.VMEM((PARTS, 2, LANES), f32),
                pltpu.VMEM((PARTS, n_tp, 2, LANES), f32),
                pltpu.SemaphoreType.DMA((9,)),
                pltpu.SemaphoreType.DMA((10 + PARTS,)),
                pltpu.SemaphoreType.DMA((10 + PARTS,)),
                pltpu.SemaphoreType.REGULAR,
            ],
            compiler_params=pltpu.CompilerParams(
                collective_id=0, has_side_effects=True, vmem_limit_bytes=40 * 1024 * 1024
            ),
        )(*[pltpu.with_memory_space_constraint(x, pltpu.HBM) for x in operands])
        return pl.pallas_call(
            finish,
            out_shape=(out,) * 5,
            in_specs=[vmem] * 9,
            out_specs=(pl.BlockSpec(memory_space=pltpu.HBM),) * 5,
            scratch_shapes=[
                pltpu.VMEM((2, length * SUBS, LANES), f32),
                pltpu.VMEM((2, length, channels), jnp.bfloat16),
                pltpu.SemaphoreType.DMA((5,)),
            ],
            compiler_params=pltpu.CompilerParams(vmem_limit_bytes=8 * 1024 * 1024),
        )(*results)

    seq_tp = P("seq", "tp")
    return jax.shard_map(
        body,
        mesh=mesh,
        in_specs=(
            seq_tp,
            seq_tp,
            seq_tp,
            seq_tp,
            P(None, None, "tp"),
            P(None, "tp"),
            P(None, "tp"),
            P("tp"),
            seq_tp,
        ),
        out_specs=(seq_tp,) * 5,
        check_vma=False,
    )
```

```python
import functools

import jax
import jax.numpy as jnp
from jax import lax
from jax.experimental import pallas as pl
from jax.experimental.pallas import tpu as pltpu
from jax.sharding import PartitionSpec as P

MESH = pl.DeviceIdType.MESH
f32 = jnp.float32
epsilon = 1e-05
LANES = 128
SUBS = 8
PARTS = 2
ROWS = 16


def swap_halves(first, second, upper):
    return (
        jnp.where(upper, pltpu.roll(second, 64, 1), first),
        jnp.where(upper, second, pltpu.roll(first, 64, 1)),
    )


def kernel(
    n_seq,
    n_tp,
    q_hbm,
    k_hbm,
    v_hbm,
    s_hbm,
    c_hbm,
    taps_hbm,
    rate_hbm,
    res_hbm,
    gain_hbm,
    normed_ref,
    sgrad_ref,
    qgrad_ref,
    km,
    vm,
    dp,
    dec,
    tapn,
    tail,
    inb,
    taps_ref,
    rate_ref,
    res_ref,
    gain_ref,
    nat,
    par,
    res,
    qm,
    pr,
    cv,
    st,
    sc,
    mx,
    dm,
    dc,
    rows,
    halo_s,
    halo_r,
    head_s,
    head_r,
    fsf,
    fsb,
    rxf,
    rxb,
    dsl,
    lift,
    powers,
    ax,
    ar,
    total,
    across,
    bump,
    growth,
    starts,
    pss,
    psr,
    in_sem,
    send_sem,
    recv_sem,
    ready,
):
    me = lax.axis_index("seq")
    mt = lax.axis_index("tp")
    n_half = n_seq // 2
    half, place = me // n_half, lax.rem(me, n_half)
    base = half * n_half
    length = km.shape[0]
    modes = rate_ref.shape[0]
    chunks = length // SUBS
    width = float(n_tp * SUBS * LANES)

    barrier = pltpu.get_barrier_semaphore()

    in_half = [(3, 2), (1, 2), (2, 2), (3, 1), (3, 3), (1, 1), (1, 3), (2, 1), (2, 3)]
    in_half += [(3, 0), (1, 0), (2, 0), (0, 2), (0, 1), (0, 3)]
    to_other = [(dz, dy) for dy in (2, 1, 3, 0) for dz in (0, 1, 3, 2)]
    along_tp = (4, 5, 3, 2, 6, 7, 1)

    def at_step(step):
        dz, dy = step
        return lax.rem(place // 4 + dz, n_half // 4) * 4 + lax.rem(place + dy, 4)

    def greet(device):
        pl.semaphore_signal(barrier, inc=1, device_id={"seq": device}, device_id_type=MESH)

    def greet_later(k, carry):
        greet(n_half + k)
        return carry

    @pl.when(me == n_half)
    def _():
        greet(me - 1)

    for step in in_half:
        greet(base + at_step(step))
    for step in along_tp:
        other = lax.rem(mt + step, n_tp)
        pl.semaphore_signal(barrier, inc=1, device_id={"tp": other}, device_id_type=MESH)

    @pl.when(half == 0)
    def _():
        lax.fori_loop(0, n_half, greet_later, 0)


    loads = []
    for a, (src, into) in enumerate(
        (
            (k_hbm, inb.at[0]),
            (v_hbm, inb.at[1]),
            (q_hbm, inb.at[2]),
            (taps_hbm, taps_ref),
            (rate_hbm, rate_ref),
            (s_hbm, inb.at[3]),
            (c_hbm, inb.at[4]),
            (res_hbm, res_ref),
            (gain_hbm, gain_ref),
        )
    ):
        copy = pltpu.make_async_copy(src, into, in_sem.at[a])
        copy.start()
        loads.append(copy)
    at_load = (0, 1, 2, 5, 6)


    def per_mode(source, into):
        for i in range(modes // SUBS):
            for j in range(SUBS):
                par[pl.ds(i * 64 + j * 8, 8), :] = source[
                    pl.ds(i * 8, 8), pl.ds(j * LANES, LANES)
                ]
        for m in range(modes):
            into[m] = par[pl.ds((m // 8) * 64 + m % 8, 8, stride=8), :]

    def tap_rows():
        for a in range(3):
            for j in range(SUBS):
                tapn[pl.ds((a * 8 + j) * 8, 3), :] = taps_ref[a, :, pl.ds(j * LANES, LANES)]

    def tap(a, b):
        return tapn[pl.ds(a * 64 + b, 8, stride=8), :]

    def to_tiles(a, first, last):
        def step(i, carry):
            block = inb[a, pl.ds(pl.multiple_of(i * 16, 16), 16), :].astype(f32)
            for h in range(2):
                for j in range(SUBS):
                    nat[a, pl.ds(pl.multiple_of(i * 128 + h * 64 + j * 8, 8), 8), :] = block[
                        h * 8 : h * 8 + 8, j * LANES : (j + 1) * LANES
                    ]
            return carry

        lax.fori_loop(first, last, step, 0)

    def row(a, i, s):
        return nat[a, pl.ds(i * 64 + s, 8, stride=8), :]

    def put_row(a, i, s, value):
        nat[a, pl.ds(i * 64 + s, 8, stride=8), :] = value

    zero = jnp.zeros((SUBS, LANES), f32)
    blocks = length // 16
    for a in range(2):
        loads[a].wait()
        to_tiles(a, 0, blocks)
    loads[3].wait()
    tap_rows()
    loads[4].wait()
    per_mode(rate_ref, dec)
    dec[...] = jnp.exp(-dec[...])

    def first_pass(i, carry):
        state, k1, k2, v1, v2 = carry
        d = dec[...]
        for s in range(SUBS):
            k0, v0 = row(0, i, s), row(1, i, s)
            kmix = tap(1, 0) * k0 + tap(1, 1) * k1 + tap(1, 2) * k2
            vmix = tap(2, 0) * v0 + tap(2, 1) * v1 + tap(2, 2) * v2
            prod = kmix * vmix
            km[i * 8 + s] = kmix
            vm[i * 8 + s] = vmix
            pr[i * 8 + s] = prod
            state = d * state + prod[None]
            k1, k2, v1, v2 = k0, k1, v0, v1
        return state, k1, k2, v1, v2

    state0 = jnp.zeros((modes, SUBS, LANES), f32)
    final, k1, k2, v1, v2 = lax.fori_loop(0, chunks, first_pass, (state0, zero, zero, zero, zero))
    upper = lax.broadcasted_iota(jnp.int32, (SUBS, LANES), 1) >= 64
    groups = modes // 2

    def put_slices(into, values, row0=0):
        for a in range(len(values) // 2):
            tiles = swap_halves(values[2 * a], values[2 * a + 1], upper)
            for q in range(2):
                into[pl.ds(q * 8, 8), row0 + a, :] = tiles[q]

    def get_state(source):
        out = []
        for a in range(groups):
            out += swap_halves(source[pl.ds(0, 8), a, :], source[pl.ds(8, 8), a, :], upper)
        return jnp.stack(out)

    def each(value):
        return [value[m] for m in range(modes)]

    kt0, kt1 = tap(1, 1) * k1 + tap(1, 2) * k2, tap(1, 2) * k1
    vt0, vt1 = tap(2, 1) * v1 + tap(2, 2) * v2, tap(2, 2) * v1
    halo_s[0], halo_s[1], halo_s[2], halo_s[3] = kt0, kt1, vt0, vt1

    put_slices(fsf, each(final))
    edges = (km[0], km[1], kt0, kt1, vm[0], vm[1], vt0, vt1)
    put_slices(fsf, edges, groups)
    loads[2].wait()
    to_tiles(2, 0, blocks)
    q1, q2 = row(2, chunks - 1, 7), row(2, chunks - 1, 6)
    halo_s[4] = tap(0, 1) * q1 + tap(0, 2) * q2
    halo_s[5] = tap(0, 2) * q1
    per_mode(rate_ref, res)

    first_of_later = (1 - half) * ((me + 1) // n_half)
    pl.semaphore_wait(barrier, n_half - 1 + n_tp - 1 + half * n_half + first_of_later)

    def halo_copy():
        return pltpu.make_async_remote_copy(
            src_ref=halo_s,
            dst_ref=halo_r,
            send_sem=send_sem.at[0],
            recv_sem=recv_sem.at[0],
            device_id={"seq": me + 1},
            device_id_type=MESH,
        )

    @pl.when(me == 0)
    def _():
        halo_r[...] = jnp.zeros_like(halo_r)

    def first_rows():
        for t in range(2):
            km[t] = km[t] + halo_r[t]
            vm[t] = vm[t] + halo_r[2 + t]
            pr[t] = km[t] * vm[t]

    def exchange(which, source, into, shift=0):
        for step in in_half:
            other = at_step(step)
            pltpu.make_async_remote_copy(
                src_ref=source.at[other],
                dst_ref=into.at[place + shift],
                send_sem=send_sem.at[which],
                recv_sem=recv_sem.at[which],
                device_id={"seq": base + other},
                device_id_type=MESH,
            ).start()
        into[place + shift] = source[place]

    def landed(which, into):
        others = into.at[pl.ds(0, n_half - 1)]
        pltpu.make_async_copy(others, others, recv_sem.at[which]).wait()

    def sent(which, source):
        others = source.at[pl.ds(0, n_half - 1)]
        pltpu.make_async_copy(others, others, send_sem.at[which]).wait()

    def send_across(which, slot, target):
        for step in to_other:
            pltpu.make_async_remote_copy(
                src_ref=total.at[slot],
                dst_ref=across.at[slot, place],
                send_sem=send_sem.at[which],
                recv_sem=recv_sem.at[which],
                device_id={"seq": target + at_step(step)},
                device_id_type=MESH,
            ).start()

    def wait_across(sem, slot):
        pltpu.make_async_copy(across.at[slot], across.at[slot], sem).wait()

    exchange(1, fsf, rxf, 1)

    @pl.when(me < n_seq - 1)
    def _():
        halo_copy().start()

    def tell(k, carry):
        pl.semaphore_signal(ready, inc=1, device_id={"seq": k}, device_id_type=MESH)
        return carry

    @pl.when(half == 1)
    def _():
        lax.fori_loop(0, n_half, tell, 0)
        across[1] = jnp.zeros(across.shape[1:], f32)

    @pl.when(half == 0)
    def _():
        across[0] = jnp.zeros(across.shape[1:], f32)

    rate = res[...]
    put_slices(dsl.at[0], each(jnp.exp(rate * (-float(length)))))
    put_slices(dsl.at[1], each(jnp.exp(rate * (-float(length - 2)))))
    put_slices(dsl.at[2], [dec[m] for m in range(modes)])
    before = (place * length).astype(f32)
    after = ((n_half - 1 - place) * length).astype(f32)
    put_slices(powers.at[0], each(jnp.exp(rate * -before)))
    put_slices(powers.at[1], each(jnp.exp(rate * -after)))
    growth[0] = jnp.exp(rate * (1.0 - before))
    growth[1] = jnp.exp(rate * (2.0 - before))
    for part in range(1, PARTS):
        starts[part] = jnp.exp(rate * (-float(part * (length // PARTS))))
    pss[...] = jnp.zeros_like(pss)
    for a in range(3, 5):
        loads[at_load[a]].wait()
        to_tiles(a, 0, blocks)
    loads[7].wait()
    per_mode(res_ref, res)
    loads[8].wait()
    gain = gain_ref[...]

    def middle_pass(i, carry):
        q1, q2 = carry
        for s in range(SUBS):
            q0 = row(2, i, s)
            qm[i * 8 + s] = tap(0, 0) * q0 + tap(0, 1) * q1 + tap(0, 2) * q2
            st[i * 8 + s] = row(3, i, s)
            sc[i * 8 + s] = gain * row(4, i, s)
            q1, q2 = q0, q1
        return q1, q2

    lax.fori_loop(0, chunks, middle_pass, (zero, zero))

    @pl.when(me > 0)
    def _():
        halo_copy().wait_recv()

    old0, old1 = pr[0], pr[1]
    first_rows()
    bump[0, 0], bump[0, 1] = pr[0] - old0, pr[1] - old1

    def bump_copy(other):
        return pltpu.make_async_remote_copy(
            src_ref=bump.at[0],
            dst_ref=bump.at[1],
            send_sem=send_sem.at[9],
            recv_sem=recv_sem.at[9],
            device_id={"seq": other},
            device_id_type=MESH,
        )

    def tell_bump(k, carry):
        bump_copy(n_half + 1 + k).start()
        return carry

    @pl.when(me == n_half)
    def _():
        lax.fori_loop(0, n_half - 1, tell_bump, 0)

    @pl.when(me <= n_half)
    def _():
        bump[1] = jnp.zeros(bump.shape[1:], f32)

    qm[0] = qm[0] + halo_r[4]
    qm[1] = qm[1] + halo_r[5]

    rxf[0] = jnp.zeros(rxf.shape[1:], f32)
    landed(1, rxf)
    kh, vh = rxf[pl.ds(1, n_half), groups, :], rxf[pl.ds(1, n_half), groups + 2, :]
    kmix = kh + rxf[pl.ds(0, n_half), groups + 1, :]
    vmix = vh + rxf[pl.ds(0, n_half), groups + 3, :]
    extra = kmix * vmix - kh * vh
    turned = pltpu.roll(extra, 64, 1)
    high = lax.broadcasted_iota(jnp.int32, (n_half, LANES), 1) >= 64
    lift[0] = jnp.where(high, turned, extra)
    lift[1] = jnp.where(high, extra, turned)
    step_decay, lift_decay, one_decay = dsl[0, place], dsl[1, place], dsl[2, place]

    def scan_forward(p, state):
        ax[0, p] = state
        added = one_decay * lift[0, pl.ds(p, 1), :] + lift[1, pl.ds(p, 1), :]
        return step_decay * state + (rxf[p + 1, 0:groups, :] + lift_decay * added)

    passed = jnp.zeros((groups, LANES), f32)
    for p in range(n_half):
        passed = scan_forward(p, passed)
    total[0] = passed
    exchange(2, ax.at[0], ar.at[0])

    @pl.when(half == 0)
    def _():
        pl.semaphore_wait(ready, n_half)
        send_across(7, 0, n_half)

    def local_pass(i, state):
        d, r = dec[...], res[...]
        block = pr[pl.ds(i * 8, 8)]
        for s in range(SUBS):
            state = d * state + block[s][None]
            cv[i * 8 + s] = jnp.sum(r * state, axis=0)
        return state

    lax.fori_loop(0, chunks, local_pass, state0)

    landed(2, ar.at[0])

    @pl.when(half == 1)
    def _():
        wait_across(recv_sem.at[7], 0)

    @pl.when(me > n_half)
    def _():
        bump_copy(me).wait_recv()

    ar[0] = ar[0] + powers[0] * across[0]
    entered = get_state(ar.at[0]) + growth[0] * bump[1, 0] + growth[1] * bump[1, 1]
    arrived = res[...] * dec[...] * entered

    def join_pass(i, state):
        d = dec[...]
        for s in range(ROWS):
            t = i * ROWS + s
            conv = cv[t] + jnp.sum(state, axis=0)
            state = d * state
            mixed = st[t] + qm[t] * conv
            cv[t] = conv
            mx[t] = mixed
            put_row(0, i * (ROWS // 8) + s // 8, s % 8, mixed * mixed)
            put_row(1, i * (ROWS // 8) + s // 8, s % 8, sc[t] * mixed)
        return state

    span = length // PARTS
    step_chunks = chunks // PARTS
    order = list(reversed(range(PARTS)))

    for part in order:
        first = part * step_chunks
        start = arrived if part == 0 else arrived * starts[part]
        lax.fori_loop(part * span // ROWS, (part + 1) * span // ROWS, join_pass, start)
        for a in range(2):
            for i in range(first, first + step_chunks):
                partial = nat[a, pl.ds(i * 64, 8), :]
                for j in range(1, SUBS):
                    partial = partial + nat[a, pl.ds(i * 64 + j * 8, 8), :]
                rows[a, pl.ds(i * 8, 8), :] = partial
            summed = rows[a, pl.ds(part * span, span), :].T
            pss[part, pl.ds(a, 1), pl.ds(0, span)] = jnp.sum(summed, axis=0, keepdims=True)
        for step in along_tp:
            pltpu.make_async_remote_copy(
                src_ref=pss.at[part],
                dst_ref=psr.at[part, mt],
                send_sem=send_sem.at[10 + part],
                recv_sem=recv_sem.at[10 + part],
                device_id={"tp": lax.rem(mt + step, n_tp)},
                device_id_type=MESH,
            ).start()
        psr[part, mt] = pss[part]

    def peers(part):
        return psr.at[part, pl.ds(0, n_tp - 1)]

    def spread(a, t):
        return jnp.broadcast_to(rows[a, pl.ds(t, 1), :], (SUBS, LANES))

    def back_pass(n, state):
        i = length // ROWS - 1 - n
        d = dec[...]
        for s in reversed(range(ROWS)):
            t = i * ROWS + s
            dmixed = spread(0, t) * sc[t] - mx[t] * spread(1, t)
            dconv = dmixed * qm[t]
            dm[t] = dmixed
            dc[t] = dconv
            state = d * state + dconv[None]
        return state

    final_back = state0
    for turn, part in enumerate(order):
        pltpu.make_async_copy(peers(part), peers(part), recv_sem.at[10 + part]).wait()
        totals = jnp.sum(psr[part], axis=0)
        inverse = lax.rsqrt(totals[0:1, 0:span] / width + epsilon)
        factor = inverse * inverse * inverse * totals[1:2, 0:span] / width
        rows[0, pl.ds(part * span, span), :] = jnp.broadcast_to(inverse, (LANES, span)).T
        rows[1, pl.ds(part * span, span), :] = jnp.broadcast_to(factor, (LANES, span)).T
        final_back = lax.fori_loop(
            turn * span // ROWS, (turn + 1) * span // ROWS, back_pass, final_back
        )
    put_slices(fsb, each(final_back))
    exchange(4, fsb, rxb)

    head_s[0] = dm[0] * cv[0]
    head_s[1] = dm[1] * cv[1]
    head_s[2] = dc[0]
    head_s[3], head_s[4] = km[0], km[1]
    head_s[5], head_s[6] = vm[0], vm[1]

    def head_copy():
        return pltpu.make_async_remote_copy(
            src_ref=head_s,
            dst_ref=head_r,
            send_sem=send_sem.at[6],
            recv_sem=recv_sem.at[6],
            device_id={"seq": me - 1},
            device_id_type=MESH,
        )

    @pl.when(me > 0)
    def _():
        head_copy().start()

    @pl.when(me == n_seq - 1)
    def _():
        head_r[...] = jnp.zeros_like(head_r)

    landed(4, rxb)

    def scan_backward(n, state):
        p = n_half - 1 - n
        ax[1, p] = state
        return step_decay * state + rxb[p]

    passed = jnp.zeros((groups, LANES), f32)
    for n in range(n_half):
        passed = scan_backward(n, passed)
    total[1] = passed

    @pl.when(half == 1)
    def _():
        send_across(8, 1, 0)

    exchange(5, ax.at[1], ar.at[1])

    def adjoint_pass(n, state):
        i = chunks - 1 - n
        d, r = dec[...], res[...]
        for s in reversed(range(SUBS)):
            state = d * state + dc[i * 8 + s][None]
            dp[i * 8 + s] = jnp.sum(r * state, axis=0)
        return state

    lax.fori_loop(0, chunks, adjoint_pass, state0)

    @pl.when(me < n_seq - 1)
    def _():
        head_copy().wait_recv()

    def query_pass(n, carry):
        g1, g2 = carry
        i = chunks - 1 - n
        for s in reversed(range(SUBS)):
            t = i * 8 + s
            dmixed = dm[t]
            g0 = dmixed * cv[t]
            put_row(0, i, s, mx[t] * spread(0, t) * gain)
            put_row(1, i, s, dmixed)
            put_row(2, i, s, tap(0, 0) * g0 + tap(0, 1) * g1 + tap(0, 2) * g2)
            g1, g2 = g0, g1
        return g1, g2

    lax.fori_loop(0, chunks, query_pass, (head_r[0], head_r[1]))

    def from_tiles(a, target):
        def step(i, carry):
            for j in range(SUBS):
                block = jnp.concatenate(
                    [
                        nat[a, pl.ds(pl.multiple_of(i * 128 + j * 8, 8), 8), :],
                        nat[a, pl.ds(pl.multiple_of(i * 128 + 64 + j * 8, 8), 8), :],
                    ],
                    axis=0,
                )
                target[pl.ds(pl.multiple_of(i * 16, 16), 16), pl.ds(j * LANES, LANES)] = (
                    block.astype(jnp.bfloat16)
                )
            return carry

        lax.fori_loop(0, length // 16, step, 0)

    from_tiles(0, normed_ref)
    from_tiles(1, sgrad_ref)
    from_tiles(2, qgrad_ref)

    landed(5, ar.at[1])

    @pl.when(half == 0)
    def _():
        wait_across(recv_sem.at[8], 1)

    d, r = dec[...], res[...]
    ar[1] = ar[1] + powers[1] * across[1]
    after = get_state(ar.at[1])
    arrived_back = r * d * after
    dp0 = jnp.sum(r * after, axis=0)
    dp1 = jnp.sum(r * ((after - head_r[2][None]) / d), axis=0)
    tail[pl.ds(0, modes)] = arrived_back
    tail[modes], tail[modes + 1] = dp0 * head_r[5], dp1 * head_r[6]
    tail[modes + 2], tail[modes + 3] = dp0 * head_r[3], dp1 * head_r[4]

    @pl.when(me < n_seq - 1)
    def _():
        halo_copy().wait_send()

    @pl.when(me > 0)
    def _():
        head_copy().wait_send()

    @pl.when(me == n_half)
    def _():
        as_many = km.at[pl.ds(0, 2 * (n_half - 1))]
        pltpu.make_async_copy(as_many, as_many, send_sem.at[9]).wait()

    @pl.when(half == 0)
    def _():
        wait_across(send_sem.at[7], 0)

    @pl.when(half == 1)
    def _():
        wait_across(send_sem.at[8], 1)

    sent(1, fsf)
    sent(2, ax.at[0])
    sent(4, fsb)
    sent(5, ax.at[1])
    for part in order:
        pltpu.make_async_copy(peers(part), peers(part), send_sem.at[10 + part]).wait()


def finish(
    normed_ref,
    sgrad_ref,
    qgrad_ref,
    km,
    vm,
    dp,
    dec,
    tapn,
    tail,
    normed_hbm,
    sgrad_hbm,
    qgrad_hbm,
    kgrad_hbm,
    vgrad_hbm,
    nat,
    outb,
    sem,
):
    early = [
        pltpu.make_async_copy(source, target, sem.at[2 + a])
        for a, (source, target) in enumerate(
            ((normed_ref, normed_hbm), (sgrad_ref, sgrad_hbm), (qgrad_ref, qgrad_hbm))
        )
    ]
    for copy in early:
        copy.start()
    modes = dec.shape[0]
    blocks = km.shape[0] // 16

    def tap(a, b):
        return tapn[pl.ds(a * 64 + b, 8, stride=8), :]

    def late(a, first, count):
        target = (kgrad_hbm, vgrad_hbm)[a]
        return pltpu.make_async_copy(
            outb.at[a, pl.ds(first, count), :], target.at[pl.ds(first, count), :], sem.at[a]
        )

    def last_pass(n, carry):
        state, a1, a2, b1, b2 = carry
        block = blocks - 1 - n
        d = dec[...]
        for s in reversed(range(16)):
            t = block * 16 + s
            at = block * 128 + (s // 8) * 64 + s % 8
            dproduct = dp[t] + jnp.sum(state, axis=0)
            state = d * state
            a0 = dproduct * vm[t]
            b0 = dproduct * km[t]
            nat[0, pl.ds(at, 8, stride=8), :] = tap(1, 0) * a0 + tap(1, 1) * a1 + tap(1, 2) * a2
            nat[1, pl.ds(at, 8, stride=8), :] = tap(2, 0) * b0 + tap(2, 1) * b1 + tap(2, 2) * b2
            a1, a2, b1, b2 = a0, a1, b0, b1
        first = pl.multiple_of(block * 16, 16)
        for a in range(2):
            for j in range(SUBS):
                rows = [
                    nat[a, pl.ds(pl.multiple_of(block * 128 + h * 64 + j * 8, 8), 8), :]
                    for h in range(2)
                ]
                outb[a, pl.ds(first, 16), pl.ds(j * LANES, LANES)] = jnp.concatenate(
                    rows, axis=0
                ).astype(jnp.bfloat16)
            late(a, first, 16).start()
        return state, a1, a2, b1, b2

    edges = tuple(tail[modes + a] for a in range(4))
    lax.fori_loop(0, blocks, last_pass, (tail[pl.ds(0, modes)],) + edges)
    for a in range(2):
        late(a, 0, blocks * 16).wait()
    for copy in early:
        copy.wait()


def solution(mesh):
    n_seq, n_tp = mesh.shape["seq"], mesh.shape["tp"]

    def body(q, k, v, stream, taps, rate, residue, gain, cotangent):
        length, channels = q.shape
        modes = rate.shape[0]
        assert channels == SUBS * LANES and n_seq == 32 and modes == 16 and length == LANES
        hbm = pl.BlockSpec(memory_space=pl.ANY)
        vmem = pl.BlockSpec(memory_space=pltpu.VMEM)
        out = jax.ShapeDtypeStruct((length, channels), jnp.bfloat16)
        tiles = pltpu.VMEM((length, SUBS, LANES), f32)
        per_mode = pltpu.VMEM((modes, SUBS, LANES), f32)
        n_half, groups = n_seq // 2, modes // 2
        slices = (n_half, groups, LANES)
        operands = (q, k, v, stream, cotangent, taps, rate, residue, gain.reshape(SUBS, LANES))
        results = pl.pallas_call(
            functools.partial(kernel, n_seq, n_tp),
            out_shape=(out,) * 3
            + (jax.ShapeDtypeStruct((length, SUBS, LANES), f32),) * 3
            + (
                jax.ShapeDtypeStruct((modes, SUBS, LANES), f32),
                jax.ShapeDtypeStruct((3 * 64, LANES), f32),
                jax.ShapeDtypeStruct((modes + 4, SUBS, LANES), f32),
            ),
            in_specs=[hbm] * 9,
            out_specs=(vmem,) * 9,
            scratch_shapes=[
                pltpu.VMEM((5, length, channels), jnp.bfloat16),
                pltpu.VMEM(taps.shape, f32),
                pltpu.VMEM(rate.shape, f32),
                pltpu.VMEM(rate.shape, f32),
                pltpu.VMEM((SUBS, LANES), f32),
                pltpu.VMEM((5, length * SUBS, LANES), f32),
                pltpu.VMEM((modes * SUBS, LANES), f32),
                per_mode,
            ]
            + [tiles] * 8
            + [
                pltpu.VMEM((2, length, LANES), f32),
                pltpu.VMEM((6, SUBS, LANES), f32),
                pltpu.VMEM((6, SUBS, LANES), f32),
                pltpu.VMEM((7, SUBS, LANES), f32),
                pltpu.VMEM((7, SUBS, LANES), f32),
                pltpu.VMEM((n_half, groups + 4, LANES), f32),
                pltpu.VMEM(slices, f32),
                pltpu.VMEM((n_half + 1, groups + 4, LANES), f32),
                pltpu.VMEM(slices, f32),
                pltpu.VMEM((3,) + slices, f32),
                pltpu.VMEM((2, n_half, LANES), f32),
                pltpu.VMEM((2,) + slices, f32),
                pltpu.VMEM((2,) + slices, f32),
                pltpu.VMEM((2,) + slices, f32),
                pltpu.VMEM((2, groups, LANES), f32),
                pltpu.VMEM((2,) + slices, f32),
                pltpu.VMEM((2, 2, SUBS, LANES), f32),
                pltpu.VMEM((2, modes, SUBS, LANES), f32),
                pltpu.VMEM((PARTS, modes, SUBS, LANES), f32),
                pltpu.VMEM((PARTS, 2, LANES), f32),
                pltpu.VMEM((PARTS, n_tp, 2, LANES), f32),
                pltpu.SemaphoreType.DMA((9,)),
                pltpu.SemaphoreType.DMA((10 + PARTS,)),
                pltpu.SemaphoreType.DMA((10 + PARTS,)),
                pltpu.SemaphoreType.REGULAR,
            ],
            compiler_params=pltpu.CompilerParams(
                collective_id=0, has_side_effects=True, vmem_limit_bytes=40 * 1024 * 1024
            ),
        )(*[pltpu.with_memory_space_constraint(x, pltpu.HBM) for x in operands])
        return pl.pallas_call(
            finish,
            out_shape=(out,) * 5,
            in_specs=[vmem] * 9,
            out_specs=(pl.BlockSpec(memory_space=pltpu.HBM),) * 5,
            scratch_shapes=[
                pltpu.VMEM((2, length * SUBS, LANES), f32),
                pltpu.VMEM((2, length, channels), jnp.bfloat16),
                pltpu.SemaphoreType.DMA((5,)),
            ],
            compiler_params=pltpu.CompilerParams(vmem_limit_bytes=8 * 1024 * 1024),
        )(*results)

    seq_tp = P("seq", "tp")
    return jax.shard_map(
        body,
        mesh=mesh,
        in_specs=(
            seq_tp,
            seq_tp,
            seq_tp,
            seq_tp,
            P(None, None, "tp"),
            P(None, "tp"),
            P(None, "tp"),
            P("tp"),
            seq_tp,
        ),
        out_specs=(seq_tp,) * 5,
        check_vma=False,
    )
```
